512 devices in a mesh: rows: 8 (over z_hi, core), feat: 64 (over z_lo, x, y).
Axes of the slice: x: 4, y: 4, z: 16 (z_hi: 4, z_lo: 4; z = z_hi * 4 + z_lo), core: 2. Of those that a mesh axis runs over, the one named last changes fastest.
Arguments:
- genotypes: bfloat16 [4096, 131072], P('rows', 'feat')
- labels: int32 [4096], P('rows'), may hold values from 0 to 63
- base_margin: float32 [4096, 64], P('rows')
- winners: int32 [2, 64], replicated, may hold values from 0 to 131071, as said below
Outputs:
- logits: float32 [4096, 64], P('rows')
- scores: float32 [3, 64, 131072], P(None, 'rows', 'feat')
The draws below stay inside these ranges and needn't reach their ends.
Inputs may be any that keep to these rules, and one draw needn't show every extreme that they name: `winners`: in every iteration each of the 64 aligned blocks of 2048 columns holds the winning column of exactly one class.
All inputs are finite; a program needn't handle non-finite values.
Results may differ from the reference program's by a relative error of at most 0.012.
Values may be sent and summed in bfloat16 or wider, within the bound.
No kernel may reach another device: no remote copies, remote signals or barrier semaphores. Data moves between devices by JAX's collectives and lax.ppermute only.
A program may use at most 64 MiB of HBM per device.

```python
import jax
import jax.numpy as jnp
from jax import lax

K = 64
PDEV = 2048
ROWS_DEV = 512
ITERS = 2
P_SIZE = 131072
SAMPLES = 4096
N_ROWS = 8


def draw_genotypes(key, part):
    return jax.random.randint(key, (SAMPLES, P_SIZE), 0, 3).astype(jnp.float32).astype(jnp.bfloat16)


def draw_base_margin(key, part):
    first = jax.random.fold_in(jax.random.fold_in(key, 7), 0)
    return jnp.clip(0.05 * jax.random.normal(first, (SAMPLES, K), jnp.float32), -0.2, 0.2)


def draw_winners(key, part):
    rows_out = []
    blocks = P_SIZE // PDEV
    for step in range(ITERS):
        sub = jax.random.fold_in(key, 100 + step)
        order = jax.random.permutation(jax.random.fold_in(sub, 1), K).astype(jnp.int32)
        owner = order % blocks
        offset = jax.random.randint(jax.random.fold_in(sub, 2), (K,), 0, PDEV).astype(jnp.int32)
        offset = jnp.where(order == K - 1, PDEV - 1, jnp.where(order == 0, 0, offset)).astype(jnp.int32)
        rows_out.append(owner * PDEV + offset)
    return jnp.stack(rows_out).astype(jnp.int32)


def set_ends(drawn, own_key, smallest, top_value):
    spot = [jax.random.randint(jax.random.fold_in(own_key, axis), (), 0, length) for axis, length in enumerate(drawn.shape)]
    main_axis = drawn.shape.index(max(drawn.shape))
    beside = spot[:main_axis] + [(spot[main_axis] + 1) % drawn.shape[main_axis]] + spot[main_axis + 1:]
    return drawn.at[tuple(spot)].set(smallest).at[tuple(beside)].set(top_value)


def setup_inputs(seed: int = 0) -> dict:
    key_list = jax.random.split(jax.random.key(seed), 5)
    genotypes = draw_genotypes(jax.random.fold_in(key_list[4], 71), 0)
    labels = set_ends(jax.random.randint(key_list[1], (SAMPLES,), 0, K), jax.random.fold_in(key_list[1], 1), 0, K - 1).astype(jnp.int32)
    base_margin = draw_base_margin(jax.random.fold_in(key_list[4], 71), 0)
    winners = draw_winners(jax.random.fold_in(key_list[4], 71), 0)
    return {"genotypes": genotypes, "labels": labels, "base_margin": base_margin, "winners": winners}


shrink_rate = 0.5
ridge_term = 1.0


def softmax_rows(values):
    top = jnp.max(values, axis=1, keepdims=True)
    expo = jnp.exp(values - top)
    return expo / jnp.sum(expo, axis=1, keepdims=True)


def group_scores(resid, genotypes):
    resid_groups = resid.reshape(N_ROWS, ROWS_DEV, K)
    geno_groups = genotypes.reshape(N_ROWS, ROWS_DEV, genotypes.shape[1])

    def add_group(total, pair):
        term = jnp.dot(pair[0].T, pair[1], preferred_element_type=jnp.float32).astype(jnp.bfloat16)
        term = lax.optimization_barrier(term)
        return total + term.astype(jnp.float32), None

    start = jnp.zeros((K, genotypes.shape[1]), jnp.float32)
    total, unused = lax.scan(add_group, start, (resid_groups, geno_groups))
    return total


def reference(genotypes, labels, base_margin, winners):
    onehot = (labels[:, None] == jnp.arange(K, dtype=jnp.int32)[None, :]).astype(jnp.float32)
    logits = base_margin
    tables = []
    for step in range(ITERS + 1):
        prob = softmax_rows(logits)
        resid = (onehot - prob).astype(jnp.bfloat16)
        tables.append(group_scores(resid, genotypes))
        if step < ITERS:
            picked = jnp.take(genotypes, winners[step], axis=1).astype(jnp.float32)
            grad = jnp.sum(resid.astype(jnp.float32) * picked, axis=0)
            curv = jnp.sum(prob * (1.0 - prob) * picked * picked, axis=0)
            coef = shrink_rate * grad / (curv + ridge_term)
            logits = logits + coef[None, :] * picked
    return logits, jnp.stack(tables)
```

```python
import jax
import jax.numpy as jnp
from jax import lax
from jax.sharding import PartitionSpec as P

K = 64
ITERS = 2


shrink_rate = 0.5
ridge_term = 1.0


def softmax_rows(values):
    top = jnp.max(values, axis=1, keepdims=True)
    expo = jnp.exp(values - top)
    return expo / jnp.sum(expo, axis=1, keepdims=True)


def shards(genotypes, labels, base_margin, winners):
    sample_count, column_count = genotypes.shape
    feat_count = lax.axis_size("feat")
    rows_count = lax.axis_size("rows")
    class_share = K // rows_count
    feat_pos = lax.axis_index("feat")
    classes = jnp.arange(K, dtype=jnp.int32)
    onehot = (labels[:, None] == classes[None, :]).astype(jnp.float32)
    contract = (((0,), (0,)), ((), ()))

    owner = winners // column_count
    local_cols = jnp.sum(
        jnp.where(owner == feat_pos, winners - feat_pos * column_count, 0), axis=1
    )
    pick = (
        jnp.arange(column_count, dtype=jnp.int32)[None, :] == local_cols[:, None]
    ).astype(jnp.bfloat16)
    own = lax.dot_general(
        pick, genotypes, (((1,), (1,)), ((), ())), preferred_element_type=jnp.float32
    ).astype(jnp.bfloat16)
    sent = jnp.broadcast_to(own[None], (feat_count, ITERS, sample_count))
    columns = lax.all_to_all(sent, "feat", 0, 0, tiled=True)

    def partial_table(resid):
        return lax.dot_general(
            resid, genotypes, contract, preferred_element_type=jnp.float32
        ).astype(jnp.bfloat16)

    logits = base_margin
    tables = []
    for step in range(ITERS + 1):
        prob = softmax_rows(logits)
        resid = (onehot - prob).astype(jnp.bfloat16)
        part = partial_table(resid)
        if step < ITERS:
            tables.append(
                lax.psum_scatter(part, "rows", scatter_dimension=0, tiled=True).astype(
                    jnp.float32
                )
            )
            place = (
                jnp.arange(feat_count, dtype=jnp.int32)[:, None] == owner[step][None, :]
            ).astype(jnp.bfloat16)
            picked = lax.dot_general(
                columns[:, step], place, contract, preferred_element_type=jnp.float32
            )
            grad = jnp.sum(resid.astype(jnp.float32) * picked, axis=0)
            curv = jnp.sum(prob * (1.0 - prob) * picked * picked, axis=0)
            sums = jnp.concatenate([grad, curv])
            shared = lax.all_to_all(
                jnp.broadcast_to(sums[None], (rows_count, 2 * K)), "rows", 0, 0, tiled=True
            )
            sums = jnp.sum(shared, axis=0)
            coef = shrink_rate * sums[:K] / (sums[K:] + ridge_term)
            logits = logits + coef[None, :] * picked
        else:
            shared = lax.all_to_all(part, "rows", 0, 0, tiled=True)
            shared = shared.reshape(rows_count, class_share, column_count)
            tables.append(jnp.sum(shared.astype(jnp.float32), axis=0))
    return (logits, jnp.stack(tables))


def solution(mesh):
    in_specs = (P("rows", "feat"), P("rows"), P("rows", None), P())
    out_specs = (P("rows", None), P(None, "rows", "feat"))
    return jax.shard_map(shards, mesh=mesh, in_specs=in_specs, out_specs=out_specs, check_vma=False)
```

```python
import jax
import jax.numpy as jnp
from jax import lax
from jax.sharding import PartitionSpec as P

K = 64
ITERS = 2


shrink_rate = 0.5
ridge_term = 1.0

bf16 = jnp.bfloat16
f32 = jnp.float32


def softmax_classes(values):
    top = jnp.max(values, axis=0, keepdims=True)
    expo = jnp.exp(values - top)
    return expo / jnp.sum(expo, axis=0, keepdims=True)


def split3(values):
    high = lax.reduce_precision(values, 8, 7)
    rest = values - high
    middle = lax.reduce_precision(rest, 8, 7)
    return high, middle, rest - middle


def shards(genotypes, labels, base_margin, winners):
    sample_count, column_count = genotypes.shape
    feat_count = lax.axis_size("feat")
    rows_count = lax.axis_size("rows")
    class_share = K // rows_count
    half = column_count // 2
    feat_pos = lax.axis_index("feat")
    side = lax.rem(lax.axis_index("rows"), 2)
    partners = [(i, i ^ 1) for i in range(rows_count)]
    classes = jnp.arange(K, dtype=jnp.int32)
    contract = (((0,), (0,)), ((), ()))

    owner = winners // column_count
    local_cols = jnp.sum(
        jnp.where(owner == feat_pos, winners - feat_pos * column_count, 0), axis=1
    )
    pick = (
        jnp.arange(column_count, dtype=jnp.int32)[None, :] == local_cols[:, None]
    ).astype(bf16)
    own = lax.dot_general(
        pick, genotypes, (((1,), (1,)), ((), ())), preferred_element_type=f32
    ).astype(bf16)
    sent = jnp.broadcast_to(own[None], (feat_count, ITERS, sample_count))
    columns = lax.all_to_all(sent, "feat", 0, 0, tiled=True)

    kept = lax.dynamic_slice_in_dim(genotypes, side * half, half, 1)
    given = lax.dynamic_slice_in_dim(genotypes, (1 - side) * half, half, 1)
    taken = lax.ppermute(given, "rows", partners)
    margin = base_margin.T
    state = jnp.concatenate(
        [margin, jnp.broadcast_to(labels.astype(f32)[None, :], (8, sample_count))]
    )
    state_taken = lax.ppermute(state, "rows", partners)
    labels_taken = state_taken[K].astype(jnp.int32)

    onehot = (classes[:, None] == labels[None, :]).astype(f32)
    onehot_taken = (classes[:, None] == labels_taken[None, :]).astype(f32)
    logits, logits_taken = margin, state_taken[:K]
    columns_taken = lax.ppermute(columns, "rows", partners)

    def half_table(resid, resid_taken):
        rows_dim = (((1,), (0,)), ((), ()))
        first = lax.dot_general(resid, kept, rows_dim, preferred_element_type=f32)
        second = lax.dot_general(resid_taken, taken, rows_dim, preferred_element_type=f32)
        return (first + second).astype(bf16).reshape(rows_count, class_share, half)

    def finish_table(shared):
        parts = shared.astype(f32).reshape(rows_count // 2, 2, class_share, half)
        total = jnp.sum(parts, axis=0)
        return jnp.concatenate([total[0], total[1]], axis=1)

    tables = []
    for step in range(ITERS + 1):
        prob = softmax_classes(logits)
        resid = (onehot - prob).astype(bf16)
        resid_taken = (onehot_taken - softmax_classes(logits_taken)).astype(bf16)
        part = half_table(resid, resid_taken)
        if step < ITERS:
            place = (
                jnp.arange(feat_count, dtype=jnp.int32)[:, None] == owner[step][None, :]
            ).astype(bf16)
            picked = lax.dot_general(
                place, columns[:, step], contract, preferred_element_type=f32
            )
            picked_taken = lax.dot_general(
                place, columns_taken[:, step], contract, preferred_element_type=f32
            )
            grad = jnp.sum(resid.astype(f32) * picked, axis=1)
            curv = jnp.sum(prob * (1.0 - prob) * picked * picked, axis=1)
            terms = split3(0.5 * jnp.concatenate([grad, curv]))
            terms = jnp.stack(list(terms) + [jnp.zeros_like(grad, shape=(2 * K,))] * 5)
            terms = jnp.broadcast_to(terms.astype(bf16)[None], (rows_count, 8, 2 * K))
            shared = lax.all_to_all(
                jnp.concatenate([part, terms], axis=2), "rows", 0, 0, tiled=True
            )
            sums = jnp.sum(shared[:, :3, half:].astype(f32), axis=1)
            sums = 2.0 * jnp.sum(sums, axis=0)
            coef = (shrink_rate * sums[:K] / (sums[K:] + ridge_term))[:, None]
            logits = logits + coef * picked
            logits_taken = logits_taken + coef * picked_taken
            tables.append(finish_table(shared[:, :, :half]))
        else:
            shared = lax.all_to_all(part, "rows", 0, 0, tiled=True)
            tables.append(finish_table(shared))
    return (logits.T, jnp.stack(tables))


def solution(mesh):
    in_specs = (P("rows", "feat"), P("rows"), P("rows", None), P())
    out_specs = (P("rows", None), P(None, "rows", "feat"))
    return jax.shard_map(shards, mesh=mesh, in_specs=in_specs, out_specs=out_specs, check_vma=False)
```

```python
import jax
import jax.numpy as jnp
from jax import lax
from jax.experimental import pallas as pl
from jax.experimental.pallas import tpu as pltpu
from jax.sharding import PartitionSpec as P

K = 64
ITERS = 2
LANES = 128


shrink_rate = 0.5
ridge_term = 1.0

bf16 = jnp.bfloat16
f32 = jnp.float32
i32 = jnp.int32
VMEM = pl.BlockSpec(memory_space=pltpu.VMEM)
HBM = pl.BlockSpec(memory_space=pltpu.HBM)


def call(body, out_shape, in_specs, scratch=(), flops=0, moved=0, room=16 << 20):
    out_specs = jax.tree.map(lambda _: VMEM, out_shape)
    return pl.pallas_call(
        body,
        out_shape=out_shape,
        in_specs=in_specs,
        out_specs=out_specs,
        scratch_shapes=list(scratch),
        cost_estimate=pl.CostEstimate(flops=flops, bytes_accessed=moved, transcendentals=0),
        compiler_params=pltpu.CompilerParams(vmem_limit_bytes=room),
    )


def rounded(values):
    return values.astype(bf16).astype(f32)


def split3(values):
    high = rounded(values)
    rest = values - high
    middle = rounded(rest)
    return high, middle, rest - middle


def softmax_classes(values):
    top = jnp.max(values, axis=0, keepdims=True)
    expo = jnp.exp(values - top)
    return expo / jnp.sum(expo, axis=0, keepdims=True)


def residuals(logits, label_row):
    prob = softmax_classes(logits)
    classes = lax.broadcasted_iota(i32, logits.shape, 0).astype(f32)
    onehot = jnp.where(classes == label_row, 1.0, 0.0)
    return (onehot - prob).astype(bf16), prob


def pick_body(win_ref, geno_ref, out_ref, block_ref, sem_ref):
    samples, columns = geno_ref.shape
    local = win_ref[...] - lax.axis_index("feat") * columns
    mine = jnp.where((local >= 0) & (local < columns), local, 0).astype(f32)
    copies, lanes = [], []
    for step in range(ITERS):
        col = jnp.sum(mine[step : step + 1]).astype(i32)
        start = pl.multiple_of((col // LANES) * LANES, LANES)
        copy = pltpu.make_async_copy(
            geno_ref.at[:, pl.ds(start, LANES)], block_ref.at[step], sem_ref.at[step]
        )
        copy.start()
        copies.append(copy)
        lanes.append(col - start)
    rows = lax.broadcasted_iota(i32, (8, LANES), 0)
    lane = lax.broadcasted_iota(i32, (8, LANES), 1)
    tile = jnp.zeros((8, LANES), f32)
    for step in range(ITERS):
        copies[step].wait()
        pick = jnp.where(lane == lanes[step], 1.0, 0.0).astype(bf16)
        x = lax.dot_general(
            pick, block_ref[step], (((1,), (1,)), ((), ())), preferred_element_type=f32
        )
        for j in range(samples // LANES):
            here = rows == step * (samples // LANES) + j
            tile = tile + jnp.where(here, x[:, j * LANES : (j + 1) * LANES], 0.0)
    out_ref[...] = jnp.broadcast_to(tile.astype(bf16)[None], out_ref.shape)


def load_halves(geno_ref, taken_ref, both_ref, sem_ref):
    samples, half = taken_ref.shape
    side = lax.rem(lax.axis_index("rows"), 2)
    start = pl.multiple_of(side * half, LANES)
    first = pltpu.make_async_copy(
        geno_ref.at[:, pl.ds(start, half)], both_ref.at[pl.ds(0, samples)], sem_ref.at[0]
    )
    second = pltpu.make_async_copy(taken_ref, both_ref.at[pl.ds(samples, samples)], sem_ref.at[1])
    first.start()
    second.start()
    return first, second


def half_table(resid, resid_taken, both_ref):
    whole = jnp.concatenate([resid, resid_taken], axis=1)
    return jnp.dot(whole, both_ref[...], preferred_element_type=f32)


def sums_tile(resid, prob, picked):
    grad = resid.astype(f32) * picked
    curv = prob * (1.0 - prob) * picked * picked
    both = 0.5 * jnp.concatenate([grad, curv], axis=0)
    folded = both[:, :LANES]
    for j in range(1, both.shape[1] // LANES):
        folded = folded + both[:, j * LANES : (j + 1) * LANES]
    ones = jnp.ones((8, LANES), bf16)
    total = jnp.zeros((8, 2 * K), f32)
    for term in split3(folded):
        total = total + lax.dot_general(
            ones, term.astype(bf16), (((1,), (1,)), ((), ())), preferred_element_type=f32
        )
    high, middle, low = split3(total)
    row = lax.broadcasted_iota(i32, total.shape, 0)
    tile = jnp.where(row == 0, high, jnp.where(row == 1, middle, jnp.where(row == 2, low, 0.0)))
    return tile.astype(bf16)


def coefficients(shared_ref, half):
    tiles = shared_ref[:, :, half:].astype(f32)
    row = jnp.sum(jnp.sum(tiles, axis=0), axis=0, keepdims=True)
    column = jnp.transpose(jnp.broadcast_to(row, (2 * K, LANES)))
    return shrink_rate * (2.0 * column[:K]) / (2.0 * column[K:] + ridge_term)


def lane_tile(values, count):
    return jnp.concatenate([values] * count, axis=1)


def first_table_body(state_ref, state_taken_ref, geno_ref, taken_ref, out_ref, both_ref, sem_ref):
    copies = load_halves(geno_ref, taken_ref, both_ref, sem_ref)
    resid, _ = residuals(state_ref[:K], state_ref[K : K + 1])
    resid_taken, _ = residuals(state_taken_ref[:K], state_taken_ref[K : K + 1])
    for copy in copies:
        copy.wait()
    table = half_table(resid, resid_taken, both_ref)
    out_ref[...] = table.reshape(out_ref.shape).astype(bf16)


def first_sums_body(cols_ref, win_ref, state_ref, table_ref, out_ref, picked_ref, *, columns):
    half = table_ref.shape[2]
    feats = cols_ref.shape[0]
    blocks = state_ref.shape[1] // LANES
    cols = cols_ref[...].astype(f32)
    feat = lax.broadcasted_iota(i32, (feats, K), 0)
    for step in range(ITERS):
        owner = win_ref[step : step + 1] // columns
        place = jnp.where(feat == owner, 1.0, 0.0).astype(bf16)
        for j in range(blocks):
            piece = cols[:, step * blocks + j, :].astype(bf16)
            picked = lax.dot_general(
                place, piece, (((0,), (0,)), ((), ())), preferred_element_type=f32
            )
            picked_ref[step, :, j * LANES : (j + 1) * LANES] = picked.astype(bf16)
    resid, prob = residuals(state_ref[:K], state_ref[K : K + 1])
    tile = sums_tile(resid, prob, picked_ref[0].astype(f32))
    out_ref[:, :, :half] = table_ref[...]
    out_ref[:, :, half:] = jnp.broadcast_to(tile[None], (out_ref.shape[0], 8, 2 * K))


def next_table_body(
    shared_ref, logits_ref, logits_taken_ref, state_ref, state_taken_ref, picked_ref,
    picked_taken_ref, geno_ref, taken_ref, out_ref, new_ref, *rest, step,
):
    half = taken_ref.shape[1]
    last = step == ITERS - 1
    new_taken_ref = None if last else rest[0]
    both_ref, sem_ref = rest[-2:]
    copies = load_halves(geno_ref, taken_ref, both_ref, sem_ref)
    coef = coefficients(shared_ref, half)
    coef = lane_tile(coef, new_ref.shape[1] // LANES)
    logits = logits_ref[:K] + coef * picked_ref[step].astype(f32)
    new_ref[...] = logits
    resid, prob = residuals(logits, state_ref[K : K + 1])
    if not last:
        tile = sums_tile(resid, prob, picked_ref[step + 1].astype(f32))
        out_ref[:, :, half:] = jnp.broadcast_to(tile[None], (out_ref.shape[0], 8, 2 * K))
    logits_taken = logits_taken_ref[:K] + coef * picked_taken_ref[step].astype(f32)
    if not last:
        new_taken_ref[...] = logits_taken
    resid_taken, _ = residuals(logits_taken, state_taken_ref[K : K + 1])
    for copy in copies:
        copy.wait()
    table = half_table(resid, resid_taken, both_ref)
    out_ref[:, :, :half] = table.reshape(out_ref.shape[0], -1, half).astype(bf16)


def shards(genotypes, labels, base_margin, winners):
    samples, columns = genotypes.shape
    feat_count = lax.axis_size("feat")
    rows_count = lax.axis_size("rows")
    class_share = K // rows_count
    half = columns // 2
    side = lax.rem(lax.axis_index("rows"), 2)
    partners = [(i, i ^ 1) for i in range(rows_count)]
    shape = jax.ShapeDtypeStruct
    work = 2 * K * 2 * samples * half
    halves = [pltpu.VMEM((2 * samples, half), bf16), pltpu.SemaphoreType.DMA((2,))]

    sent = call(
        pick_body,
        shape((feat_count, ITERS * samples // LANES, LANES), bf16),
        [VMEM, HBM],
        [pltpu.VMEM((ITERS, samples, LANES), bf16), pltpu.SemaphoreType.DMA((ITERS,))],
        moved=samples * LANES * 4,
        room=None,
    )(winners, genotypes)
    cols = lax.all_to_all(sent, "feat", 0, 0, tiled=True)

    sent, geno, margin, marks = lax.optimization_barrier(
        (sent, genotypes, base_margin, labels)
    )
    given = lax.dynamic_slice_in_dim(geno, (1 - side) * half, half, 1)
    taken = lax.ppermute(given, "rows", partners)
    state = jnp.concatenate(
        [margin.T, jnp.broadcast_to(marks.astype(f32)[None, :], (8, samples))]
    )
    state_taken = lax.ppermute(state, "rows", partners)

    table = call(
        first_table_body,
        shape((rows_count, class_share, half), bf16),
        [VMEM, VMEM, HBM, HBM],
        halves,
        flops=work,
        moved=4 * samples * half,
    )(state, state_taken, genotypes, taken)

    def first_sums(*refs):
        first_sums_body(*refs, columns=columns)

    payload, picked = call(
        first_sums,
        (
            shape((rows_count, class_share, half + 2 * K), bf16),
            shape((ITERS, K, samples), bf16),
        ),
        [VMEM] * 4,
        moved=4 * samples * half,
    )(cols, winners, state, table)
    shared0 = lax.all_to_all(payload, "rows", 0, 0, tiled=True)
    picked_taken = lax.ppermute(picked, "rows", partners)

    def second(*refs):
        next_table_body(*refs, step=0)

    payload, logits, logits_taken = call(
        second,
        (
            shape((rows_count, class_share, half + 2 * K), bf16),
            shape((K, samples), f32),
            shape((K, samples), f32),
        ),
        [VMEM] * 7 + [HBM] * 2,
        halves,
        flops=work,
        moved=4 * samples * half,
    )(shared0, state, state_taken, state, state_taken, picked, picked_taken, genotypes, taken)
    shared1 = lax.all_to_all(payload, "rows", 0, 0, tiled=True)

    def third(*refs):
        next_table_body(*refs, step=1)

    payload, logits = call(
        third,
        (shape((rows_count, class_share, half), bf16), shape((K, samples), f32)),
        [VMEM] * 7 + [HBM] * 2,
        halves,
        flops=work,
        moved=4 * samples * half,
    )(shared1, logits, logits_taken, state, state_taken, picked, picked_taken, genotypes, taken)
    shared2 = lax.all_to_all(payload, "rows", 0, 0, tiled=True)

    tables = []
    for shared in (shared0, shared1, shared2):
        parts = shared[:, :, :half].astype(f32).reshape(rows_count // 2, 2, class_share, half)
        total = jnp.sum(parts, axis=0)
        tables.append(jnp.concatenate([total[0], total[1]], axis=1))
    return (logits.T, jnp.stack(tables))


def solution(mesh):
    in_specs = (P("rows", "feat"), P("rows"), P("rows", None), P())
    out_specs = (P("rows", None), P(None, "rows", "feat"))
    return jax.shard_map(shards, mesh=mesh, in_specs=in_specs, out_specs=out_specs, check_vma=False)
```

```python
import jax
import jax.numpy as jnp
from jax import lax
from jax.experimental import pallas as pl
from jax.experimental.pallas import tpu as pltpu
from jax.sharding import PartitionSpec as P

K = 64
ITERS = 2
LANES = 128


shrink_rate = 0.5
ridge_term = 1.0

bf16 = jnp.bfloat16
f32 = jnp.float32
i32 = jnp.int32
BlockSpec = pl.BlockSpec
VMEM = pl.BlockSpec(memory_space=pltpu.VMEM)
HBM = pl.BlockSpec(memory_space=pltpu.HBM)


def call(body, out_shape, in_specs, scratch=(), flops=0, moved=0, room=16 << 20):
    out_specs = jax.tree.map(
        lambda out: BlockSpec(memory_space=out.memory_space), out_shape, is_leaf=is_out
    )
    return pl.pallas_call(
        body,
        out_shape=out_shape,
        in_specs=in_specs,
        out_specs=out_specs,
        scratch_shapes=list(scratch),
        cost_estimate=pl.CostEstimate(flops=flops, bytes_accessed=moved, transcendentals=0),
        compiler_params=pltpu.CompilerParams(vmem_limit_bytes=room),
    )


def is_out(value):
    return hasattr(value, "memory_space")


def far(values):
    return pltpu.with_memory_space_constraint(values, pltpu.HBM)


def load(pairs, sem_ref):
    copies = [
        pltpu.make_async_copy(source, target, sem_ref.at[i])
        for i, (source, target) in enumerate(pairs)
    ]
    for copy in copies:
        copy.start()
    return copies


def wait_all(copies):
    for copy in copies:
        copy.wait()


def near(values):
    return pltpu.with_memory_space_constraint(values, pltpu.VMEM)


def rounded(values):
    return values.astype(bf16).astype(f32)


def split3(values):
    high = rounded(values)
    rest = values - high
    middle = rounded(rest)
    return high, middle, rest - middle


def softmax_classes(values):
    top = jnp.max(values, axis=0, keepdims=True)
    expo = jnp.exp(values - top)
    return expo / jnp.sum(expo, axis=0, keepdims=True)


def residuals(logits, label_row):
    prob = softmax_classes(logits)
    classes = lax.broadcasted_iota(i32, logits.shape, 0).astype(f32)
    onehot = jnp.where(classes == label_row, 1.0, 0.0)
    return (onehot - prob).astype(bf16), prob


def pick_body(win_ref, geno_ref, out_ref, given_ref, block_ref, sem_ref):
    samples, columns = geno_ref.shape
    half = given_ref.shape[1]
    side = lax.rem(lax.axis_index("rows"), 2)
    other = pl.multiple_of((1 - side) * half, LANES)
    give = pltpu.make_async_copy(geno_ref.at[:, pl.ds(other, half)], given_ref, sem_ref.at[ITERS])
    give.start()
    local = win_ref[...] - lax.axis_index("feat") * columns
    mine = jnp.where((local >= 0) & (local < columns), local, 0).astype(f32)
    copies, lanes = [], []
    for step in range(ITERS):
        col = jnp.sum(mine[step : step + 1]).astype(i32)
        start = pl.multiple_of((col // LANES) * LANES, LANES)
        copy = pltpu.make_async_copy(
            geno_ref.at[:, pl.ds(start, LANES)], block_ref.at[step], sem_ref.at[step]
        )
        copy.start()
        copies.append(copy)
        lanes.append(col - start)
    rows = lax.broadcasted_iota(i32, (8, LANES), 0)
    lane = lax.broadcasted_iota(i32, (8, LANES), 1)
    tile = jnp.zeros((8, LANES), f32)
    for step in range(ITERS):
        copies[step].wait()
        pick = jnp.where(lane == lanes[step], 1.0, 0.0).astype(bf16)
        x = lax.dot_general(
            pick, block_ref[step], (((1,), (1,)), ((), ())), preferred_element_type=f32
        )
        for j in range(samples // LANES):
            here = rows == step * (samples // LANES) + j
            tile = tile + jnp.where(here, x[:, j * LANES : (j + 1) * LANES], 0.0)
    out_ref[...] = jnp.broadcast_to(tile.astype(bf16)[None], out_ref.shape)
    give.wait()


def load_halves(geno_ref, taken_ref, both_ref, sem_ref):
    samples, half = taken_ref.shape
    side = lax.rem(lax.axis_index("rows"), 2)
    start = pl.multiple_of(side * half, LANES)
    first = pltpu.make_async_copy(
        geno_ref.at[:, pl.ds(start, half)], both_ref.at[pl.ds(0, samples)], sem_ref.at[0]
    )
    second = pltpu.make_async_copy(taken_ref, both_ref.at[pl.ds(samples, samples)], sem_ref.at[1])
    first.start()
    second.start()
    return first, second


def half_table(resid, resid_taken, both_ref):
    whole = jnp.concatenate([resid, resid_taken], axis=1)
    return jnp.dot(whole, both_ref[...], preferred_element_type=f32)


def sums_tile(resid, prob, picked):
    grad = resid.astype(f32) * picked
    curv = prob * (1.0 - prob) * picked * picked
    both = 0.5 * jnp.concatenate([grad, curv], axis=0)
    folded = both[:, :LANES]
    for j in range(1, both.shape[1] // LANES):
        folded = folded + both[:, j * LANES : (j + 1) * LANES]
    ones = jnp.ones((8, LANES), bf16)
    total = jnp.zeros((8, 2 * K), f32)
    for term in split3(folded):
        total = total + lax.dot_general(
            ones, term.astype(bf16), (((1,), (1,)), ((), ())), preferred_element_type=f32
        )
    high, middle, low = split3(total)
    row = lax.broadcasted_iota(i32, total.shape, 0)
    tile = jnp.where(row == 0, high, jnp.where(row == 1, middle, jnp.where(row == 2, low, 0.0)))
    return tile.astype(bf16)


def coefficients(tiles):
    tiles = tiles.astype(f32)
    row = jnp.sum(jnp.sum(tiles, axis=0), axis=0, keepdims=True)
    column = jnp.transpose(jnp.broadcast_to(row, (2 * K, LANES)))
    return shrink_rate * (2.0 * column[:K]) / (2.0 * column[K:] + ridge_term)


def lane_tile(values, count):
    return jnp.concatenate([values] * count, axis=1)


def send_tile(tile, both_ref, out_ref, sem_ref):
    half = out_ref.shape[2] - 2 * K
    both_ref[...] = jnp.broadcast_to(tile[None], both_ref.shape)
    copy = pltpu.make_async_copy(both_ref, out_ref.at[:, :, pl.ds(half, 2 * K)], sem_ref)
    copy.start()
    return copy


def send_table(resid, resid_taken, both_ref, table_ref, out_ref, sem_ref, pieces=2):
    whole = jnp.concatenate([resid, resid_taken], axis=1)
    width = table_ref.shape[2] // pieces
    copies = []
    for piece in range(pieces):
        span = pl.ds(piece * width, width)
        table = jnp.dot(whole, both_ref[:, span], preferred_element_type=f32)
        table_ref[:, :, span] = table.reshape(table_ref.shape[0], -1, width).astype(bf16)
        copy = pltpu.make_async_copy(
            table_ref.at[:, :, span], out_ref.at[:, :, span], sem_ref.at[piece]
        )
        copy.start()
        copies.append(copy)
    return copies


def first_table_body(
    state_ref, state_taken_ref, geno_ref, taken_ref, out_ref, both_ref, sem_ref
):
    copies = load_halves(geno_ref, taken_ref, both_ref, sem_ref)
    resid, _ = residuals(state_ref[:K], state_ref[K : K + 1])
    resid_taken, _ = residuals(state_taken_ref[:K], state_taken_ref[K : K + 1])
    for copy in copies:
        copy.wait()
    table = half_table(resid, resid_taken, both_ref)
    out_ref[...] = table.reshape(out_ref.shape).astype(bf16)


def first_sums_body(
    cols_ref, far_win_ref, state_ref, table_ref, out_ref, far_picked_ref, tiles_ref, picked_ref,
    win_ref, sem_ref, *, columns,
):
    half = table_ref.shape[2]
    blocks = state_ref.shape[1] // LANES
    first = pltpu.make_async_copy(
        table_ref, out_ref.at[:, :, pl.ds(0, half)], sem_ref.at[0]
    )
    wins = pltpu.make_async_copy(far_win_ref, win_ref, sem_ref.at[3])
    wins.start()
    first.start()
    resid, prob = residuals(state_ref[:K], state_ref[K : K + 1])
    cols = cols_ref[...].astype(f32)
    feat = lax.broadcasted_iota(i32, (cols.shape[0], K), 0)
    wins.wait()
    for step in range(ITERS):
        owner = win_ref[step : step + 1] // columns
        place = jnp.where(feat == owner, 1.0, 0.0).astype(bf16)
        for j in range(blocks):
            piece = cols[:, step * blocks + j, :].astype(bf16)
            picked = lax.dot_general(
                place, piece, (((0,), (0,)), ((), ())), preferred_element_type=f32
            )
            picked_ref[step, :, j * LANES : (j + 1) * LANES] = picked.astype(bf16)
    third = pltpu.make_async_copy(picked_ref, far_picked_ref, sem_ref.at[2])
    third.start()
    tile = sums_tile(resid, prob, picked_ref[0].astype(f32))
    second = send_tile(tile, tiles_ref, out_ref, sem_ref.at[1])
    wait_all([first, second, third])


def second_table_body(
    shared_ref, state_ref, far_state_ref, far_picked_ref, far_picked_taken_ref, geno_ref,
    taken_ref, out_ref, far_coef_ref, both_ref, table_ref, tiles_ref, got_ref, state_taken_ref,
    picked_ref, picked_taken_ref, coef_ref, sem_ref, load_ref,
):
    half = taken_ref.shape[1]
    loads = load(
        [
            (shared_ref.at[:, :, pl.ds(half, 2 * K)], got_ref),
            (far_picked_ref, picked_ref),
            (far_state_ref, state_taken_ref),
            (far_picked_taken_ref, picked_taken_ref),
        ],
        load_ref,
    )
    copies = load_halves(geno_ref, taken_ref, both_ref, sem_ref)
    loads[0].wait()
    coef = coefficients(got_ref[...])
    coef_ref[...] = coef
    coef_copy = pltpu.make_async_copy(coef_ref, far_coef_ref, sem_ref.at[5])
    coef_copy.start()
    coef = lane_tile(coef, state_ref.shape[1] // LANES)
    loads[1].wait()
    logits = state_ref[:K] + coef * picked_ref[0].astype(f32)
    resid, prob = residuals(logits, state_ref[K : K + 1])
    tile = sums_tile(resid, prob, picked_ref[1].astype(f32))
    sums_copy = send_tile(tile, tiles_ref, out_ref, sem_ref.at[2])
    wait_all(loads[2:])
    logits_taken = state_taken_ref[:K] + coef * picked_taken_ref[0].astype(f32)
    resid_taken, _ = residuals(logits_taken, state_taken_ref[K : K + 1])
    wait_all(copies)
    table_copies = send_table(
        resid, resid_taken, both_ref, table_ref, out_ref, sem_ref.at[pl.ds(3, 2)]
    )
    wait_all([coef_copy, sums_copy] + table_copies)


def third_table_body(
    shared_ref, far_coef_ref, state_ref, far_state_ref, far_picked_ref, far_picked_taken_ref,
    geno_ref, taken_ref, out_ref, logits_ref, both_ref, table_ref, new_ref, got_ref,
    state_taken_ref, picked_ref, picked_taken_ref, coef_ref, sem_ref, load_ref,
):
    half = taken_ref.shape[1]
    loads = load(
        [
            (shared_ref.at[:, :, pl.ds(half, 2 * K)], got_ref),
            (far_coef_ref, coef_ref),
            (far_picked_ref, picked_ref),
            (far_state_ref, state_taken_ref),
            (far_picked_taken_ref, picked_taken_ref),
        ],
        load_ref,
    )
    copies = load_halves(geno_ref, taken_ref, both_ref, sem_ref)
    blocks = state_ref.shape[1] // LANES
    wait_all(loads[:2])
    coefs = [lane_tile(coef, blocks) for coef in (coef_ref[...], coefficients(got_ref[...]))]

    def updated(start, columns_ref):
        for step in range(ITERS):
            start = start + coefs[step] * columns_ref[step].astype(f32)
        return start

    loads[2].wait()
    logits = updated(state_ref[:K], picked_ref)
    new_ref[...] = logits
    logits_copy = pltpu.make_async_copy(new_ref, logits_ref, sem_ref.at[2])
    logits_copy.start()
    resid, _ = residuals(logits, state_ref[K : K + 1])
    wait_all(loads[3:])
    resid_taken, _ = residuals(
        updated(state_taken_ref[:K], picked_taken_ref), state_taken_ref[K : K + 1]
    )
    wait_all(copies)
    table_copies = send_table(
        resid, resid_taken, both_ref, table_ref, out_ref, sem_ref.at[pl.ds(3, 2)]
    )
    wait_all([logits_copy] + table_copies)


def shards(genotypes, labels, base_margin, winners):
    samples, columns = genotypes.shape
    feat_count = lax.axis_size("feat")
    rows_count = lax.axis_size("rows")
    class_share = K // rows_count
    half = columns // 2
    partners = [(i, i ^ 1) for i in range(rows_count)]
    work = 2 * K * 2 * samples * half
    payload_shape = (rows_count, class_share, half + 2 * K)
    table_shape = (rows_count, class_share, half)
    tiles = pltpu.VMEM((rows_count, 8, 2 * K), bf16)
    both = pltpu.VMEM((2 * samples, half), bf16)
    sems = pltpu.SemaphoreType.DMA
    loaded = [
        tiles,
        pltpu.VMEM((K + 8, samples), f32),
        pltpu.VMEM((ITERS, K, samples), bf16),
        pltpu.VMEM((ITERS, K, samples), bf16),
        pltpu.VMEM((K, LANES), f32),
    ]

    sent, given = call(
        pick_body,
        (
            pltpu.VMEM((feat_count, ITERS * samples // LANES, LANES), bf16),
            pltpu.HBM((samples, half), bf16),
        ),
        [VMEM, HBM],
        [pltpu.VMEM((ITERS, samples, LANES), bf16), sems((ITERS + 1,))],
        moved=samples * LANES * 4,
        room=None,
    )(winners, genotypes)
    cols = lax.all_to_all(sent, "feat", 0, 0, tiled=True)

    sent, margin, marks = lax.optimization_barrier((sent, base_margin, labels))
    state = jnp.concatenate(
        [margin.T, jnp.broadcast_to(marks.astype(f32)[None, :], (8, samples))]
    )
    state, given = lax.optimization_barrier((state, given))
    taken = lax.ppermute(given, "rows", partners)
    state_taken = far(lax.ppermute(state, "rows", partners))
    state = near(state)

    table = call(
        first_table_body,
        pltpu.VMEM(table_shape, bf16),
        [VMEM, VMEM, HBM, HBM],
        [both, sems((2,))],
        flops=work,
        moved=4 * samples * half,
    )(state, state_taken, genotypes, taken)

    def first_sums(*refs):
        first_sums_body(*refs, columns=columns)

    payload, picked = call(
        first_sums,
        (pltpu.HBM(payload_shape, bf16), pltpu.HBM((ITERS, K, samples), bf16)),
        [VMEM, HBM, VMEM, VMEM],
        [tiles, pltpu.VMEM((ITERS, K, samples), bf16), pltpu.VMEM((ITERS, K), i32), sems((4,))],
        moved=4 * samples * half,
    )(near(cols), far(winners), state, table)
    shared0 = lax.all_to_all(payload, "rows", 0, 0, tiled=True)
    picked_taken = far(lax.ppermute(picked, "rows", partners))

    payload, coef = call(
        second_table_body,
        (pltpu.HBM(payload_shape, bf16), pltpu.HBM((K, LANES), f32)),
        [HBM, VMEM] + [HBM] * 5,
        [both, pltpu.VMEM(table_shape, bf16), tiles] + loaded + [sems((6,)), sems((4,))],
        flops=work,
        moved=4 * samples * half,
    )(far(shared0), state, state_taken, picked, picked_taken, genotypes, taken)
    shared1 = lax.all_to_all(payload, "rows", 0, 0, tiled=True)

    payload, logits = call(
        third_table_body,
        (pltpu.HBM(table_shape, bf16), pltpu.HBM((K, samples), f32)),
        [HBM, HBM, VMEM] + [HBM] * 5,
        [both, pltpu.VMEM(table_shape, bf16), pltpu.VMEM((K, samples), f32)]
        + loaded
        + [sems((5,)), sems((5,))],
        flops=work,
        moved=4 * samples * half,
    )(far(shared1), far(coef), state, state_taken, picked, picked_taken, genotypes, taken)
    shared2 = lax.all_to_all(payload, "rows", 0, 0, tiled=True)

    tables = []
    for shared in (shared0, shared1, shared2):
        parts = shared[:, :, :half].astype(f32).reshape(rows_count // 2, 2, class_share, half)
        total = jnp.sum(parts, axis=0)
        tables.append(jnp.concatenate([total[0], total[1]], axis=1))
    return (logits.T, jnp.stack(tables))


def solution(mesh):
    in_specs = (P("rows", "feat"), P("rows"), P("rows", None), P())
    out_specs = (P("rows", None), P(None, "rows", "feat"))
    return jax.shard_map(shards, mesh=mesh, in_specs=in_specs, out_specs=out_specs, check_vma=False)
```

```python
import jax
import jax.numpy as jnp
from jax import lax
from jax.experimental import pallas as pl
from jax.experimental.pallas import tpu as pltpu
from jax.sharding import PartitionSpec as P

K = 64
ITERS = 2
LANES = 128


shrink_rate = 0.5
ridge_term = 1.0

bf16 = jnp.bfloat16
f32 = jnp.float32
i32 = jnp.int32
BlockSpec = pl.BlockSpec
VMEM = pl.BlockSpec(memory_space=pltpu.VMEM)
HBM = pl.BlockSpec(memory_space=pltpu.HBM)


def call(body, out_shape, in_specs, scratch=(), flops=0, moved=0, room=16 << 20):
    out_specs = jax.tree.map(
        lambda out: BlockSpec(memory_space=out.memory_space), out_shape, is_leaf=is_out
    )
    return pl.pallas_call(
        body,
        out_shape=out_shape,
        in_specs=in_specs,
        out_specs=out_specs,
        scratch_shapes=list(scratch),
        cost_estimate=pl.CostEstimate(flops=flops, bytes_accessed=moved, transcendentals=0),
        compiler_params=pltpu.CompilerParams(vmem_limit_bytes=room),
    )


def is_out(value):
    return hasattr(value, "memory_space")


def far(values):
    return pltpu.with_memory_space_constraint(values, pltpu.HBM)


def load(pairs, sem_ref):
    copies = [
        pltpu.make_async_copy(source, target, sem_ref.at[i])
        for i, (source, target) in enumerate(pairs)
    ]
    for copy in copies:
        copy.start()
    return copies


def wait_all(copies):
    for copy in copies:
        copy.wait()


def near(values):
    return pltpu.with_memory_space_constraint(values, pltpu.VMEM)


def rounded(values):
    return values.astype(bf16).astype(f32)


def split3(values):
    high = rounded(values)
    rest = values - high
    middle = rounded(rest)
    return high, middle, rest - middle


def softmax_classes(values):
    top = jnp.max(values, axis=0, keepdims=True)
    expo = jnp.exp(values - top)
    return expo / jnp.sum(expo, axis=0, keepdims=True)


def residuals(logits, label_row):
    prob = softmax_classes(logits)
    classes = lax.broadcasted_iota(i32, logits.shape, 0).astype(f32)
    onehot = jnp.where(classes == label_row, 1.0, 0.0)
    return (onehot - prob).astype(bf16), prob


def pick_body(
    win_ref, geno_ref, margin_ref, labels_ref, out_ref, given_ref, state_ref, block_ref, half_ref,
    sem_ref,
):
    samples, columns = geno_ref.shape
    half = given_ref.shape[1]
    side = lax.rem(lax.axis_index("rows"), 2)
    other = pl.multiple_of((1 - side) * half, LANES)
    give = pltpu.make_async_copy(geno_ref.at[:, pl.ds(other, half)], half_ref, sem_ref.at[ITERS])
    give.start()
    margins = pltpu.make_async_copy(margin_ref, state_ref.at[pl.ds(0, K)], sem_ref.at[ITERS + 1])
    margins.start()
    state_ref[K:] = jnp.broadcast_to(labels_ref[...].astype(f32), (8, samples))
    local = win_ref[...] - lax.axis_index("feat") * columns
    mine = jnp.where((local >= 0) & (local < columns), local, 0).astype(f32)
    copies, lanes = [], []
    for step in range(ITERS):
        col = jnp.sum(mine[step : step + 1]).astype(i32)
        start = pl.multiple_of((col // LANES) * LANES, LANES)
        copy = pltpu.make_async_copy(
            geno_ref.at[:, pl.ds(start, LANES)], block_ref.at[step], sem_ref.at[step]
        )
        copy.start()
        copies.append(copy)
        lanes.append(col - start)
    rows = lax.broadcasted_iota(i32, (8, LANES), 0)
    lane = lax.broadcasted_iota(i32, (8, LANES), 1)
    tile = jnp.zeros((8, LANES), f32)
    give.wait()
    give = pltpu.make_async_copy(half_ref, given_ref, sem_ref.at[ITERS])
    give.start()
    for step in range(ITERS):
        copies[step].wait()
        pick = jnp.where(lane == lanes[step], 1.0, 0.0).astype(bf16)
        x = lax.dot_general(
            pick, block_ref[step], (((1,), (1,)), ((), ())), preferred_element_type=f32
        )
        for j in range(samples // LANES):
            here = rows == step * (samples // LANES) + j
            tile = tile + jnp.where(here, x[:, j * LANES : (j + 1) * LANES], 0.0)
    out_ref[...] = jnp.broadcast_to(tile.astype(bf16)[None], out_ref.shape)
    margins.wait()
    give.wait()


def load_halves(geno_ref, taken_ref, both_ref, sem_ref):
    samples, half = taken_ref.shape
    side = lax.rem(lax.axis_index("rows"), 2)
    start = pl.multiple_of(side * half, LANES)
    first = pltpu.make_async_copy(
        geno_ref.at[:, pl.ds(start, half)], both_ref.at[pl.ds(0, samples)], sem_ref.at[0]
    )
    second = pltpu.make_async_copy(taken_ref, both_ref.at[pl.ds(samples, samples)], sem_ref.at[1])
    first.start()
    second.start()
    return first, second


def half_table(resid, resid_taken, both_ref):
    whole = jnp.concatenate([resid, resid_taken], axis=1)
    return jnp.dot(whole, both_ref[...], preferred_element_type=f32)


def sums_tile(resid, prob, picked):
    grad = resid.astype(f32) * picked
    curv = prob * (1.0 - prob) * picked * picked
    both = 0.5 * jnp.concatenate([grad, curv], axis=0)
    folded = both[:, :LANES]
    for j in range(1, both.shape[1] // LANES):
        folded = folded + both[:, j * LANES : (j + 1) * LANES]
    ones = jnp.ones((8, LANES), bf16)
    total = jnp.zeros((8, 2 * K), f32)
    for term in split3(folded):
        total = total + lax.dot_general(
            ones, term.astype(bf16), (((1,), (1,)), ((), ())), preferred_element_type=f32
        )
    high, middle, low = split3(total)
    row = lax.broadcasted_iota(i32, total.shape, 0)
    tile = jnp.where(row == 0, high, jnp.where(row == 1, middle, jnp.where(row == 2, low, 0.0)))
    return tile.astype(bf16)


def coefficients(tiles):
    tiles = tiles.astype(f32)
    row = jnp.sum(jnp.sum(tiles, axis=0), axis=0, keepdims=True)
    column = jnp.transpose(jnp.broadcast_to(row, (2 * K, LANES)))
    return shrink_rate * (2.0 * column[:K]) / (2.0 * column[K:] + ridge_term)


def lane_tile(values, count):
    return jnp.concatenate([values] * count, axis=1)


def send_tile(tile, both_ref, out_ref, sem_ref):
    half = out_ref.shape[2] - 2 * K
    both_ref[...] = jnp.broadcast_to(tile[None], both_ref.shape)
    copy = pltpu.make_async_copy(both_ref, out_ref.at[:, :, pl.ds(half, 2 * K)], sem_ref)
    copy.start()
    return copy


def send_table(resid, resid_taken, both_ref, table_ref, out_ref, sem_ref, pieces=2):
    whole = jnp.concatenate([resid, resid_taken], axis=1)
    width = table_ref.shape[2] // pieces
    copies = []
    for piece in range(pieces):
        span = pl.ds(piece * width, width)
        table = jnp.dot(whole, both_ref[:, span], preferred_element_type=f32)
        table_ref[:, :, span] = table.reshape(table_ref.shape[0], -1, width).astype(bf16)
        copy = pltpu.make_async_copy(
            table_ref.at[:, :, span], out_ref.at[:, :, span], sem_ref.at[piece]
        )
        copy.start()
        copies.append(copy)
    return copies


def first_table_body(
    state_ref, state_taken_ref, geno_ref, taken_ref, out_ref, both_ref, sem_ref
):
    copies = load_halves(geno_ref, taken_ref, both_ref, sem_ref)
    resid, _ = residuals(state_ref[:K], state_ref[K : K + 1])
    resid_taken, _ = residuals(state_taken_ref[:K], state_taken_ref[K : K + 1])
    for copy in copies:
        copy.wait()
    table = half_table(resid, resid_taken, both_ref)
    out_ref[...] = table.reshape(out_ref.shape).astype(bf16)


def first_sums_body(
    cols_ref, far_win_ref, state_ref, table_ref, out_ref, far_picked_ref, tiles_ref, picked_ref,
    win_ref, sem_ref, *, columns,
):
    half = table_ref.shape[2]
    blocks = state_ref.shape[1] // LANES
    first = pltpu.make_async_copy(
        table_ref, out_ref.at[:, :, pl.ds(0, half)], sem_ref.at[0]
    )
    wins = pltpu.make_async_copy(far_win_ref, win_ref, sem_ref.at[3])
    wins.start()
    first.start()
    resid, prob = residuals(state_ref[:K], state_ref[K : K + 1])
    cols = cols_ref[...].astype(f32)
    feat = lax.broadcasted_iota(i32, (cols.shape[0], K), 0)
    wins.wait()
    for step in range(ITERS):
        owner = win_ref[step : step + 1] // columns
        place = jnp.where(feat == owner, 1.0, 0.0).astype(bf16)
        for j in range(blocks):
            piece = cols[:, step * blocks + j, :].astype(bf16)
            picked = lax.dot_general(
                place, piece, (((0,), (0,)), ((), ())), preferred_element_type=f32
            )
            picked_ref[step, :, j * LANES : (j + 1) * LANES] = picked.astype(bf16)
    third = pltpu.make_async_copy(picked_ref, far_picked_ref, sem_ref.at[2])
    third.start()
    tile = sums_tile(resid, prob, picked_ref[0].astype(f32))
    second = send_tile(tile, tiles_ref, out_ref, sem_ref.at[1])
    wait_all([first, second, third])


def second_table_body(
    shared_ref, state_ref, far_state_ref, far_picked_ref, far_picked_taken_ref, geno_ref,
    taken_ref, out_ref, far_coef_ref, both_ref, table_ref, tiles_ref, got_ref, state_taken_ref,
    picked_ref, picked_taken_ref, coef_ref, sem_ref, load_ref,
):
    half = taken_ref.shape[1]
    loads = load(
        [
            (shared_ref.at[:, :, pl.ds(half, 2 * K)], got_ref),
            (far_picked_ref, picked_ref),
            (far_state_ref, state_taken_ref),
            (far_picked_taken_ref, picked_taken_ref),
        ],
        load_ref,
    )
    copies = load_halves(geno_ref, taken_ref, both_ref, sem_ref)
    loads[0].wait()
    coef = coefficients(got_ref[...])
    coef_ref[...] = coef
    coef_copy = pltpu.make_async_copy(coef_ref, far_coef_ref, sem_ref.at[5])
    coef_copy.start()
    coef = lane_tile(coef, state_ref.shape[1] // LANES)
    loads[1].wait()
    logits = state_ref[:K] + coef * picked_ref[0].astype(f32)
    resid, prob = residuals(logits, state_ref[K : K + 1])
    tile = sums_tile(resid, prob, picked_ref[1].astype(f32))
    sums_copy = send_tile(tile, tiles_ref, out_ref, sem_ref.at[2])
    wait_all(loads[2:])
    logits_taken = state_taken_ref[:K] + coef * picked_taken_ref[0].astype(f32)
    resid_taken, _ = residuals(logits_taken, state_taken_ref[K : K + 1])
    wait_all(copies)
    table_copies = send_table(
        resid, resid_taken, both_ref, table_ref, out_ref, sem_ref.at[pl.ds(3, 2)]
    )
    wait_all([coef_copy, sums_copy] + table_copies)


def third_table_body(
    shared_ref, far_coef_ref, state_ref, far_state_ref, far_picked_ref, far_picked_taken_ref,
    geno_ref, taken_ref, out_ref, logits_ref, both_ref, table_ref, new_ref, got_ref,
    state_taken_ref, picked_ref, picked_taken_ref, coef_ref, sem_ref, load_ref,
):
    half = taken_ref.shape[1]
    loads = load(
        [
            (shared_ref.at[:, :, pl.ds(half, 2 * K)], got_ref),
            (far_coef_ref, coef_ref),
            (far_picked_ref, picked_ref),
            (far_state_ref, state_taken_ref),
            (far_picked_taken_ref, picked_taken_ref),
        ],
        load_ref,
    )
    copies = load_halves(geno_ref, taken_ref, both_ref, sem_ref)
    blocks = state_ref.shape[1] // LANES
    wait_all(loads[:2])
    coefs = [lane_tile(coef, blocks) for coef in (coef_ref[...], coefficients(got_ref[...]))]

    def updated(start, columns_ref):
        for step in range(ITERS):
            start = start + coefs[step] * columns_ref[step].astype(f32)
        return start

    loads[2].wait()
    logits = updated(state_ref[:K], picked_ref)
    new_ref[...] = logits
    logits_copy = pltpu.make_async_copy(new_ref, logits_ref, sem_ref.at[2])
    logits_copy.start()
    resid, _ = residuals(logits, state_ref[K : K + 1])
    wait_all(loads[3:])
    resid_taken, _ = residuals(
        updated(state_taken_ref[:K], picked_taken_ref), state_taken_ref[K : K + 1]
    )
    wait_all(copies)
    table_copies = send_table(
        resid, resid_taken, both_ref, table_ref, out_ref, sem_ref.at[pl.ds(3, 2)]
    )
    wait_all([logits_copy] + table_copies)


def shards(genotypes, labels, base_margin, winners):
    samples, columns = genotypes.shape
    feat_count = lax.axis_size("feat")
    rows_count = lax.axis_size("rows")
    class_share = K // rows_count
    half = columns // 2
    partners = [(i, i ^ 1) for i in range(rows_count)]
    work = 2 * K * 2 * samples * half
    payload_shape = (rows_count, class_share, half + 2 * K)
    table_shape = (rows_count, class_share, half)
    tiles = pltpu.VMEM((rows_count, 8, 2 * K), bf16)
    both = pltpu.VMEM((2 * samples, half), bf16)
    sems = pltpu.SemaphoreType.DMA
    loaded = [
        tiles,
        pltpu.VMEM((K + 8, samples), f32),
        pltpu.VMEM((ITERS, K, samples), bf16),
        pltpu.VMEM((ITERS, K, samples), bf16),
        pltpu.VMEM((K, LANES), f32),
    ]

    sent, given, state = call(
        pick_body,
        (
            pltpu.VMEM((feat_count, ITERS * samples // LANES, LANES), bf16),
            pltpu.HBM((samples, half), bf16),
            pltpu.VMEM((K + 8, samples), f32),
        ),
        [VMEM, HBM, HBM, VMEM],
        [
            pltpu.VMEM((ITERS, samples, LANES), bf16),
            pltpu.VMEM((samples, half), bf16),
            sems((ITERS + 2,)),
        ],
        moved=samples * LANES * 4,
        room=None,
    )(winners, far(genotypes), far(base_margin.T), labels[None, :])
    cols = lax.all_to_all(sent, "feat", 0, 0, tiled=True)

    taken = lax.ppermute(given, "rows", partners)
    state_taken = far(lax.ppermute(state, "rows", partners))
    state = near(state)

    table = call(
        first_table_body,
        pltpu.VMEM(table_shape, bf16),
        [VMEM, VMEM, HBM, HBM],
        [both, sems((2,))],
        flops=work,
        moved=4 * samples * half,
    )(state, state_taken, genotypes, taken)

    def first_sums(*refs):
        first_sums_body(*refs, columns=columns)

    payload, picked = call(
        first_sums,
        (pltpu.HBM(payload_shape, bf16), pltpu.HBM((ITERS, K, samples), bf16)),
        [VMEM, HBM, VMEM, VMEM],
        [tiles, pltpu.VMEM((ITERS, K, samples), bf16), pltpu.VMEM((ITERS, K), i32), sems((4,))],
        moved=4 * samples * half,
    )(near(cols), far(winners), state, table)
    shared0 = lax.all_to_all(payload, "rows", 0, 0, tiled=True)
    picked_taken = far(lax.ppermute(picked, "rows", partners))

    payload, coef = call(
        second_table_body,
        (pltpu.HBM(payload_shape, bf16), pltpu.HBM((K, LANES), f32)),
        [HBM, VMEM] + [HBM] * 5,
        [both, pltpu.VMEM(table_shape, bf16), tiles] + loaded + [sems((6,)), sems((4,))],
        flops=work,
        moved=4 * samples * half,
    )(far(shared0), state, state_taken, far(picked), picked_taken, genotypes, taken)
    shared1 = lax.all_to_all(payload, "rows", 0, 0, tiled=True)

    payload, logits = call(
        third_table_body,
        (pltpu.HBM(table_shape, bf16), pltpu.HBM((K, samples), f32)),
        [HBM, HBM, VMEM] + [HBM] * 5,
        [both, pltpu.VMEM(table_shape, bf16), pltpu.VMEM((K, samples), f32)]
        + loaded
        + [sems((5,)), sems((5,))],
        flops=work,
        moved=4 * samples * half,
    )(far(shared1), far(coef), state, state_taken, far(picked), picked_taken, genotypes, taken)
    shared2 = lax.all_to_all(payload, "rows", 0, 0, tiled=True)

    tables = []
    for shared in (shared0, shared1, shared2):
        parts = shared[:, :, :half].astype(f32).reshape(rows_count // 2, 2, class_share, half)
        total = jnp.sum(parts, axis=0)
        tables.append(jnp.concatenate([total[0], total[1]], axis=1))
    return (logits.T, jnp.stack(tables))


def solution(mesh):
    in_specs = (P("rows", "feat"), P("rows"), P("rows", None), P())
    out_specs = (P("rows", None), P(None, "rows", "feat"))
    return jax.shard_map(shards, mesh=mesh, in_specs=in_specs, out_specs=out_specs, check_vma=False)
```

```python
import jax
import jax.numpy as jnp
from jax import lax
from jax.experimental import pallas as pl
from jax.experimental.pallas import tpu as pltpu
from jax.sharding import PartitionSpec as P

K = 64
ITERS = 2
LANES = 128


shrink_rate = 0.5
ridge_term = 1.0

bf16 = jnp.bfloat16
f32 = jnp.float32
i32 = jnp.int32
BlockSpec = pl.BlockSpec
VMEM = pl.BlockSpec(memory_space=pltpu.VMEM)
HBM = pl.BlockSpec(memory_space=pltpu.HBM)


def call(body, out_shape, in_specs, scratch=(), flops=0, moved=0, room=8 << 20):
    out_specs = jax.tree.map(
        lambda out: BlockSpec(memory_space=out.memory_space), out_shape, is_leaf=is_out
    )
    return pl.pallas_call(
        body,
        out_shape=out_shape,
        in_specs=in_specs,
        out_specs=out_specs,
        scratch_shapes=list(scratch),
        cost_estimate=pl.CostEstimate(flops=flops, bytes_accessed=moved, transcendentals=0),
        compiler_params=pltpu.CompilerParams(vmem_limit_bytes=room),
    )


def is_out(value):
    return hasattr(value, "memory_space")


def far(values):
    return pltpu.with_memory_space_constraint(values, pltpu.HBM)


def load(pairs, sem_ref):
    copies = [
        pltpu.make_async_copy(source, target, sem_ref.at[i])
        for i, (source, target) in enumerate(pairs)
    ]
    for copy in copies:
        copy.start()
    return copies


def wait_all(copies):
    for copy in copies:
        copy.wait()


def near(values):
    return pltpu.with_memory_space_constraint(values, pltpu.VMEM)


def rounded(values):
    return values.astype(bf16).astype(f32)


def split3(values):
    high = rounded(values)
    rest = values - high
    middle = rounded(rest)
    return high, middle, rest - middle


def softmax_classes(values):
    top = jnp.max(values, axis=0, keepdims=True)
    expo = jnp.exp(values - top)
    return expo / jnp.sum(expo, axis=0, keepdims=True)


def residuals(logits, label_row):
    prob = softmax_classes(logits)
    classes = lax.broadcasted_iota(i32, logits.shape, 0).astype(f32)
    onehot = jnp.where(classes == label_row, 1.0, 0.0)
    return (onehot - prob).astype(bf16), prob


def pick_body(
    win_ref, geno_ref, margin_ref, labels_ref, out_ref, state_ref, block_ref, sem_ref
):
    samples, columns = geno_ref.shape
    margins = pltpu.make_async_copy(margin_ref, state_ref.at[pl.ds(0, K)], sem_ref.at[ITERS])
    margins.start()
    state_ref[K:] = jnp.broadcast_to(labels_ref[...].astype(f32), (8, samples))
    local = win_ref[...] - lax.axis_index("feat") * columns
    mine = jnp.where((local >= 0) & (local < columns), local, 0).astype(f32)
    copies, lanes = [], []
    for step in range(ITERS):
        col = jnp.sum(mine[step : step + 1]).astype(i32)
        start = pl.multiple_of((col // LANES) * LANES, LANES)
        copy = pltpu.make_async_copy(
            geno_ref.at[:, pl.ds(start, LANES)], block_ref.at[step], sem_ref.at[step]
        )
        copy.start()
        copies.append(copy)
        lanes.append(col - start)
    rows = lax.broadcasted_iota(i32, (8, LANES), 0)
    lane = lax.broadcasted_iota(i32, (8, LANES), 1)
    tile = jnp.zeros((8, LANES), f32)
    for step in range(ITERS):
        copies[step].wait()
        pick = jnp.where(lane == lanes[step], 1.0, 0.0).astype(bf16)
        x = lax.dot_general(
            pick, block_ref[step], (((1,), (1,)), ((), ())), preferred_element_type=f32
        )
        for j in range(samples // LANES):
            here = rows == step * (samples // LANES) + j
            tile = tile + jnp.where(here, x[:, j * LANES : (j + 1) * LANES], 0.0)
    out_ref[...] = jnp.broadcast_to(tile.astype(bf16)[None], out_ref.shape)
    margins.wait()


def half_start(geno_ref):
    half = geno_ref.shape[1] // 2
    return pl.multiple_of(lax.rem(lax.axis_index("rows"), 2) * half, LANES)


def half_table(resid, resid_taken, geno_ref, taken_ref, start, width):
    own_span = pl.ds(pl.multiple_of(half_start(geno_ref) + start, LANES), width)
    first = jnp.dot(resid, geno_ref[:, own_span], preferred_element_type=f32)
    second = taken_ref[:, pl.ds(start, width)]
    return first + jnp.dot(resid_taken, second, preferred_element_type=f32)


def load_half(whole_ref, half_ref, sem_ref):
    start = half_start(whole_ref)
    copy = pltpu.make_async_copy(
        whole_ref.at[:, pl.ds(start, half_ref.shape[1])], half_ref, sem_ref
    )
    copy.start()
    return copy


def sums_tile(resid, prob, picked):
    grad = resid.astype(f32) * picked
    curv = prob * (1.0 - prob) * picked * picked
    both = 0.5 * jnp.concatenate([grad, curv], axis=0)
    folded = both[:, :LANES]
    for j in range(1, both.shape[1] // LANES):
        folded = folded + both[:, j * LANES : (j + 1) * LANES]
    ones = jnp.ones((8, LANES), bf16)
    total = jnp.zeros((8, 2 * K), f32)
    for term in split3(folded):
        total = total + lax.dot_general(
            ones, term.astype(bf16), (((1,), (1,)), ((), ())), preferred_element_type=f32
        )
    high, middle, low = split3(total)
    row = lax.broadcasted_iota(i32, total.shape, 0)
    tile = jnp.where(row == 0, high, jnp.where(row == 1, middle, jnp.where(row == 2, low, 0.0)))
    return tile.astype(bf16)


def coefficients(tiles):
    tiles = tiles.astype(f32)
    row = jnp.sum(jnp.sum(tiles, axis=0), axis=0, keepdims=True)
    column = jnp.transpose(jnp.broadcast_to(row, (2 * K, LANES)))
    return shrink_rate * (2.0 * column[:K]) / (2.0 * column[K:] + ridge_term)


def lane_tile(values, count):
    return jnp.concatenate([values] * count, axis=1)


def send_tile(tile, both_ref, out_ref, sem_ref):
    half = out_ref.shape[2] - 2 * K
    both_ref[...] = jnp.broadcast_to(tile[None], both_ref.shape)
    copy = pltpu.make_async_copy(both_ref, out_ref.at[:, :, pl.ds(half, 2 * K)], sem_ref)
    copy.start()
    return copy


def send_table(resid, resid_taken, geno_ref, taken_ref, table_ref, out_ref, sem_ref, pieces=2):
    width = table_ref.shape[2] // pieces
    copies = []
    for piece in range(pieces):
        span = pl.ds(piece * width, width)
        table = half_table(
            resid, resid_taken, geno_ref, taken_ref, piece * width, width
        )
        table_ref[:, :, span] = table.reshape(table_ref.shape[0], -1, width).astype(bf16)
        copy = pltpu.make_async_copy(
            table_ref.at[:, :, span], out_ref.at[:, :, span], sem_ref.at[piece]
        )
        copy.start()
        copies.append(copy)
    return copies


def first_table_body(
    state_ref, state_taken_ref, geno_ref, far_taken_ref, out_ref, taken_ref, sem_ref
):
    taken = load_half(far_taken_ref, taken_ref, sem_ref.at[0])
    resid, _ = residuals(state_ref[:K], state_ref[K : K + 1])
    resid_taken, _ = residuals(state_taken_ref[:K], state_taken_ref[K : K + 1])
    taken.wait()
    table = half_table(resid, resid_taken, geno_ref, taken_ref, 0, out_ref.shape[2])
    out_ref[...] = table.reshape(out_ref.shape).astype(bf16)


def first_sums_body(
    cols_ref, far_win_ref, state_ref, table_ref, out_ref, far_picked_ref, tiles_ref, picked_ref,
    win_ref, sem_ref, *, columns,
):
    half = table_ref.shape[2]
    blocks = state_ref.shape[1] // LANES
    first = pltpu.make_async_copy(
        table_ref, out_ref.at[:, :, pl.ds(0, half)], sem_ref.at[0]
    )
    wins = pltpu.make_async_copy(far_win_ref, win_ref, sem_ref.at[3])
    wins.start()
    first.start()
    resid, prob = residuals(state_ref[:K], state_ref[K : K + 1])
    cols = cols_ref[...].astype(f32)
    feat = lax.broadcasted_iota(i32, (cols.shape[0], K), 0)
    wins.wait()
    for step in range(ITERS):
        owner = win_ref[step : step + 1] // columns
        place = jnp.where(feat == owner, 1.0, 0.0).astype(bf16)
        for j in range(blocks):
            piece = cols[:, step * blocks + j, :].astype(bf16)
            picked = lax.dot_general(
                place, piece, (((0,), (0,)), ((), ())), preferred_element_type=f32
            )
            picked_ref[step, :, j * LANES : (j + 1) * LANES] = picked.astype(bf16)
    third = pltpu.make_async_copy(picked_ref, far_picked_ref, sem_ref.at[2])
    third.start()
    tile = sums_tile(resid, prob, picked_ref[0].astype(f32))
    second = send_tile(tile, tiles_ref, out_ref, sem_ref.at[1])
    wait_all([first, second, third])


def second_table_body(
    shared_ref, state_ref, far_state_ref, far_picked_ref, far_picked_taken_ref, geno_ref,
    far_taken_ref, out_ref, far_coef_ref, taken_ref, table_ref, tiles_ref, state_taken_ref,
    picked_ref, picked_taken_ref, coef_ref, sem_ref, load_ref,
):
    half = table_ref.shape[2]
    loads = load(
        [
            (far_picked_ref, picked_ref),
            (far_state_ref, state_taken_ref),
            (far_picked_taken_ref, picked_taken_ref),
        ],
        load_ref,
    )
    taken = load_half(far_taken_ref, taken_ref, sem_ref.at[4])
    coef = coefficients(shared_ref[:, :, half:])
    coef_ref[...] = coef
    coef_copy = pltpu.make_async_copy(coef_ref, far_coef_ref, sem_ref.at[1])
    coef_copy.start()
    coef = lane_tile(coef, state_ref.shape[1] // LANES)
    loads[0].wait()
    logits = state_ref[:K] + coef * picked_ref[0].astype(f32)
    resid, prob = residuals(logits, state_ref[K : K + 1])
    tile = sums_tile(resid, prob, picked_ref[1].astype(f32))
    sums_copy = send_tile(tile, tiles_ref, out_ref, sem_ref.at[0])
    wait_all(loads[1:])
    logits_taken = state_taken_ref[:K] + coef * picked_taken_ref[0].astype(f32)
    resid_taken, _ = residuals(logits_taken, state_taken_ref[K : K + 1])
    taken.wait()
    table_copies = send_table(
        resid, resid_taken, geno_ref, taken_ref, table_ref, out_ref, sem_ref.at[pl.ds(2, 2)]
    )
    wait_all([coef_copy, sums_copy] + table_copies)


def third_table_body(
    shared_ref, far_coef_ref, state_ref, far_state_ref, far_picked_ref, far_picked_taken_ref,
    geno_ref, far_taken_ref, out_ref, logits_ref, taken_ref, table_ref, new_ref,
    state_taken_ref, picked_ref, picked_taken_ref, coef_ref, sem_ref, load_ref,
):
    half = table_ref.shape[2]
    loads = load(
        [
            (far_coef_ref, coef_ref),
            (far_picked_ref, picked_ref),
            (far_state_ref, state_taken_ref),
            (far_picked_taken_ref, picked_taken_ref),
        ],
        load_ref,
    )
    taken = load_half(far_taken_ref, taken_ref, sem_ref.at[4])
    blocks = state_ref.shape[1] // LANES
    now = coefficients(shared_ref[:, :, half:])
    loads[0].wait()
    coefs = [lane_tile(coef, blocks) for coef in (coef_ref[...], now)]

    def updated(start, columns_ref):
        for step in range(ITERS):
            start = start + coefs[step] * columns_ref[step].astype(f32)
        return start

    loads[1].wait()
    logits = updated(state_ref[:K], picked_ref)
    new_ref[...] = logits
    logits_copy = pltpu.make_async_copy(new_ref, logits_ref, sem_ref.at[0])
    logits_copy.start()
    resid, _ = residuals(logits, state_ref[K : K + 1])
    wait_all(loads[2:])
    resid_taken, _ = residuals(
        updated(state_taken_ref[:K], picked_taken_ref), state_taken_ref[K : K + 1]
    )
    taken.wait()
    table_copies = send_table(
        resid, resid_taken, geno_ref, taken_ref, table_ref, out_ref, sem_ref.at[pl.ds(2, 2)]
    )
    wait_all([logits_copy] + table_copies)


def shards(genotypes, labels, base_margin, winners):
    samples, columns = genotypes.shape
    feat_count = lax.axis_size("feat")
    rows_count = lax.axis_size("rows")
    class_share = K // rows_count
    half = columns // 2
    partners = [(i, i ^ 1) for i in range(rows_count)]
    work = 2 * K * 2 * samples * half
    payload_shape = (rows_count, class_share, half + 2 * K)
    table_shape = (rows_count, class_share, half)
    tiles = pltpu.VMEM((rows_count, 8, 2 * K), bf16)
    sems = pltpu.SemaphoreType.DMA
    got_half = pltpu.VMEM((samples, half), bf16)
    loaded = [
        pltpu.VMEM((K + 8, samples), f32),
        pltpu.VMEM((ITERS, K, samples), bf16),
        pltpu.VMEM((ITERS, K, samples), bf16),
        pltpu.VMEM((K, LANES), f32),
    ]

    sent, state = call(
        pick_body,
        (
            pltpu.VMEM((feat_count, ITERS * samples // LANES, LANES), bf16),
            pltpu.VMEM((K + 8, samples), f32),
        ),
        [VMEM, HBM, HBM, VMEM],
        [
            pltpu.VMEM((ITERS, samples, LANES), bf16),
            sems((ITERS + 1,)),
        ],
        moved=samples * LANES * 4,
    )(winners, far(genotypes), far(base_margin.T), labels[None, :])
    cols = lax.all_to_all(sent, "feat", 0, 0, tiled=True)

    taken = far(lax.ppermute(genotypes, "rows", partners))
    geno = near(genotypes)
    state_taken = far(lax.ppermute(state, "rows", partners))
    state = near(state)

    table = call(
        first_table_body,
        pltpu.VMEM(table_shape, bf16),
        [VMEM] * 3 + [HBM],
        [got_half, sems((1,))],
        flops=work,
        moved=4 * samples * half,
    )(state, state_taken, geno, taken)

    def first_sums(*refs):
        first_sums_body(*refs, columns=columns)

    payload, picked = call(
        first_sums,
        (pltpu.HBM(payload_shape, bf16), pltpu.HBM((ITERS, K, samples), bf16)),
        [VMEM, HBM, VMEM, VMEM],
        [tiles, pltpu.VMEM((ITERS, K, samples), bf16), pltpu.VMEM((ITERS, K), i32), sems((4,))],
        moved=4 * samples * half,
    )(near(cols), far(winners), state, table)
    shared0 = lax.all_to_all(payload, "rows", 0, 0, tiled=True)
    picked_taken = far(lax.ppermute(picked, "rows", partners))

    payload, coef = call(
        second_table_body,
        (pltpu.HBM(payload_shape, bf16), pltpu.HBM((K, LANES), f32)),
        [VMEM, VMEM] + [HBM] * 3 + [VMEM, HBM],
        [got_half, pltpu.VMEM(table_shape, bf16), tiles] + loaded + [sems((5,)), sems((3,))],
        flops=work,
        moved=4 * samples * half,
    )(near(shared0), state, state_taken, far(picked), picked_taken, geno, taken)
    shared1 = lax.all_to_all(payload, "rows", 0, 0, tiled=True)

    payload, logits = call(
        third_table_body,
        (pltpu.HBM(table_shape, bf16), pltpu.HBM((K, samples), f32)),
        [VMEM, HBM, VMEM] + [HBM] * 3 + [VMEM, HBM],
        [got_half, pltpu.VMEM(table_shape, bf16), pltpu.VMEM((K, samples), f32)]
        + loaded
        + [sems((5,)), sems((4,))],
        flops=work,
        moved=4 * samples * half,
    )(near(shared1), far(coef), state, state_taken, far(picked), picked_taken, geno, taken)
    shared2 = lax.all_to_all(payload, "rows", 0, 0, tiled=True)

    tables = []
    for shared in (shared0, shared1, shared2):
        parts = shared[:, :, :half].astype(f32).reshape(rows_count // 2, 2, class_share, half)
        total = jnp.sum(parts, axis=0)
        tables.append(jnp.concatenate([total[0], total[1]], axis=1))
    return (logits.T, jnp.stack(tables))


def solution(mesh):
    in_specs = (P("rows", "feat"), P("rows"), P("rows", None), P())
    out_specs = (P("rows", None), P(None, "rows", "feat"))
    return jax.shard_map(shards, mesh=mesh, in_specs=in_specs, out_specs=out_specs, check_vma=False)
```

```python
import jax
import jax.numpy as jnp
from jax import lax
from jax.experimental import pallas as pl
from jax.experimental.pallas import tpu as pltpu
from jax.sharding import PartitionSpec as P

K = 64
ITERS = 2
LANES = 128


shrink_rate = 0.5
ridge_term = 1.0

bf16 = jnp.bfloat16
f32 = jnp.float32
i32 = jnp.int32
BlockSpec = pl.BlockSpec
VMEM = pl.BlockSpec(memory_space=pltpu.VMEM)
HBM = pl.BlockSpec(memory_space=pltpu.HBM)


def call(body, out_shape, in_specs, scratch=(), flops=0, moved=0, room=8 << 20):
    out_specs = jax.tree.map(
        lambda out: BlockSpec(memory_space=out.memory_space), out_shape, is_leaf=is_out
    )
    return pl.pallas_call(
        body,
        out_shape=out_shape,
        in_specs=in_specs,
        out_specs=out_specs,
        scratch_shapes=list(scratch),
        cost_estimate=pl.CostEstimate(flops=flops, bytes_accessed=moved, transcendentals=0),
        compiler_params=pltpu.CompilerParams(vmem_limit_bytes=room),
    )


def is_out(value):
    return hasattr(value, "memory_space")


def far(values):
    return pltpu.with_memory_space_constraint(values, pltpu.HBM)


def load(pairs, sem_ref):
    copies = [
        pltpu.make_async_copy(source, target, sem_ref.at[i])
        for i, (source, target) in enumerate(pairs)
    ]
    for copy in copies:
        copy.start()
    return copies


def wait_all(copies):
    for copy in copies:
        copy.wait()


def near(values):
    return pltpu.with_memory_space_constraint(values, pltpu.VMEM)


def rounded(values):
    return values.astype(bf16).astype(f32)


def split3(values):
    high = rounded(values)
    rest = values - high
    middle = rounded(rest)
    return high, middle, rest - middle


def softmax_classes(values):
    top = jnp.max(values, axis=0, keepdims=True)
    expo = jnp.exp(values - top)
    return expo / jnp.sum(expo, axis=0, keepdims=True)


def residuals(logits, label_row):
    prob = softmax_classes(logits)
    classes = lax.broadcasted_iota(i32, logits.shape, 0).astype(f32)
    onehot = jnp.where(classes == label_row, 1.0, 0.0)
    return (onehot - prob).astype(bf16), prob


def pick_body(
    far_win_ref, geno_ref, margin_ref, far_labels_ref, out_ref, state_ref, block_ref, win_ref,
    labels_ref, sem_ref,
):
    samples, columns = geno_ref.shape
    wins = pltpu.make_async_copy(far_win_ref, win_ref, sem_ref.at[ITERS + 1])
    wins.start()
    marks = pltpu.make_async_copy(far_labels_ref, labels_ref, sem_ref.at[ITERS + 2])
    marks.start()
    margins = pltpu.make_async_copy(margin_ref, state_ref.at[pl.ds(0, K)], sem_ref.at[ITERS])
    margins.start()
    wins.wait()
    local = win_ref[...] - lax.axis_index("feat") * columns
    mine = jnp.where((local >= 0) & (local < columns), local, 0).astype(f32)
    copies, lanes = [], []
    for step in range(ITERS):
        col = jnp.sum(mine[step : step + 1]).astype(i32)
        start = pl.multiple_of((col // LANES) * LANES, LANES)
        copy = pltpu.make_async_copy(
            geno_ref.at[:, pl.ds(start, LANES)], block_ref.at[step], sem_ref.at[step]
        )
        copy.start()
        copies.append(copy)
        lanes.append(col - start)
    marks.wait()
    state_ref[K:] = jnp.broadcast_to(labels_ref[...].astype(f32), (8, samples))
    rows = lax.broadcasted_iota(i32, (8, LANES), 0)
    lane = lax.broadcasted_iota(i32, (8, LANES), 1)
    tile = jnp.zeros((8, LANES), f32)
    for step in range(ITERS):
        copies[step].wait()
        pick = jnp.where(lane == lanes[step], 1.0, 0.0).astype(bf16)
        x = lax.dot_general(
            pick, block_ref[step], (((1,), (1,)), ((), ())), preferred_element_type=f32
        )
        for j in range(samples // LANES):
            here = rows == step * (samples // LANES) + j
            tile = tile + jnp.where(here, x[:, j * LANES : (j + 1) * LANES], 0.0)
    out_ref[...] = jnp.broadcast_to(tile.astype(bf16)[None], out_ref.shape)
    margins.wait()


def half_start(geno_ref):
    half = geno_ref.shape[1] // 2
    return pl.multiple_of(lax.rem(lax.axis_index("rows"), 2) * half, LANES)


def half_table(resid, resid_taken, geno_ref, taken_ref, start, width):
    own_span = pl.ds(pl.multiple_of(half_start(geno_ref) + start, LANES), width)
    first = jnp.dot(resid, geno_ref[:, own_span], preferred_element_type=f32)
    second = taken_ref[:, pl.ds(start, width)]
    return first + jnp.dot(resid_taken, second, preferred_element_type=f32)


def load_half(whole_ref, half_ref, sem_ref):
    start = half_start(whole_ref)
    copy = pltpu.make_async_copy(
        whole_ref.at[:, pl.ds(start, half_ref.shape[1])], half_ref, sem_ref
    )
    copy.start()
    return copy


def sums_tile(resid, prob, picked):
    grad = resid.astype(f32) * picked
    curv = prob * (1.0 - prob) * picked * picked
    both = 0.5 * jnp.concatenate([grad, curv], axis=0)
    folded = both[:, :LANES]
    for j in range(1, both.shape[1] // LANES):
        folded = folded + both[:, j * LANES : (j + 1) * LANES]
    ones = jnp.ones((8, LANES), bf16)
    total = jnp.zeros((8, 2 * K), f32)
    for term in split3(folded):
        total = total + lax.dot_general(
            ones, term.astype(bf16), (((1,), (1,)), ((), ())), preferred_element_type=f32
        )
    high, middle, low = split3(total)
    row = lax.broadcasted_iota(i32, total.shape, 0)
    tile = jnp.where(row == 0, high, jnp.where(row == 1, middle, jnp.where(row == 2, low, 0.0)))
    return tile.astype(bf16)


def coefficients(tiles):
    tiles = tiles.astype(f32)
    row = jnp.sum(jnp.sum(tiles, axis=0), axis=0, keepdims=True)
    column = jnp.transpose(jnp.broadcast_to(row, (2 * K, LANES)))
    return shrink_rate * (2.0 * column[:K]) / (2.0 * column[K:] + ridge_term)


def lane_tile(values, count):
    return jnp.concatenate([values] * count, axis=1)


def send_tile(tile, both_ref, out_ref, sem_ref):
    half = out_ref.shape[2] - 2 * K
    both_ref[...] = jnp.broadcast_to(tile[None], both_ref.shape)
    copy = pltpu.make_async_copy(both_ref, out_ref.at[:, :, pl.ds(half, 2 * K)], sem_ref)
    copy.start()
    return copy


def send_table(resid, resid_taken, geno_ref, taken_ref, table_ref, out_ref, sem_ref, pieces=2):
    width = table_ref.shape[2] // pieces
    copies = []
    for piece in range(pieces):
        span = pl.ds(piece * width, width)
        table = half_table(
            resid, resid_taken, geno_ref, taken_ref, piece * width, width
        )
        table_ref[:, :, span] = table.reshape(table_ref.shape[0], -1, width).astype(bf16)
        copy = pltpu.make_async_copy(
            table_ref.at[:, :, span], out_ref.at[:, :, span], sem_ref.at[piece]
        )
        copy.start()
        copies.append(copy)
    return copies


def first_table_body(
    state_ref, state_taken_ref, geno_ref, far_taken_ref, out_ref, taken_ref, sem_ref
):
    taken = load_half(far_taken_ref, taken_ref, sem_ref.at[0])
    resid, _ = residuals(state_ref[:K], state_ref[K : K + 1])
    resid_taken, _ = residuals(state_taken_ref[:K], state_taken_ref[K : K + 1])
    taken.wait()
    table = half_table(resid, resid_taken, geno_ref, taken_ref, 0, out_ref.shape[2])
    out_ref[...] = table.reshape(out_ref.shape).astype(bf16)


def first_sums_body(
    cols_ref, far_win_ref, state_ref, table_ref, out_ref, far_picked_ref, tiles_ref, picked_ref,
    win_ref, sem_ref, *, columns,
):
    half = table_ref.shape[2]
    blocks = state_ref.shape[1] // LANES
    first = pltpu.make_async_copy(
        table_ref, out_ref.at[:, :, pl.ds(0, half)], sem_ref.at[0]
    )
    wins = pltpu.make_async_copy(far_win_ref, win_ref, sem_ref.at[3])
    wins.start()
    first.start()
    resid, prob = residuals(state_ref[:K], state_ref[K : K + 1])
    cols = cols_ref[...].astype(f32)
    feat = lax.broadcasted_iota(i32, (cols.shape[0], K), 0)
    wins.wait()
    for step in range(ITERS):
        owner = win_ref[step : step + 1] // columns
        place = jnp.where(feat == owner, 1.0, 0.0).astype(bf16)
        for j in range(blocks):
            piece = cols[:, step * blocks + j, :].astype(bf16)
            picked = lax.dot_general(
                place, piece, (((0,), (0,)), ((), ())), preferred_element_type=f32
            )
            picked_ref[step, :, j * LANES : (j + 1) * LANES] = picked.astype(bf16)
    third = pltpu.make_async_copy(picked_ref, far_picked_ref, sem_ref.at[2])
    third.start()
    tile = sums_tile(resid, prob, picked_ref[0].astype(f32))
    second = send_tile(tile, tiles_ref, out_ref, sem_ref.at[1])
    wait_all([first, second, third])


def second_table_body(
    shared_ref, state_ref, far_state_ref, far_picked_ref, far_picked_taken_ref, geno_ref,
    taken_ref, out_ref, far_coef_ref, table_ref, tiles_ref, state_taken_ref,
    picked_ref, picked_taken_ref, coef_ref, sem_ref, load_ref,
):
    half = table_ref.shape[2]
    loads = load(
        [
            (far_picked_ref, picked_ref),
            (far_state_ref, state_taken_ref),
            (far_picked_taken_ref, picked_taken_ref),
        ],
        load_ref,
    )
    coef = coefficients(shared_ref[:, :, half:])
    coef_ref[...] = coef
    coef_copy = pltpu.make_async_copy(coef_ref, far_coef_ref, sem_ref.at[1])
    coef_copy.start()
    coef = lane_tile(coef, state_ref.shape[1] // LANES)
    wait_all(loads)
    logits = state_ref[:K] + coef * picked_ref[0].astype(f32)
    resid, prob = residuals(logits, state_ref[K : K + 1])
    tile = sums_tile(resid, prob, picked_ref[1].astype(f32))
    sums_copy = send_tile(tile, tiles_ref, out_ref, sem_ref.at[0])
    logits_taken = state_taken_ref[:K] + coef * picked_taken_ref[0].astype(f32)
    resid_taken, _ = residuals(logits_taken, state_taken_ref[K : K + 1])
    table_copies = send_table(
        resid, resid_taken, geno_ref, taken_ref, table_ref, out_ref, sem_ref.at[pl.ds(2, 2)]
    )
    wait_all([coef_copy, sums_copy] + table_copies)


def third_table_body(
    shared_ref, far_coef_ref, state_ref, far_state_ref, far_picked_ref, far_picked_taken_ref,
    geno_ref, taken_ref, out_ref, logits_ref, table_ref, new_ref,
    state_taken_ref, picked_ref, picked_taken_ref, coef_ref, sem_ref, load_ref,
):
    half = table_ref.shape[2]
    loads = load(
        [
            (far_coef_ref, coef_ref),
            (far_picked_ref, picked_ref),
            (far_state_ref, state_taken_ref),
            (far_picked_taken_ref, picked_taken_ref),
        ],
        load_ref,
    )
    blocks = state_ref.shape[1] // LANES
    now = coefficients(shared_ref[:, :, half:])
    wait_all(loads)
    coefs = [lane_tile(coef, blocks) for coef in (coef_ref[...], now)]

    def updated(start, columns_ref):
        for step in range(ITERS):
            start = start + coefs[step] * columns_ref[step].astype(f32)
        return start

    logits = updated(state_ref[:K], picked_ref)
    new_ref[...] = logits
    logits_copy = pltpu.make_async_copy(new_ref, logits_ref, sem_ref.at[0])
    logits_copy.start()
    resid, _ = residuals(logits, state_ref[K : K + 1])
    resid_taken, _ = residuals(
        updated(state_taken_ref[:K], picked_taken_ref), state_taken_ref[K : K + 1]
    )
    table_copies = send_table(
        resid, resid_taken, geno_ref, taken_ref, table_ref, out_ref, sem_ref.at[pl.ds(2, 2)]
    )
    wait_all([logits_copy] + table_copies)


def shards(genotypes, labels, base_margin, winners):
    samples, columns = genotypes.shape
    feat_count = lax.axis_size("feat")
    rows_count = lax.axis_size("rows")
    class_share = K // rows_count
    half = columns // 2
    partners = [(i, i ^ 1) for i in range(rows_count)]
    work = 2 * K * 2 * samples * half
    payload_shape = (rows_count, class_share, half + 2 * K)
    table_shape = (rows_count, class_share, half)
    tiles = pltpu.VMEM((rows_count, 8, 2 * K), bf16)
    sems = pltpu.SemaphoreType.DMA
    loaded = [
        pltpu.VMEM((K + 8, samples), f32),
        pltpu.VMEM((ITERS, K, samples), bf16),
        pltpu.VMEM((ITERS, K, samples), bf16),
        pltpu.VMEM((K, LANES), f32),
    ]

    sent, state = call(
        pick_body,
        (
            pltpu.VMEM((feat_count, ITERS * samples // LANES, LANES), bf16),
            pltpu.VMEM((K + 8, samples), f32),
        ),
        [HBM] * 4,
        [
            pltpu.VMEM((ITERS, samples, LANES), bf16),
            pltpu.VMEM((ITERS, K), i32),
            pltpu.VMEM((1, samples), i32),
            sems((ITERS + 3,)),
        ],
        moved=samples * LANES * 4,
    )(far(winners), far(genotypes), far(base_margin.T), far(labels[None, :]))
    cols = lax.all_to_all(sent, "feat", 0, 0, tiled=True)

    taken = far(lax.ppermute(genotypes, "rows", partners))
    geno = near(genotypes)
    state_taken = far(lax.ppermute(state, "rows", partners))
    state = near(state)

    table, taken = call(
        first_table_body,
        (pltpu.VMEM(table_shape, bf16), pltpu.VMEM((samples, half), bf16)),
        [VMEM] * 3 + [HBM],
        [sems((1,))],
        flops=work,
        moved=4 * samples * half,
    )(state, state_taken, geno, taken)

    def first_sums(*refs):
        first_sums_body(*refs, columns=columns)

    payload, picked = call(
        first_sums,
        (pltpu.HBM(payload_shape, bf16), pltpu.HBM((ITERS, K, samples), bf16)),
        [VMEM, HBM, VMEM, VMEM],
        [tiles, pltpu.VMEM((ITERS, K, samples), bf16), pltpu.VMEM((ITERS, K), i32), sems((4,))],
        moved=4 * samples * half,
    )(near(cols), far(winners), state, table)
    shared0 = lax.all_to_all(payload, "rows", 0, 0, tiled=True)
    picked_taken = far(lax.ppermute(picked, "rows", partners))

    payload, coef = call(
        second_table_body,
        (pltpu.HBM(payload_shape, bf16), pltpu.HBM((K, LANES), f32)),
        [VMEM, VMEM] + [HBM] * 3 + [VMEM] * 2,
        [pltpu.VMEM(table_shape, bf16), tiles] + loaded + [sems((5,)), sems((3,))],
        flops=work,
        moved=4 * samples * half,
    )(near(shared0), state, state_taken, far(picked), picked_taken, geno, taken)
    shared1 = lax.all_to_all(payload, "rows", 0, 0, tiled=True)

    payload, logits = call(
        third_table_body,
        (pltpu.HBM(table_shape, bf16), pltpu.HBM((K, samples), f32)),
        [VMEM, HBM, VMEM] + [HBM] * 3 + [VMEM] * 2,
        [pltpu.VMEM(table_shape, bf16), pltpu.VMEM((K, samples), f32)]
        + loaded
        + [sems((5,)), sems((4,))],
        flops=work,
        moved=4 * samples * half,
    )(near(shared1), far(coef), state, state_taken, far(picked), picked_taken, geno, taken)
    shared2 = lax.all_to_all(payload, "rows", 0, 0, tiled=True)

    tables = []
    for shared in (shared0, shared1, shared2):
        parts = shared[:, :, :half].astype(f32).reshape(rows_count // 2, 2, class_share, half)
        total = jnp.sum(parts, axis=0)
        tables.append(jnp.concatenate([total[0], total[1]], axis=1))
    return (logits.T, jnp.stack(tables))


def solution(mesh):
    in_specs = (P("rows", "feat"), P("rows"), P("rows", None), P())
    out_specs = (P("rows", None), P(None, "rows", "feat"))
    return jax.shard_map(shards, mesh=mesh, in_specs=in_specs, out_specs=out_specs, check_vma=False)
```

```python
import jax
import jax.numpy as jnp
from jax import lax
from jax.experimental import pallas as pl
from jax.experimental.pallas import tpu as pltpu
from jax.sharding import PartitionSpec as P

K = 64
ITERS = 2
LANES = 128


shrink_rate = 0.5
ridge_term = 1.0

bf16 = jnp.bfloat16
f32 = jnp.float32
i32 = jnp.int32
BlockSpec = pl.BlockSpec
VMEM = pl.BlockSpec(memory_space=pltpu.VMEM)
HBM = pl.BlockSpec(memory_space=pltpu.HBM)


def call(body, out_shape, in_specs, scratch=(), flops=0, moved=0, room=8 << 20):
    out_specs = jax.tree.map(
        lambda out: BlockSpec(memory_space=out.memory_space), out_shape, is_leaf=is_out
    )
    return pl.pallas_call(
        body,
        out_shape=out_shape,
        in_specs=in_specs,
        out_specs=out_specs,
        scratch_shapes=list(scratch),
        cost_estimate=pl.CostEstimate(flops=flops, bytes_accessed=moved, transcendentals=0),
        compiler_params=pltpu.CompilerParams(vmem_limit_bytes=room),
    )


def is_out(value):
    return hasattr(value, "memory_space")


def far(values):
    return pltpu.with_memory_space_constraint(values, pltpu.HBM)


def wait_all(copies):
    for copy in copies:
        copy.wait()


def near(values):
    return pltpu.with_memory_space_constraint(values, pltpu.VMEM)


def rounded(values):
    return values.astype(bf16).astype(f32)


def split3(values):
    high = rounded(values)
    rest = values - high
    middle = rounded(rest)
    return high, middle, rest - middle


def softmax_classes(values):
    top = jnp.max(values, axis=0, keepdims=True)
    expo = jnp.exp(values - top)
    return expo / jnp.sum(expo, axis=0, keepdims=True)


def residuals(logits, label_row):
    prob = softmax_classes(logits)
    classes = lax.broadcasted_iota(i32, logits.shape, 0).astype(f32)
    onehot = jnp.where(classes == label_row, 1.0, 0.0)
    return (onehot - prob).astype(bf16), prob


def pick_body(
    far_win_ref, geno_ref, margin_ref, far_labels_ref, out_ref, state_ref, block_ref, win_ref,
    labels_ref, sem_ref,
):
    samples, columns = geno_ref.shape
    wins = pltpu.make_async_copy(far_win_ref, win_ref, sem_ref.at[ITERS + 1])
    wins.start()
    marks = pltpu.make_async_copy(far_labels_ref, labels_ref, sem_ref.at[ITERS + 2])
    marks.start()
    margins = pltpu.make_async_copy(margin_ref, state_ref.at[pl.ds(0, K)], sem_ref.at[ITERS])
    margins.start()
    wins.wait()
    local = win_ref[...] - lax.axis_index("feat") * columns
    mine = jnp.where((local >= 0) & (local < columns), local, 0).astype(f32)
    copies, lanes = [], []
    for step in range(ITERS):
        col = jnp.sum(mine[step : step + 1]).astype(i32)
        start = pl.multiple_of((col // LANES) * LANES, LANES)
        copy = pltpu.make_async_copy(
            geno_ref.at[:, pl.ds(start, LANES)], block_ref.at[step], sem_ref.at[step]
        )
        copy.start()
        copies.append(copy)
        lanes.append(col - start)
    marks.wait()
    state_ref[K:] = jnp.broadcast_to(labels_ref[...].astype(f32), (8, samples))
    rows = lax.broadcasted_iota(i32, (8, LANES), 0)
    lane = lax.broadcasted_iota(i32, (8, LANES), 1)
    tile = jnp.zeros((8, LANES), f32)
    for step in range(ITERS):
        copies[step].wait()
        pick = jnp.where(lane == lanes[step], 1.0, 0.0).astype(bf16)
        x = lax.dot_general(
            pick, block_ref[step], (((1,), (1,)), ((), ())), preferred_element_type=f32
        )
        for j in range(samples // LANES):
            here = rows == step * (samples // LANES) + j
            tile = tile + jnp.where(here, x[:, j * LANES : (j + 1) * LANES], 0.0)
    out_ref[...] = jnp.broadcast_to(tile.astype(bf16)[None], out_ref.shape)
    margins.wait()


def load_halves(geno_ref, far_taken_ref, both_ref, sem_ref):
    samples = geno_ref.shape[0]
    half = both_ref.shape[1]
    start = pl.multiple_of(lax.rem(lax.axis_index("rows"), 2) * half, LANES)
    copies = [
        pltpu.make_async_copy(
            whole_ref.at[:, pl.ds(start, half)],
            both_ref.at[pl.ds(place * samples, samples)],
            sem_ref.at[place],
        )
        for place, whole_ref in enumerate((geno_ref, far_taken_ref))
    ]
    for copy in copies:
        copy.start()
    return copies


def half_table(resid, resid_taken, both_ref, start, width):
    whole = jnp.concatenate([resid, resid_taken], axis=1)
    return jnp.dot(whole, both_ref[:, pl.ds(start, width)], preferred_element_type=f32)


def sums_tile(resid, prob, picked):
    grad = resid.astype(f32) * picked
    curv = prob * (1.0 - prob) * picked * picked
    both = 0.5 * jnp.concatenate([grad, curv], axis=0)
    folded = both[:, :LANES]
    for j in range(1, both.shape[1] // LANES):
        folded = folded + both[:, j * LANES : (j + 1) * LANES]
    ones = jnp.ones((8, LANES), bf16)
    total = jnp.zeros((8, 2 * K), f32)
    for term in split3(folded):
        total = total + lax.dot_general(
            ones, term.astype(bf16), (((1,), (1,)), ((), ())), preferred_element_type=f32
        )
    high, middle, low = split3(total)
    row = lax.broadcasted_iota(i32, total.shape, 0)
    tile = jnp.where(row == 0, high, jnp.where(row == 1, middle, jnp.where(row == 2, low, 0.0)))
    return tile.astype(bf16)


def coefficients(tiles):
    tiles = tiles.astype(f32)
    row = jnp.sum(jnp.sum(tiles, axis=0), axis=0, keepdims=True)
    column = jnp.transpose(jnp.broadcast_to(row, (2 * K, LANES)))
    return shrink_rate * (2.0 * column[:K]) / (2.0 * column[K:] + ridge_term)


def lane_tile(values, count):
    return jnp.concatenate([values] * count, axis=1)


def send_tile(tile, both_ref, out_ref, sem_ref):
    half = out_ref.shape[2] - 2 * K
    both_ref[...] = jnp.broadcast_to(tile[None], both_ref.shape)
    copy = pltpu.make_async_copy(both_ref, out_ref.at[:, :, pl.ds(half, 2 * K)], sem_ref)
    copy.start()
    return copy


def send_table(resid, resid_taken, both_ref, table_ref, out_ref, sem_ref, pieces=2):
    width = table_ref.shape[2] // pieces
    copies = []
    for piece in range(pieces):
        span = pl.ds(piece * width, width)
        table = half_table(resid, resid_taken, both_ref, piece * width, width)
        table_ref[:, :, span] = table.reshape(table_ref.shape[0], -1, width).astype(bf16)
        copy = pltpu.make_async_copy(
            table_ref.at[:, :, span], out_ref.at[:, :, span], sem_ref.at[piece]
        )
        copy.start()
        copies.append(copy)
    return copies


def first_table_body(
    state_ref, state_taken_ref, geno_ref, far_taken_ref, out_ref, both_ref, sem_ref
):
    copies = load_halves(geno_ref, far_taken_ref, both_ref, sem_ref)
    resid, _ = residuals(state_ref[:K], state_ref[K : K + 1])
    resid_taken, _ = residuals(state_taken_ref[:K], state_taken_ref[K : K + 1])
    wait_all(copies)
    table = half_table(resid, resid_taken, both_ref, 0, out_ref.shape[2])
    out_ref[...] = table.reshape(out_ref.shape).astype(bf16)


def first_sums_body(
    cols_ref, far_win_ref, state_ref, table_ref, out_ref, picked_ref, far_picked_ref, tiles_ref,
    win_ref, sem_ref, *, columns,
):
    half = table_ref.shape[2]
    blocks = state_ref.shape[1] // LANES
    first = pltpu.make_async_copy(
        table_ref, out_ref.at[:, :, pl.ds(0, half)], sem_ref.at[0]
    )
    wins = pltpu.make_async_copy(far_win_ref, win_ref, sem_ref.at[2])
    wins.start()
    first.start()
    resid, prob = residuals(state_ref[:K], state_ref[K : K + 1])
    cols = cols_ref[...].astype(f32)
    feat = lax.broadcasted_iota(i32, (cols.shape[0], K), 0)
    wins.wait()
    for step in range(ITERS):
        owner = win_ref[step : step + 1] // columns
        place = jnp.where(feat == owner, 1.0, 0.0).astype(bf16)
        for j in range(blocks):
            piece = cols[:, step * blocks + j, :].astype(bf16)
            picked = lax.dot_general(
                place, piece, (((0,), (0,)), ((), ())), preferred_element_type=f32
            )
            picked_ref[step, :, j * LANES : (j + 1) * LANES] = picked.astype(bf16)
    third = pltpu.make_async_copy(picked_ref, far_picked_ref, sem_ref.at[3])
    third.start()
    tile = sums_tile(resid, prob, picked_ref[0].astype(f32))
    second = send_tile(tile, tiles_ref, out_ref, sem_ref.at[1])
    wait_all([first, second, third])


def second_table_body(
    shared_ref, state_ref, state_taken_ref, picked_ref, picked_taken_ref, both_ref,
    out_ref, coef_ref, table_ref, tiles_ref, sem_ref,
):
    half = table_ref.shape[2]
    coef = coefficients(shared_ref[:, :, half:])
    coef_ref[...] = coef
    coef = lane_tile(coef, state_ref.shape[1] // LANES)
    logits = state_ref[:K] + coef * picked_ref[0].astype(f32)
    resid, prob = residuals(logits, state_ref[K : K + 1])
    tile = sums_tile(resid, prob, picked_ref[1].astype(f32))
    sums_copy = send_tile(tile, tiles_ref, out_ref, sem_ref.at[0])
    logits_taken = state_taken_ref[:K] + coef * picked_taken_ref[0].astype(f32)
    resid_taken, _ = residuals(logits_taken, state_taken_ref[K : K + 1])
    table_copies = send_table(
        resid, resid_taken, both_ref, table_ref, out_ref, sem_ref.at[pl.ds(2, 2)]
    )
    wait_all([sums_copy] + table_copies)


def third_table_body(
    shared_ref, coef_ref, state_ref, state_taken_ref, picked_ref, picked_taken_ref, both_ref,
    out_ref, logits_ref, table_ref, new_ref, sem_ref,
):
    half = table_ref.shape[2]
    blocks = state_ref.shape[1] // LANES
    now = coefficients(shared_ref[:, :, half:])
    coefs = [lane_tile(coef, blocks) for coef in (coef_ref[...], now)]

    def updated(start, columns_ref):
        for step in range(ITERS):
            start = start + coefs[step] * columns_ref[step].astype(f32)
        return start

    logits = updated(state_ref[:K], picked_ref)
    new_ref[...] = logits
    logits_copy = pltpu.make_async_copy(new_ref, logits_ref, sem_ref.at[0])
    logits_copy.start()
    resid, _ = residuals(logits, state_ref[K : K + 1])
    resid_taken, _ = residuals(
        updated(state_taken_ref[:K], picked_taken_ref), state_taken_ref[K : K + 1]
    )
    table_copies = send_table(
        resid, resid_taken, both_ref, table_ref, out_ref, sem_ref.at[pl.ds(2, 2)]
    )
    wait_all([logits_copy] + table_copies)


def shards(genotypes, labels, base_margin, winners):
    samples, columns = genotypes.shape
    feat_count = lax.axis_size("feat")
    rows_count = lax.axis_size("rows")
    class_share = K // rows_count
    half = columns // 2
    partners = [(i, i ^ 1) for i in range(rows_count)]
    work = 2 * K * 2 * samples * half
    payload_shape = (rows_count, class_share, half + 2 * K)
    table_shape = (rows_count, class_share, half)
    tiles = pltpu.VMEM((rows_count, 8, 2 * K), bf16)
    sems = pltpu.SemaphoreType.DMA

    sent, state = call(
        pick_body,
        (
            pltpu.VMEM((feat_count, ITERS * samples // LANES, LANES), bf16),
            pltpu.VMEM((K + 8, samples), f32),
        ),
        [HBM] * 4,
        [
            pltpu.VMEM((ITERS, samples, LANES), bf16),
            pltpu.VMEM((ITERS, K), i32),
            pltpu.VMEM((1, samples), i32),
            sems((ITERS + 3,)),
        ],
        moved=samples * LANES * 4,
    )(far(winners), far(genotypes), far(base_margin.T), far(labels[None, :]))
    cols = lax.all_to_all(sent, "feat", 0, 0, tiled=True)

    taken = far(lax.ppermute(genotypes, "rows", partners))
    geno = far(genotypes)
    state_taken = near(lax.ppermute(state, "rows", partners))
    state = near(state)

    table, both = call(
        first_table_body,
        (pltpu.VMEM(table_shape, bf16), pltpu.VMEM((2 * samples, half), bf16)),
        [VMEM, VMEM, HBM, HBM],
        [sems((2,))],
        flops=work,
        moved=4 * samples * half,
    )(state, state_taken, geno, taken)

    def first_sums(*refs):
        first_sums_body(*refs, columns=columns)

    picked_shape = (ITERS, K, samples)
    payload, picked, far_picked = call(
        first_sums,
        (
            pltpu.HBM(payload_shape, bf16),
            pltpu.VMEM(picked_shape, bf16),
            pltpu.HBM(picked_shape, bf16),
        ),
        [VMEM, HBM, VMEM, VMEM],
        [tiles, pltpu.VMEM((ITERS, K), i32), sems((4,))],
        moved=4 * samples * half,
    )(near(cols), far(winners), state, table)
    shared0 = lax.all_to_all(payload, "rows", 0, 0, tiled=True)
    picked_taken = near(lax.ppermute(far_picked, "rows", partners))

    payload, coef = call(
        second_table_body,
        (pltpu.HBM(payload_shape, bf16), pltpu.VMEM((K, LANES), f32)),
        [VMEM] * 6,
        [pltpu.VMEM(table_shape, bf16), tiles, sems((4,))],
        flops=work,
        moved=4 * samples * half,
    )(near(shared0), state, state_taken, near(picked), picked_taken, both)
    shared1 = lax.all_to_all(payload, "rows", 0, 0, tiled=True)

    payload, logits = call(
        third_table_body,
        (pltpu.HBM(table_shape, bf16), pltpu.HBM((K, samples), f32)),
        [VMEM] * 7,
        [pltpu.VMEM(table_shape, bf16), pltpu.VMEM((K, samples), f32), sems((4,))],
        flops=work,
        moved=4 * samples * half,
    )(near(shared1), near(coef), state, state_taken, near(picked), picked_taken, both)
    shared2 = lax.all_to_all(payload, "rows", 0, 0, tiled=True)

    tables = []
    for shared in (shared0, shared1, shared2):
        parts = shared[:, :, :half].astype(f32).reshape(rows_count // 2, 2, class_share, half)
        total = jnp.sum(parts, axis=0)
        tables.append(jnp.concatenate([total[0], total[1]], axis=1))
    return (logits.T, jnp.stack(tables))


def solution(mesh):
    in_specs = (P("rows", "feat"), P("rows"), P("rows", None), P())
    out_specs = (P("rows", None), P(None, "rows", "feat"))
    return jax.shard_map(shards, mesh=mesh, in_specs=in_specs, out_specs=out_specs, check_vma=False)
```

```python
import jax
import jax.numpy as jnp
from jax import lax
from jax.experimental import pallas as pl
from jax.experimental.pallas import tpu as pltpu
from jax.sharding import PartitionSpec as P

K = 64
ITERS = 2
LANES = 128


shrink_rate = 0.5
ridge_term = 1.0

bf16 = jnp.bfloat16
f32 = jnp.float32
i32 = jnp.int32
BlockSpec = pl.BlockSpec
VMEM = pl.BlockSpec(memory_space=pltpu.VMEM)
HBM = pl.BlockSpec(memory_space=pltpu.HBM)


def call(body, out_shape, in_specs, scratch=(), flops=0, moved=0, room=8 << 20):
    out_specs = jax.tree.map(
        lambda out: BlockSpec(memory_space=out.memory_space), out_shape, is_leaf=is_out
    )
    return pl.pallas_call(
        body,
        out_shape=out_shape,
        in_specs=in_specs,
        out_specs=out_specs,
        scratch_shapes=list(scratch),
        cost_estimate=pl.CostEstimate(flops=flops, bytes_accessed=moved, transcendentals=0),
        compiler_params=pltpu.CompilerParams(vmem_limit_bytes=room),
    )


def is_out(value):
    return hasattr(value, "memory_space")


def far(values):
    return pltpu.with_memory_space_constraint(values, pltpu.HBM)


def wait_all(copies):
    for copy in copies:
        copy.wait()


def near(values):
    return pltpu.with_memory_space_constraint(values, pltpu.VMEM)


def rounded(values):
    return values.astype(bf16).astype(f32)


def split3(values):
    high = rounded(values)
    rest = values - high
    middle = rounded(rest)
    return high, middle, rest - middle


def softmax_classes(values):
    top = jnp.max(values, axis=0, keepdims=True)
    expo = jnp.exp(values - top)
    return expo / jnp.sum(expo, axis=0, keepdims=True)


def residuals(logits, label_row):
    prob = softmax_classes(logits)
    classes = lax.broadcasted_iota(i32, logits.shape, 0).astype(f32)
    onehot = jnp.where(classes == label_row, 1.0, 0.0)
    return (onehot - prob).astype(bf16), prob


def pick_body(
    win_ref, geno_ref, margin_ref, far_labels_ref, out_ref, state_ref, block_ref, labels_ref,
    sem_ref,
):
    samples, columns = geno_ref.shape
    marks = pltpu.make_async_copy(far_labels_ref, labels_ref, sem_ref.at[1])
    marks.start()
    margins = pltpu.make_async_copy(margin_ref, state_ref.at[pl.ds(0, K)], sem_ref.at[0])
    margins.start()
    local = win_ref[...] - lax.axis_index("feat") * columns
    mine = jnp.where((local >= 0) & (local < columns), local, 0).astype(f32)
    copies, lanes = [], []
    for step in range(ITERS):
        col = jnp.sum(mine[step : step + 1]).astype(i32)
        start = pl.multiple_of((col // LANES) * LANES, LANES)
        copy = pltpu.make_async_copy(
            geno_ref.at[:, pl.ds(start, LANES)], block_ref.at[step], sem_ref.at[2 + step]
        )
        copy.start()
        copies.append(copy)
        lanes.append(col - start)
    marks.wait()
    state_ref[K:] = jnp.broadcast_to(labels_ref[...].astype(f32), (8, samples))
    rows = lax.broadcasted_iota(i32, (8, LANES), 0)
    lane = lax.broadcasted_iota(i32, (8, LANES), 1)
    tile = jnp.zeros((8, LANES), f32)
    for step in range(ITERS):
        copies[step].wait()
        pick = jnp.where(lane == lanes[step], 1.0, 0.0).astype(bf16)
        x = lax.dot_general(
            pick, block_ref[step], (((1,), (1,)), ((), ())), preferred_element_type=f32
        )
        for j in range(samples // LANES):
            here = rows == step * (samples // LANES) + j
            tile = tile + jnp.where(here, x[:, j * LANES : (j + 1) * LANES], 0.0)
    out_ref[...] = jnp.broadcast_to(tile.astype(bf16)[None], out_ref.shape)
    margins.wait()


def load_halves(geno_ref, far_taken_ref, both_ref, sem_ref):
    samples = geno_ref.shape[0]
    half = both_ref.shape[1]
    start = pl.multiple_of(lax.rem(lax.axis_index("rows"), 2) * half, LANES)
    copies = [
        pltpu.make_async_copy(
            whole_ref.at[:, pl.ds(start, half)],
            both_ref.at[pl.ds(place * samples, samples)],
            sem_ref.at[place],
        )
        for place, whole_ref in enumerate((geno_ref, far_taken_ref))
    ]
    for copy in copies:
        copy.start()
    return copies


def half_table(resid, resid_taken, both_ref, start, width):
    whole = jnp.concatenate([resid, resid_taken], axis=1)
    return jnp.dot(whole, both_ref[:, pl.ds(start, width)], preferred_element_type=f32)


def sums_tile(resid, prob, picked):
    grad = resid.astype(f32) * picked
    curv = prob * (1.0 - prob) * picked * picked
    both = 0.5 * jnp.concatenate([grad, curv], axis=0)
    folded = both[:, :LANES]
    for j in range(1, both.shape[1] // LANES):
        folded = folded + both[:, j * LANES : (j + 1) * LANES]
    ones = jnp.ones((8, LANES), bf16)
    total = jnp.zeros((8, 2 * K), f32)
    for term in split3(folded):
        total = total + lax.dot_general(
            ones, term.astype(bf16), (((1,), (1,)), ((), ())), preferred_element_type=f32
        )
    high, middle, low = split3(total)
    row = lax.broadcasted_iota(i32, total.shape, 0)
    tile = jnp.where(row == 0, high, jnp.where(row == 1, middle, jnp.where(row == 2, low, 0.0)))
    return tile.astype(bf16)


def coefficients(tiles):
    tiles = tiles.astype(f32)
    row = jnp.sum(jnp.sum(tiles, axis=0), axis=0, keepdims=True)
    column = jnp.transpose(jnp.broadcast_to(row, (2 * K, LANES)))
    return shrink_rate * (2.0 * column[:K]) / (2.0 * column[K:] + ridge_term)


def lane_tile(values, count):
    return jnp.concatenate([values] * count, axis=1)


def send_tile(tile, both_ref, out_ref, sem_ref):
    half = out_ref.shape[2] - 2 * K
    both_ref[...] = jnp.broadcast_to(tile[None], both_ref.shape)
    copy = pltpu.make_async_copy(both_ref, out_ref.at[:, :, pl.ds(half, 2 * K)], sem_ref)
    copy.start()
    return copy


def send_table(resid, resid_taken, both_ref, table_ref, out_ref, sem_ref, pieces=2):
    width = table_ref.shape[2] // pieces
    copies = []
    for piece in range(pieces):
        span = pl.ds(piece * width, width)
        table = half_table(resid, resid_taken, both_ref, piece * width, width)
        table_ref[:, :, span] = table.reshape(table_ref.shape[0], -1, width).astype(bf16)
        copy = pltpu.make_async_copy(
            table_ref.at[:, :, span], out_ref.at[:, :, span], sem_ref.at[piece]
        )
        copy.start()
        copies.append(copy)
    return copies


def first_table_body(
    state_ref, state_taken_ref, geno_ref, far_taken_ref, far_win_ref, out_ref, both_ref,
    place_ref, win_ref, sem_ref,
):
    wins = pltpu.make_async_copy(far_win_ref, win_ref, sem_ref.at[2])
    wins.start()
    copies = load_halves(geno_ref, far_taken_ref, both_ref, sem_ref)
    feat = lax.broadcasted_iota(i32, place_ref.shape[1:], 0)
    wins.wait()
    for step in range(ITERS):
        owner = win_ref[step : step + 1] // geno_ref.shape[1]
        place_ref[step] = jnp.where(feat == owner, 1.0, 0.0).astype(bf16)
    resid, _ = residuals(state_ref[:K], state_ref[K : K + 1])
    resid_taken, _ = residuals(state_taken_ref[:K], state_taken_ref[K : K + 1])
    wait_all(copies)
    table = half_table(resid, resid_taken, both_ref, 0, out_ref.shape[2])
    out_ref[...] = table.reshape(out_ref.shape).astype(bf16)


def first_sums_body(
    cols_ref, place_ref, state_ref, table_ref, out_ref, picked_ref, far_picked_ref, tiles_ref,
    sem_ref,
):
    half = table_ref.shape[2]
    blocks = state_ref.shape[1] // LANES
    first = pltpu.make_async_copy(
        table_ref, out_ref.at[:, :, pl.ds(0, half)], sem_ref.at[0]
    )
    first.start()
    resid, prob = residuals(state_ref[:K], state_ref[K : K + 1])
    cols = cols_ref[...].astype(f32)
    for step in range(ITERS):
        place = place_ref[step]
        for j in range(blocks):
            piece = cols[:, step * blocks + j, :].astype(bf16)
            picked = lax.dot_general(
                place, piece, (((0,), (0,)), ((), ())), preferred_element_type=f32
            )
            picked_ref[step, :, j * LANES : (j + 1) * LANES] = picked.astype(bf16)
    third = pltpu.make_async_copy(picked_ref, far_picked_ref, sem_ref.at[3])
    third.start()
    tile = sums_tile(resid, prob, picked_ref[0].astype(f32))
    second = send_tile(tile, tiles_ref, out_ref, sem_ref.at[1])
    wait_all([first, second, third])


def second_table_body(
    shared_ref, state_ref, state_taken_ref, picked_ref, picked_taken_ref, both_ref,
    out_ref, coef_ref, table_ref, tiles_ref, sem_ref,
):
    half = table_ref.shape[2]
    coef = coefficients(shared_ref[:, :, half:])
    coef_ref[...] = coef
    coef = lane_tile(coef, state_ref.shape[1] // LANES)
    logits = state_ref[:K] + coef * picked_ref[0].astype(f32)
    resid, prob = residuals(logits, state_ref[K : K + 1])
    tile = sums_tile(resid, prob, picked_ref[1].astype(f32))
    sums_copy = send_tile(tile, tiles_ref, out_ref, sem_ref.at[0])
    logits_taken = state_taken_ref[:K] + coef * picked_taken_ref[0].astype(f32)
    resid_taken, _ = residuals(logits_taken, state_taken_ref[K : K + 1])
    table_copies = send_table(
        resid, resid_taken, both_ref, table_ref, out_ref, sem_ref.at[pl.ds(2, 2)]
    )
    wait_all([sums_copy] + table_copies)


def third_table_body(
    shared_ref, coef_ref, state_ref, state_taken_ref, picked_ref, picked_taken_ref, both_ref,
    out_ref, logits_ref, table_ref, new_ref, sem_ref,
):
    half = table_ref.shape[2]
    blocks = state_ref.shape[1] // LANES
    now = coefficients(shared_ref[:, :, half:])
    coefs = [lane_tile(coef, blocks) for coef in (coef_ref[...], now)]

    def updated(start, columns_ref):
        for step in range(ITERS):
            start = start + coefs[step] * columns_ref[step].astype(f32)
        return start

    logits = updated(state_ref[:K], picked_ref)
    new_ref[...] = logits
    logits_copy = pltpu.make_async_copy(new_ref, logits_ref, sem_ref.at[0])
    logits_copy.start()
    resid, _ = residuals(logits, state_ref[K : K + 1])
    resid_taken, _ = residuals(
        updated(state_taken_ref[:K], picked_taken_ref), state_taken_ref[K : K + 1]
    )
    table_copies = send_table(
        resid, resid_taken, both_ref, table_ref, out_ref, sem_ref.at[pl.ds(2, 2)]
    )
    wait_all([logits_copy] + table_copies)


def shards(genotypes, labels, base_margin, winners):
    samples, columns = genotypes.shape
    feat_count = lax.axis_size("feat")
    rows_count = lax.axis_size("rows")
    class_share = K // rows_count
    half = columns // 2
    partners = [(i, i ^ 1) for i in range(rows_count)]
    work = 2 * K * 2 * samples * half
    payload_shape = (rows_count, class_share, half + 2 * K)
    table_shape = (rows_count, class_share, half)
    tiles = pltpu.VMEM((rows_count, 8, 2 * K), bf16)
    sems = pltpu.SemaphoreType.DMA

    sent, state = call(
        pick_body,
        (
            pltpu.VMEM((feat_count, ITERS * samples // LANES, LANES), bf16),
            pltpu.VMEM((K + 8, samples), f32),
        ),
        [VMEM, HBM, HBM, HBM],
        [
            pltpu.VMEM((ITERS, samples, LANES), bf16),
            pltpu.VMEM((1, samples), i32),
            sems((2 + ITERS,)),
        ],
        moved=samples * LANES * 4,
    )(near(winners), far(genotypes), far(base_margin.T), far(labels[None, :]))
    cols = lax.all_to_all(sent, "feat", 0, 0, tiled=True)

    taken = far(lax.ppermute(genotypes, "rows", partners))
    geno = far(genotypes)
    state_taken = near(lax.ppermute(state, "rows", partners))
    state = near(state)

    table, both, place = call(
        first_table_body,
        (
            pltpu.VMEM(table_shape, bf16),
            pltpu.VMEM((2 * samples, half), bf16),
            pltpu.VMEM((ITERS, feat_count, K), bf16),
        ),
        [VMEM, VMEM, HBM, HBM, HBM],
        [pltpu.VMEM((ITERS, K), i32), sems((3,))],
        flops=work,
        moved=4 * samples * half,
    )(state, state_taken, geno, taken, far(winners))

    picked_shape = (ITERS, K, samples)
    payload, picked, far_picked = call(
        first_sums_body,
        (
            pltpu.HBM(payload_shape, bf16),
            pltpu.VMEM(picked_shape, bf16),
            pltpu.HBM(picked_shape, bf16),
        ),
        [VMEM] * 4,
        [tiles, sems((4,))],
        moved=4 * samples * half,
    )(near(cols), place, state, table)
    shared0 = lax.all_to_all(payload, "rows", 0, 0, tiled=True)
    picked_taken = near(lax.ppermute(far_picked, "rows", partners))

    payload, coef = call(
        second_table_body,
        (pltpu.HBM(payload_shape, bf16), pltpu.VMEM((K, LANES), f32)),
        [VMEM] * 6,
        [pltpu.VMEM(table_shape, bf16), tiles, sems((4,))],
        flops=work,
        moved=4 * samples * half,
    )(near(shared0), state, state_taken, near(picked), picked_taken, both)
    shared1 = lax.all_to_all(payload, "rows", 0, 0, tiled=True)

    payload, logits = call(
        third_table_body,
        (pltpu.HBM(table_shape, bf16), pltpu.HBM((K, samples), f32)),
        [VMEM] * 7,
        [pltpu.VMEM(table_shape, bf16), pltpu.VMEM((K, samples), f32), sems((4,))],
        flops=work,
        moved=4 * samples * half,
    )(near(shared1), near(coef), state, state_taken, near(picked), picked_taken, both)
    shared2 = lax.all_to_all(payload, "rows", 0, 0, tiled=True)

    tables = []
    for shared in (shared0, shared1, shared2):
        parts = shared[:, :, :half].astype(f32).reshape(rows_count // 2, 2, class_share, half)
        total = jnp.sum(parts, axis=0)
        tables.append(jnp.concatenate([total[0], total[1]], axis=1))
    return (logits.T, jnp.stack(tables))


def solution(mesh):
    in_specs = (P("rows", "feat"), P("rows"), P("rows", None), P())
    out_specs = (P("rows", None), P(None, "rows", "feat"))
    return jax.shard_map(shards, mesh=mesh, in_specs=in_specs, out_specs=out_specs, check_vma=False)
```

```python
import jax
import jax.numpy as jnp
from jax import lax
from jax.experimental import pallas as pl
from jax.experimental.pallas import tpu as pltpu
from jax.sharding import PartitionSpec as P

K = 64
ITERS = 2
LANES = 128


shrink_rate = 0.5
ridge_term = 1.0

bf16 = jnp.bfloat16
f32 = jnp.float32
i32 = jnp.int32
BlockSpec = pl.BlockSpec
VMEM = pl.BlockSpec(memory_space=pltpu.VMEM)
HBM = pl.BlockSpec(memory_space=pltpu.HBM)


def call(body, out_shape, in_specs, scratch=(), flops=0, moved=0, room=8 << 20):
    out_specs = jax.tree.map(
        lambda out: BlockSpec(memory_space=out.memory_space), out_shape, is_leaf=is_out
    )
    return pl.pallas_call(
        body,
        out_shape=out_shape,
        in_specs=in_specs,
        out_specs=out_specs,
        scratch_shapes=list(scratch),
        cost_estimate=pl.CostEstimate(flops=flops, bytes_accessed=moved, transcendentals=0),
        compiler_params=pltpu.CompilerParams(vmem_limit_bytes=room),
    )


def is_out(value):
    return hasattr(value, "memory_space")


def far(values):
    return pltpu.with_memory_space_constraint(values, pltpu.HBM)


def wait_all(copies):
    for copy in copies:
        copy.wait()


def near(values):
    return pltpu.with_memory_space_constraint(values, pltpu.VMEM)


def rounded(values):
    return values.astype(bf16).astype(f32)


def split3(values):
    high = rounded(values)
    rest = values - high
    middle = rounded(rest)
    return high, middle, rest - middle


def softmax_classes(values):
    top = jnp.max(values, axis=0, keepdims=True)
    expo = jnp.exp(values - top)
    return expo / jnp.sum(expo, axis=0, keepdims=True)


def residuals(logits, label_row):
    prob = softmax_classes(logits)
    classes = lax.broadcasted_iota(i32, logits.shape, 0).astype(f32)
    onehot = jnp.where(classes == label_row, 1.0, 0.0)
    return (onehot - prob).astype(bf16), prob


def pick_body(
    win_ref, geno_ref, margin_ref, far_labels_ref, out_ref, state_ref, block_ref, labels_ref,
    sem_ref,
):
    samples, columns = geno_ref.shape
    marks = pltpu.make_async_copy(far_labels_ref, labels_ref, sem_ref.at[1])
    marks.start()
    margins = pltpu.make_async_copy(margin_ref, state_ref.at[pl.ds(0, K)], sem_ref.at[0])
    margins.start()
    local = win_ref[...] - lax.axis_index("feat") * columns
    mine = jnp.where((local >= 0) & (local < columns), local, 0).astype(f32)
    copies, lanes = [], []
    for step in range(ITERS):
        col = jnp.sum(mine[step : step + 1]).astype(i32)
        start = pl.multiple_of((col // LANES) * LANES, LANES)
        copy = pltpu.make_async_copy(
            geno_ref.at[:, pl.ds(start, LANES)], block_ref.at[step], sem_ref.at[2 + step]
        )
        copy.start()
        copies.append(copy)
        lanes.append(col - start)
    marks.wait()
    state_ref[K:] = jnp.broadcast_to(labels_ref[...].astype(f32), (8, samples))
    rows = lax.broadcasted_iota(i32, (8, LANES), 0)
    lane = lax.broadcasted_iota(i32, (8, LANES), 1)
    tile = jnp.zeros((8, LANES), f32)
    for step in range(ITERS):
        copies[step].wait()
        pick = jnp.where(lane == lanes[step], 1.0, 0.0).astype(bf16)
        x = lax.dot_general(
            pick, block_ref[step], (((1,), (1,)), ((), ())), preferred_element_type=f32
        )
        for j in range(samples // LANES):
            here = rows == step * (samples // LANES) + j
            tile = tile + jnp.where(here, x[:, j * LANES : (j + 1) * LANES], 0.0)
    out_ref[...] = jnp.broadcast_to(tile.astype(bf16)[None], out_ref.shape)
    margins.wait()


def load_halves(geno_ref, far_taken_ref, both_ref, sem_ref):
    samples = geno_ref.shape[0]
    half = both_ref.shape[1]
    start = pl.multiple_of(lax.rem(lax.axis_index("rows"), 2) * half, LANES)
    copies = [
        pltpu.make_async_copy(
            whole_ref.at[:, pl.ds(start, half)],
            both_ref.at[pl.ds(place * samples, samples)],
            sem_ref.at[place],
        )
        for place, whole_ref in enumerate((geno_ref, far_taken_ref))
    ]
    for copy in copies:
        copy.start()
    return copies


def half_table(resid, resid_taken, both_ref, start, width):
    whole = jnp.concatenate([resid, resid_taken], axis=1)
    return jnp.dot(whole, both_ref[:, pl.ds(start, width)], preferred_element_type=f32)


def sums_tile(resid, prob, picked):
    grad = resid.astype(f32) * picked
    curv = prob * (1.0 - prob) * picked * picked
    both = 0.5 * jnp.concatenate([grad, curv], axis=0)
    folded = both[:, :LANES]
    for j in range(1, both.shape[1] // LANES):
        folded = folded + both[:, j * LANES : (j + 1) * LANES]
    ones = jnp.ones((8, LANES), bf16)
    total = jnp.zeros((8, 2 * K), f32)
    for term in split3(folded):
        total = total + lax.dot_general(
            ones, term.astype(bf16), (((1,), (1,)), ((), ())), preferred_element_type=f32
        )
    high, middle, low = split3(total)
    row = lax.broadcasted_iota(i32, total.shape, 0)
    tile = jnp.where(row == 0, high, jnp.where(row == 1, middle, jnp.where(row == 2, low, 0.0)))
    return tile.astype(bf16)


def coefficients(tiles):
    tiles = tiles.astype(f32)
    row = jnp.sum(jnp.sum(tiles, axis=0), axis=0, keepdims=True)
    column = jnp.transpose(jnp.broadcast_to(row, (2 * K, LANES)))
    return shrink_rate * (2.0 * column[:K]) / (2.0 * column[K:] + ridge_term)


def lane_tile(values, count):
    return jnp.concatenate([values] * count, axis=1)


def send_tile(tile, both_ref, out_ref, sem_ref):
    half = out_ref.shape[2] - 2 * K
    both_ref[...] = jnp.broadcast_to(tile[None], both_ref.shape)
    copy = pltpu.make_async_copy(both_ref, out_ref.at[:, :, pl.ds(half, 2 * K)], sem_ref)
    copy.start()
    return copy


def send_table(resid, resid_taken, both_ref, table_ref, out_ref, sem_ref, pieces=2):
    width = table_ref.shape[2] // pieces
    copies = []
    for piece in range(pieces):
        span = pl.ds(piece * width, width)
        table = half_table(resid, resid_taken, both_ref, piece * width, width)
        table_ref[:, :, span] = table.reshape(table_ref.shape[0], -1, width).astype(bf16)
        copy = pltpu.make_async_copy(
            table_ref.at[:, :, span], out_ref.at[:, :, span], sem_ref.at[piece]
        )
        copy.start()
        copies.append(copy)
    return copies


def own_table_body(
    state_ref, geno_ref, far_taken_ref, far_win_ref, out_ref, both_ref, place_ref, win_ref, sem_ref
):
    wins = pltpu.make_async_copy(far_win_ref, win_ref, sem_ref.at[2])
    wins.start()
    copies = load_halves(geno_ref, far_taken_ref, both_ref, sem_ref)
    resid, _ = residuals(state_ref[:K], state_ref[K : K + 1])
    feat = lax.broadcasted_iota(i32, place_ref.shape[1:], 0)
    wins.wait()
    for step in range(ITERS):
        owner = win_ref[step : step + 1] // geno_ref.shape[1]
        place_ref[step] = jnp.where(feat == owner, 1.0, 0.0).astype(bf16)
    copies[0].wait()
    out_ref[...] = jnp.dot(resid, both_ref[: geno_ref.shape[0]], preferred_element_type=f32)
    copies[1].wait()


def pair_table_body(own_ref, state_taken_ref, both_ref, out_ref):
    samples = state_taken_ref.shape[1]
    resid_taken, _ = residuals(state_taken_ref[:K], state_taken_ref[K : K + 1])
    table = own_ref[...] + jnp.dot(resid_taken, both_ref[samples:], preferred_element_type=f32)
    out_ref[...] = table.reshape(out_ref.shape).astype(bf16)


def first_sums_body(
    cols_ref, place_ref, state_ref, table_ref, out_ref, picked_ref, far_picked_ref, tiles_ref,
    sem_ref,
):
    half = table_ref.shape[2]
    blocks = state_ref.shape[1] // LANES
    first = pltpu.make_async_copy(
        table_ref, out_ref.at[:, :, pl.ds(0, half)], sem_ref.at[0]
    )
    first.start()
    resid, prob = residuals(state_ref[:K], state_ref[K : K + 1])
    cols = cols_ref[...].astype(f32)
    for step in range(ITERS):
        place = place_ref[step]
        for j in range(blocks):
            piece = cols[:, step * blocks + j, :].astype(bf16)
            picked = lax.dot_general(
                place, piece, (((0,), (0,)), ((), ())), preferred_element_type=f32
            )
            picked_ref[step, :, j * LANES : (j + 1) * LANES] = picked.astype(bf16)
    third = pltpu.make_async_copy(picked_ref, far_picked_ref, sem_ref.at[3])
    third.start()
    tile = sums_tile(resid, prob, picked_ref[0].astype(f32))
    second = send_tile(tile, tiles_ref, out_ref, sem_ref.at[1])
    wait_all([first, second, third])


def second_table_body(
    shared_ref, state_ref, state_taken_ref, picked_ref, picked_taken_ref, both_ref,
    out_ref, coef_ref, table_ref, tiles_ref, sem_ref,
):
    half = table_ref.shape[2]
    coef = coefficients(shared_ref[:, :, half:])
    coef_ref[...] = coef
    coef = lane_tile(coef, state_ref.shape[1] // LANES)
    logits = state_ref[:K] + coef * picked_ref[0].astype(f32)
    resid, prob = residuals(logits, state_ref[K : K + 1])
    tile = sums_tile(resid, prob, picked_ref[1].astype(f32))
    sums_copy = send_tile(tile, tiles_ref, out_ref, sem_ref.at[0])
    logits_taken = state_taken_ref[:K] + coef * picked_taken_ref[0].astype(f32)
    resid_taken, _ = residuals(logits_taken, state_taken_ref[K : K + 1])
    table_copies = send_table(
        resid, resid_taken, both_ref, table_ref, out_ref, sem_ref.at[pl.ds(2, 2)]
    )
    wait_all([sums_copy] + table_copies)


def third_table_body(
    shared_ref, coef_ref, state_ref, state_taken_ref, picked_ref, picked_taken_ref, both_ref,
    out_ref, logits_ref, table_ref, new_ref, sem_ref,
):
    half = table_ref.shape[2]
    blocks = state_ref.shape[1] // LANES
    now = coefficients(shared_ref[:, :, half:])
    coefs = [lane_tile(coef, blocks) for coef in (coef_ref[...], now)]

    def updated(start, columns_ref):
        for step in range(ITERS):
            start = start + coefs[step] * columns_ref[step].astype(f32)
        return start

    logits = updated(state_ref[:K], picked_ref)
    new_ref[...] = logits
    logits_copy = pltpu.make_async_copy(new_ref, logits_ref, sem_ref.at[0])
    logits_copy.start()
    resid, _ = residuals(logits, state_ref[K : K + 1])
    resid_taken, _ = residuals(
        updated(state_taken_ref[:K], picked_taken_ref), state_taken_ref[K : K + 1]
    )
    table_copies = send_table(
        resid, resid_taken, both_ref, table_ref, out_ref, sem_ref.at[pl.ds(2, 2)]
    )
    wait_all([logits_copy] + table_copies)


def shards(genotypes, labels, base_margin, winners):
    samples, columns = genotypes.shape
    feat_count = lax.axis_size("feat")
    rows_count = lax.axis_size("rows")
    class_share = K // rows_count
    half = columns // 2
    partners = [(i, i ^ 1) for i in range(rows_count)]
    work = 2 * K * 2 * samples * half
    payload_shape = (rows_count, class_share, half + 2 * K)
    table_shape = (rows_count, class_share, half)
    tiles = pltpu.VMEM((rows_count, 8, 2 * K), bf16)
    sems = pltpu.SemaphoreType.DMA

    sent, state = call(
        pick_body,
        (
            pltpu.VMEM((feat_count, ITERS * samples // LANES, LANES), bf16),
            pltpu.VMEM((K + 8, samples), f32),
        ),
        [VMEM, HBM, HBM, HBM],
        [
            pltpu.VMEM((ITERS, samples, LANES), bf16),
            pltpu.VMEM((1, samples), i32),
            sems((2 + ITERS,)),
        ],
        moved=samples * LANES * 4,
    )(near(winners), far(genotypes), far(base_margin.T), far(labels[None, :]))
    cols = lax.all_to_all(sent, "feat", 0, 0, tiled=True)

    taken = far(lax.ppermute(genotypes, "rows", partners))
    geno = far(genotypes)
    state_taken = near(lax.ppermute(state, "rows", partners))
    state = near(state)

    own, both, place = call(
        own_table_body,
        (
            pltpu.VMEM((K, half), f32),
            pltpu.VMEM((2 * samples, half), bf16),
            pltpu.VMEM((ITERS, feat_count, K), bf16),
        ),
        [VMEM, HBM, HBM, HBM],
        [pltpu.VMEM((ITERS, K), i32), sems((3,))],
        flops=work // 2,
        moved=4 * samples * half,
    )(state, geno, taken, far(winners))
    table = call(
        pair_table_body,
        pltpu.VMEM(table_shape, bf16),
        [VMEM] * 3,
        flops=work // 2,
        moved=2 * samples * half,
    )(own, state_taken, both)

    picked_shape = (ITERS, K, samples)
    payload, picked, far_picked = call(
        first_sums_body,
        (
            pltpu.HBM(payload_shape, bf16),
            pltpu.VMEM(picked_shape, bf16),
            pltpu.HBM(picked_shape, bf16),
        ),
        [VMEM] * 4,
        [tiles, sems((4,))],
        moved=4 * samples * half,
    )(near(cols), place, state, table)
    shared0 = lax.all_to_all(payload, "rows", 0, 0, tiled=True)
    picked_taken = near(lax.ppermute(far_picked, "rows", partners))

    payload, coef = call(
        second_table_body,
        (pltpu.HBM(payload_shape, bf16), pltpu.VMEM((K, LANES), f32)),
        [VMEM] * 6,
        [pltpu.VMEM(table_shape, bf16), tiles, sems((4,))],
        flops=work,
        moved=4 * samples * half,
    )(near(shared0), state, state_taken, near(picked), picked_taken, both)
    shared1 = lax.all_to_all(payload, "rows", 0, 0, tiled=True)

    payload, logits = call(
        third_table_body,
        (pltpu.HBM(table_shape, bf16), pltpu.HBM((K, samples), f32)),
        [VMEM] * 7,
        [pltpu.VMEM(table_shape, bf16), pltpu.VMEM((K, samples), f32), sems((4,))],
        flops=work,
        moved=4 * samples * half,
    )(near(shared1), near(coef), state, state_taken, near(picked), picked_taken, both)
    shared2 = lax.all_to_all(payload, "rows", 0, 0, tiled=True)

    tables = []
    for shared in (shared0, shared1, shared2):
        parts = shared[:, :, :half].astype(f32).reshape(rows_count // 2, 2, class_share, half)
        total = jnp.sum(parts, axis=0)
        tables.append(jnp.concatenate([total[0], total[1]], axis=1))
    return (logits.T, jnp.stack(tables))


def solution(mesh):
    in_specs = (P("rows", "feat"), P("rows"), P("rows", None), P())
    out_specs = (P("rows", None), P(None, "rows", "feat"))
    return jax.shard_map(shards, mesh=mesh, in_specs=in_specs, out_specs=out_specs, check_vma=False)
```

```python
import jax
import jax.numpy as jnp
from jax import lax
from jax.experimental import pallas as pl
from jax.experimental.pallas import tpu as pltpu
from jax.sharding import PartitionSpec as P

K = 64
ITERS = 2
LANES = 128


shrink_rate = 0.5
ridge_term = 1.0

bf16 = jnp.bfloat16
f32 = jnp.float32
i32 = jnp.int32
BlockSpec = pl.BlockSpec
VMEM = pl.BlockSpec(memory_space=pltpu.VMEM)
HBM = pl.BlockSpec(memory_space=pltpu.HBM)


def call(body, out_shape, in_specs, scratch=(), flops=0, moved=0, room=8 << 20):
    out_specs = jax.tree.map(
        lambda out: BlockSpec(memory_space=out.memory_space), out_shape, is_leaf=is_out
    )
    return pl.pallas_call(
        body,
        out_shape=out_shape,
        in_specs=in_specs,
        out_specs=out_specs,
        scratch_shapes=list(scratch),
        cost_estimate=pl.CostEstimate(flops=flops, bytes_accessed=moved, transcendentals=0),
        compiler_params=pltpu.CompilerParams(vmem_limit_bytes=room),
    )


def is_out(value):
    return hasattr(value, "memory_space")


def far(values):
    return pltpu.with_memory_space_constraint(values, pltpu.HBM)


def wait_all(copies):
    for copy in copies:
        copy.wait()


def near(values):
    return pltpu.with_memory_space_constraint(values, pltpu.VMEM)


def rounded(values):
    return values.astype(bf16).astype(f32)


def split3(values):
    high = rounded(values)
    rest = values - high
    middle = rounded(rest)
    return high, middle, rest - middle


def softmax_classes(values):
    top = jnp.max(values, axis=0, keepdims=True)
    expo = jnp.exp(values - top)
    return expo / jnp.sum(expo, axis=0, keepdims=True)


def residuals(logits, label_row):
    prob = softmax_classes(logits)
    classes = lax.broadcasted_iota(i32, logits.shape, 0).astype(f32)
    onehot = jnp.where(classes == label_row, 1.0, 0.0)
    return (onehot - prob).astype(bf16), prob


def pick_body(
    win_ref, geno_ref, margin_ref, far_labels_ref, out_ref, state_ref, block_ref, labels_ref,
    sem_ref,
):
    samples, columns = geno_ref.shape
    marks = pltpu.make_async_copy(far_labels_ref, labels_ref, sem_ref.at[1])
    marks.start()
    margins = pltpu.make_async_copy(margin_ref, state_ref.at[pl.ds(0, K)], sem_ref.at[0])
    margins.start()
    local = win_ref[...] - lax.axis_index("feat") * columns
    mine = jnp.where((local >= 0) & (local < columns), local, 0).astype(f32)
    copies, lanes = [], []
    for step in range(ITERS):
        col = jnp.sum(mine[step : step + 1]).astype(i32)
        start = pl.multiple_of((col // LANES) * LANES, LANES)
        copy = pltpu.make_async_copy(
            geno_ref.at[:, pl.ds(start, LANES)], block_ref.at[step], sem_ref.at[2 + step]
        )
        copy.start()
        copies.append(copy)
        lanes.append(col - start)
    marks.wait()
    state_ref[K:] = jnp.broadcast_to(labels_ref[...].astype(f32), (8, samples))
    rows = lax.broadcasted_iota(i32, (8, LANES), 0)
    lane = lax.broadcasted_iota(i32, (8, LANES), 1)
    tile = jnp.zeros((8, LANES), f32)
    for step in range(ITERS):
        copies[step].wait()
        pick = jnp.where(lane == lanes[step], 1.0, 0.0).astype(bf16)
        x = lax.dot_general(
            pick, block_ref[step], (((1,), (1,)), ((), ())), preferred_element_type=f32
        )
        for j in range(samples // LANES):
            here = rows == step * (samples // LANES) + j
            tile = tile + jnp.where(here, x[:, j * LANES : (j + 1) * LANES], 0.0)
    out_ref[...] = jnp.broadcast_to(tile.astype(bf16)[None], out_ref.shape)
    margins.wait()


def load_halves(geno_ref, far_taken_ref, both_ref, sem_ref):
    samples = geno_ref.shape[0]
    half = both_ref.shape[1]
    start = pl.multiple_of(lax.rem(lax.axis_index("rows"), 2) * half, LANES)
    copies = [
        pltpu.make_async_copy(
            whole_ref.at[:, pl.ds(start, half)],
            both_ref.at[pl.ds(place * samples, samples)],
            sem_ref.at[place],
        )
        for place, whole_ref in enumerate((geno_ref, far_taken_ref))
    ]
    for copy in copies:
        copy.start()
    return copies


def sums_tile(resid, prob, picked):
    grad = resid.astype(f32) * picked
    curv = prob * (1.0 - prob) * picked * picked
    both = 0.5 * jnp.concatenate([grad, curv], axis=0)
    folded = both[:, :LANES]
    for j in range(1, both.shape[1] // LANES):
        folded = folded + both[:, j * LANES : (j + 1) * LANES]
    ones = jnp.ones((8, LANES), bf16)
    total = jnp.zeros((8, 2 * K), f32)
    for term in split3(folded):
        total = total + lax.dot_general(
            ones, term.astype(bf16), (((1,), (1,)), ((), ())), preferred_element_type=f32
        )
    high, middle, low = split3(total)
    row = lax.broadcasted_iota(i32, total.shape, 0)
    tile = jnp.where(row == 0, high, jnp.where(row == 1, middle, jnp.where(row == 2, low, 0.0)))
    return tile.astype(bf16)


def coefficients(tiles):
    tiles = tiles.astype(f32)
    row = jnp.sum(jnp.sum(tiles, axis=0), axis=0, keepdims=True)
    column = jnp.transpose(jnp.broadcast_to(row, (2 * K, LANES)))
    return shrink_rate * (2.0 * column[:K]) / (2.0 * column[K:] + ridge_term)


def lane_tile(values, count):
    return jnp.concatenate([values] * count, axis=1)


def fill_tile(tile, tiles_ref):
    tiles_ref[...] = jnp.broadcast_to(tile[None], tiles_ref.shape)


def send(pairs, sem_ref):
    copies = [
        pltpu.make_async_copy(source, target, sem_ref.at[i])
        for i, (source, target) in enumerate(pairs)
    ]
    for copy in copies:
        copy.start()
    wait_all(copies)


def fill_table(resid, resid_taken, both_ref, table_ref):
    whole = jnp.concatenate([resid, resid_taken], axis=1)
    table = jnp.dot(whole, both_ref[...], preferred_element_type=f32)
    table_ref[...] = table.reshape(table_ref.shape).astype(bf16)


def own_table_body(
    state_ref, geno_ref, far_taken_ref, far_win_ref, out_ref, both_ref, place_ref, win_ref, sem_ref
):
    wins = pltpu.make_async_copy(far_win_ref, win_ref, sem_ref.at[2])
    wins.start()
    copies = load_halves(geno_ref, far_taken_ref, both_ref, sem_ref)
    resid, _ = residuals(state_ref[:K], state_ref[K : K + 1])
    feat = lax.broadcasted_iota(i32, place_ref.shape[1:], 0)
    wins.wait()
    for step in range(ITERS):
        owner = win_ref[step : step + 1] // geno_ref.shape[1]
        place_ref[step] = jnp.where(feat == owner, 1.0, 0.0).astype(bf16)
    copies[0].wait()
    out_ref[...] = jnp.dot(resid, both_ref[: geno_ref.shape[0]], preferred_element_type=f32)
    copies[1].wait()


def pair_table_body(own_ref, state_taken_ref, both_ref, out_ref):
    samples = state_taken_ref.shape[1]
    resid_taken, _ = residuals(state_taken_ref[:K], state_taken_ref[K : K + 1])
    table = own_ref[...] + jnp.dot(resid_taken, both_ref[samples:], preferred_element_type=f32)
    out_ref[...] = table.reshape(out_ref.shape).astype(bf16)


def first_sums_body(
    cols_ref, place_ref, state_ref, table_ref, out_ref, picked_ref, far_picked_ref, tiles_ref,
    sem_ref,
):
    half = table_ref.shape[2]
    blocks = state_ref.shape[1] // LANES
    first = pltpu.make_async_copy(
        table_ref, out_ref.at[:, :, pl.ds(0, half)], sem_ref.at[0]
    )
    first.start()
    resid, prob = residuals(state_ref[:K], state_ref[K : K + 1])
    cols = cols_ref[...].astype(f32)
    for step in range(ITERS):
        place = place_ref[step]
        for j in range(blocks):
            piece = cols[:, step * blocks + j, :].astype(bf16)
            picked = lax.dot_general(
                place, piece, (((0,), (0,)), ((), ())), preferred_element_type=f32
            )
            picked_ref[step, :, j * LANES : (j + 1) * LANES] = picked.astype(bf16)
    third = pltpu.make_async_copy(picked_ref, far_picked_ref, sem_ref.at[3])
    third.start()
    tile = sums_tile(resid, prob, picked_ref[0].astype(f32))
    fill_tile(tile, tiles_ref)
    send([(tiles_ref, out_ref.at[:, :, pl.ds(half, 2 * K)])], sem_ref.at[pl.ds(1, 1)])
    wait_all([first, third])


def second_table_body(
    shared_ref, state_ref, state_taken_ref, picked_ref, picked_taken_ref, both_ref,
    out_ref, coef_ref, table_ref, tiles_ref, sem_ref,
):
    half = table_ref.shape[2]
    coef = coefficients(shared_ref[:, :, half:])
    coef_ref[...] = coef
    coef = lane_tile(coef, state_ref.shape[1] // LANES)
    logits = state_ref[:K] + coef * picked_ref[0].astype(f32)
    resid, prob = residuals(logits, state_ref[K : K + 1])
    tile = sums_tile(resid, prob, picked_ref[1].astype(f32))
    fill_tile(tile, tiles_ref)
    logits_taken = state_taken_ref[:K] + coef * picked_taken_ref[0].astype(f32)
    resid_taken, _ = residuals(logits_taken, state_taken_ref[K : K + 1])
    fill_table(resid, resid_taken, both_ref, table_ref)
    send(
        [
            (table_ref, out_ref.at[:, :, pl.ds(0, half)]),
            (tiles_ref, out_ref.at[:, :, pl.ds(half, 2 * K)]),
        ],
        sem_ref,
    )


def third_table_body(
    shared_ref, coef_ref, state_ref, state_taken_ref, picked_ref, picked_taken_ref, both_ref,
    out_ref, logits_ref, table_ref, new_ref, sem_ref,
):
    half = table_ref.shape[2]
    blocks = state_ref.shape[1] // LANES
    now = coefficients(shared_ref[:, :, half:])
    coefs = [lane_tile(coef, blocks) for coef in (coef_ref[...], now)]

    def updated(start, columns_ref):
        for step in range(ITERS):
            start = start + coefs[step] * columns_ref[step].astype(f32)
        return start

    logits = updated(state_ref[:K], picked_ref)
    new_ref[...] = logits
    resid, _ = residuals(logits, state_ref[K : K + 1])
    resid_taken, _ = residuals(
        updated(state_taken_ref[:K], picked_taken_ref), state_taken_ref[K : K + 1]
    )
    fill_table(resid, resid_taken, both_ref, table_ref)
    send([(table_ref, out_ref), (new_ref, logits_ref)], sem_ref)


def shards(genotypes, labels, base_margin, winners):
    samples, columns = genotypes.shape
    feat_count = lax.axis_size("feat")
    rows_count = lax.axis_size("rows")
    class_share = K // rows_count
    half = columns // 2
    partners = [(i, i ^ 1) for i in range(rows_count)]
    work = 2 * K * 2 * samples * half
    payload_shape = (rows_count, class_share, half + 2 * K)
    table_shape = (rows_count, class_share, half)
    tiles = pltpu.VMEM((rows_count, 8, 2 * K), bf16)
    sems = pltpu.SemaphoreType.DMA

    sent, state = call(
        pick_body,
        (
            pltpu.VMEM((feat_count, ITERS * samples // LANES, LANES), bf16),
            pltpu.VMEM((K + 8, samples), f32),
        ),
        [VMEM, HBM, HBM, HBM],
        [
            pltpu.VMEM((ITERS, samples, LANES), bf16),
            pltpu.VMEM((1, samples), i32),
            sems((2 + ITERS,)),
        ],
        moved=samples * LANES * 4,
    )(near(winners), far(genotypes), far(base_margin.T), far(labels[None, :]))
    cols = lax.all_to_all(sent, "feat", 0, 0, tiled=True)

    taken = far(lax.ppermute(genotypes, "rows", partners))
    geno = far(genotypes)
    state_taken = near(lax.ppermute(state, "rows", partners))
    state = near(state)

    own, both, place = call(
        own_table_body,
        (
            pltpu.VMEM((K, half), f32),
            pltpu.VMEM((2 * samples, half), bf16),
            pltpu.VMEM((ITERS, feat_count, K), bf16),
        ),
        [VMEM, HBM, HBM, HBM],
        [pltpu.VMEM((ITERS, K), i32), sems((3,))],
        flops=work // 2,
        moved=4 * samples * half,
    )(state, geno, taken, far(winners))
    table = call(
        pair_table_body,
        pltpu.VMEM(table_shape, bf16),
        [VMEM] * 3,
        flops=work // 2,
        moved=2 * samples * half,
    )(own, state_taken, both)

    picked_shape = (ITERS, K, samples)
    payload, picked, far_picked = call(
        first_sums_body,
        (
            pltpu.HBM(payload_shape, bf16),
            pltpu.VMEM(picked_shape, bf16),
            pltpu.HBM(picked_shape, bf16),
        ),
        [VMEM] * 4,
        [tiles, sems((4,))],
        moved=4 * samples * half,
    )(near(cols), place, state, table)
    shared0 = lax.all_to_all(payload, "rows", 0, 0, tiled=True)
    picked_taken = near(lax.ppermute(far_picked, "rows", partners))

    payload, coef = call(
        second_table_body,
        (pltpu.HBM(payload_shape, bf16), pltpu.VMEM((K, LANES), f32)),
        [VMEM] * 6,
        [pltpu.VMEM(table_shape, bf16), tiles, sems((2,))],
        flops=work,
        moved=4 * samples * half,
    )(near(shared0), state, state_taken, near(picked), picked_taken, both)
    shared1 = lax.all_to_all(payload, "rows", 0, 0, tiled=True)

    payload, logits = call(
        third_table_body,
        (pltpu.HBM(table_shape, bf16), pltpu.HBM((K, samples), f32)),
        [VMEM] * 7,
        [pltpu.VMEM(table_shape, bf16), pltpu.VMEM((K, samples), f32), sems((2,))],
        flops=work,
        moved=4 * samples * half,
    )(near(shared1), near(coef), state, state_taken, near(picked), picked_taken, both)
    shared2 = lax.all_to_all(payload, "rows", 0, 0, tiled=True)

    tables = []
    for shared in (shared0, shared1, shared2):
        parts = shared[:, :, :half].astype(f32).reshape(rows_count // 2, 2, class_share, half)
        total = jnp.sum(parts, axis=0)
        tables.append(jnp.concatenate([total[0], total[1]], axis=1))
    return (logits.T, jnp.stack(tables))


def solution(mesh):
    in_specs = (P("rows", "feat"), P("rows"), P("rows", None), P())
    out_specs = (P("rows", None), P(None, "rows", "feat"))
    return jax.shard_map(shards, mesh=mesh, in_specs=in_specs, out_specs=out_specs, check_vma=False)
```

```python
import jax
import jax.numpy as jnp
from jax import lax
from jax.experimental import pallas as pl
from jax.experimental.pallas import tpu as pltpu
from jax.sharding import PartitionSpec as P

K = 64
ITERS = 2
LANES = 128
SUMS_ORDER = (0, 4, 2, 6, 1, 5, 3, 7)
LAST_ORDER = (0, 2, 6, 4, 1, 3, 7, 5)


shrink_rate = 0.5
ridge_term = 1.0

bf16 = jnp.bfloat16
f32 = jnp.float32
i32 = jnp.int32
BlockSpec = pl.BlockSpec
VMEM = pl.BlockSpec(memory_space=pltpu.VMEM)
HBM = pl.BlockSpec(memory_space=pltpu.HBM)


def call(body, out_shape, in_specs, scratch=(), flops=0, moved=0, room=8 << 20):
    out_specs = jax.tree.map(
        lambda out: BlockSpec(memory_space=out.memory_space), out_shape, is_leaf=is_out
    )
    return pl.pallas_call(
        body,
        out_shape=out_shape,
        in_specs=in_specs,
        out_specs=out_specs,
        scratch_shapes=list(scratch),
        cost_estimate=pl.CostEstimate(flops=flops, bytes_accessed=moved, transcendentals=0),
        compiler_params=pltpu.CompilerParams(vmem_limit_bytes=room),
    )


def is_out(value):
    return hasattr(value, "memory_space")


def far(values):
    return pltpu.with_memory_space_constraint(values, pltpu.HBM)


def wait_all(copies):
    for copy in copies:
        copy.wait()


def near(values):
    return pltpu.with_memory_space_constraint(values, pltpu.VMEM)


def reverse_bits(values, count):
    bits = count.bit_length() - 1
    return sum(((values >> bit) & 1) << (bits - 1 - bit) for bit in range(bits))


def place_classes(table, out_ref, span, order):
    share = out_ref.shape[1]
    for place, peer in enumerate(order):
        out_ref[place, :, span] = table[peer * share : (peer + 1) * share].astype(bf16)


def exchange(payload, order):
    return lax.all_to_all(
        payload, "rows", 0, 0, tiled=True, axis_index_groups=[list(order)]
    )


def rounded(values):
    return values.astype(bf16).astype(f32)


def split3(values):
    high = rounded(values)
    rest = values - high
    middle = rounded(rest)
    return high, middle, rest - middle


def softmax_classes(values):
    top = jnp.max(values, axis=0, keepdims=True)
    expo = jnp.exp(values - top)
    return expo / jnp.sum(expo, axis=0, keepdims=True)


def residuals(logits, label_row):
    prob = softmax_classes(logits)
    classes = lax.broadcasted_iota(i32, logits.shape, 0).astype(f32)
    onehot = jnp.where(classes == label_row, 1.0, 0.0)
    return (onehot - prob).astype(bf16), prob


def pick_body(
    win_ref, geno_ref, margin_ref, far_labels_ref, out_ref, state_ref, block_ref, labels_ref,
    sem_ref,
):
    samples, columns = geno_ref.shape
    marks = pltpu.make_async_copy(far_labels_ref, labels_ref, sem_ref.at[1])
    marks.start()
    margins = pltpu.make_async_copy(margin_ref, state_ref.at[pl.ds(0, K)], sem_ref.at[0])
    margins.start()
    local = win_ref[...] - lax.axis_index("feat") * columns
    mine = jnp.where((local >= 0) & (local < columns), local, 0).astype(f32)
    copies, lanes = [], []
    for step in range(ITERS):
        col = jnp.sum(mine[step : step + 1]).astype(i32)
        start = pl.multiple_of((col // LANES) * LANES, LANES)
        copy = pltpu.make_async_copy(
            geno_ref.at[:, pl.ds(start, LANES)], block_ref.at[step], sem_ref.at[2 + step]
        )
        copy.start()
        copies.append(copy)
        lanes.append(col - start)
    marks.wait()
    state_ref[K:] = jnp.broadcast_to(labels_ref[...].astype(f32), (8, samples))
    rows = lax.broadcasted_iota(i32, (8, LANES), 0)
    lane = lax.broadcasted_iota(i32, (8, LANES), 1)
    tile = jnp.zeros((8, LANES), f32)
    for step in range(ITERS):
        copies[step].wait()
        pick = jnp.where(lane == lanes[step], 1.0, 0.0).astype(bf16)
        x = lax.dot_general(
            pick, block_ref[step], (((1,), (1,)), ((), ())), preferred_element_type=f32
        )
        for j in range(samples // LANES):
            here = rows == step * (samples // LANES) + j
            tile = tile + jnp.where(here, x[:, j * LANES : (j + 1) * LANES], 0.0)
    out_ref[...] = jnp.broadcast_to(tile.astype(bf16)[None], out_ref.shape)
    margins.wait()


def load_halves(geno_ref, far_taken_ref, both_ref, sem_ref):
    samples = geno_ref.shape[0]
    half = both_ref.shape[1]
    start = pl.multiple_of(lax.rem(lax.axis_index("rows"), 2) * half, LANES)
    copies = [
        pltpu.make_async_copy(
            whole_ref.at[:, pl.ds(start, half)],
            both_ref.at[pl.ds(place * samples, samples)],
            sem_ref.at[place],
        )
        for place, whole_ref in enumerate((geno_ref, far_taken_ref))
    ]
    for copy in copies:
        copy.start()
    return copies


def half_table(resid, resid_taken, both_ref, start, width):
    whole = jnp.concatenate([resid, resid_taken], axis=1)
    return jnp.dot(whole, both_ref[:, pl.ds(start, width)], preferred_element_type=f32)


def sums_tile(resid, prob, picked):
    grad = resid.astype(f32) * picked
    curv = prob * (1.0 - prob) * picked * picked
    both = 0.5 * jnp.concatenate([grad, curv], axis=0)
    folded = both[:, :LANES]
    for j in range(1, both.shape[1] // LANES):
        folded = folded + both[:, j * LANES : (j + 1) * LANES]
    ones = jnp.ones((8, LANES), bf16)
    total = jnp.zeros((8, 2 * K), f32)
    for term in split3(folded):
        total = total + lax.dot_general(
            ones, term.astype(bf16), (((1,), (1,)), ((), ())), preferred_element_type=f32
        )
    high, middle, low = split3(total)
    row = lax.broadcasted_iota(i32, total.shape, 0)
    tile = jnp.where(row == 0, high, jnp.where(row == 1, middle, jnp.where(row == 2, low, 0.0)))
    return tile.astype(bf16)


def coefficients(tiles):
    tiles = tiles.astype(f32)
    row = jnp.sum(jnp.sum(tiles, axis=0), axis=0, keepdims=True)
    column = jnp.transpose(jnp.broadcast_to(row, (2 * K, LANES)))
    return shrink_rate * (2.0 * column[:K]) / (2.0 * column[K:] + ridge_term)


def lane_tile(values, count):
    return jnp.concatenate([values] * count, axis=1)


def send_tile(tile, both_ref, out_ref, sem_ref):
    half = out_ref.shape[2] - 2 * K
    both_ref[...] = jnp.broadcast_to(tile[None], both_ref.shape)
    copy = pltpu.make_async_copy(both_ref, out_ref.at[:, :, pl.ds(half, 2 * K)], sem_ref)
    copy.start()
    return copy


def send_table(resid, resid_taken, both_ref, table_ref, out_ref, sem_ref, order, pieces=2):
    width = table_ref.shape[2] // pieces
    copies = []
    for piece in range(pieces):
        span = pl.ds(piece * width, width)
        table = half_table(resid, resid_taken, both_ref, piece * width, width)
        place_classes(table, table_ref, span, order)
        copy = pltpu.make_async_copy(
            table_ref.at[:, :, span], out_ref.at[:, :, span], sem_ref.at[piece]
        )
        copy.start()
        copies.append(copy)
    return copies


def own_table_body(
    state_ref, geno_ref, far_taken_ref, far_win_ref, out_ref, both_ref, place_ref, win_ref, sem_ref
):
    wins = pltpu.make_async_copy(far_win_ref, win_ref, sem_ref.at[2])
    wins.start()
    copies = load_halves(geno_ref, far_taken_ref, both_ref, sem_ref)
    resid, _ = residuals(state_ref[:K], state_ref[K : K + 1])
    feat = reverse_bits(
        lax.broadcasted_iota(i32, place_ref.shape[1:], 0), place_ref.shape[1]
    )
    wins.wait()
    for step in range(ITERS):
        owner = win_ref[step : step + 1] // geno_ref.shape[1]
        place_ref[step] = jnp.where(feat == owner, 1.0, 0.0).astype(bf16)
    copies[0].wait()
    out_ref[...] = jnp.dot(resid, both_ref[: geno_ref.shape[0]], preferred_element_type=f32)
    copies[1].wait()


def pair_table_body(own_ref, state_taken_ref, both_ref, out_ref):
    samples = state_taken_ref.shape[1]
    resid_taken, _ = residuals(state_taken_ref[:K], state_taken_ref[K : K + 1])
    table = own_ref[...] + jnp.dot(resid_taken, both_ref[samples:], preferred_element_type=f32)
    place_classes(table, out_ref, slice(None), SUMS_ORDER)


def first_sums_body(
    cols_ref, place_ref, state_ref, table_ref, out_ref, picked_ref, far_picked_ref, tiles_ref,
    sem_ref,
):
    half = table_ref.shape[2]
    blocks = state_ref.shape[1] // LANES
    first = pltpu.make_async_copy(
        table_ref, out_ref.at[:, :, pl.ds(0, half)], sem_ref.at[0]
    )
    first.start()
    resid, prob = residuals(state_ref[:K], state_ref[K : K + 1])
    cols = cols_ref[...].astype(f32)
    for step in range(ITERS):
        place = place_ref[step]
        for j in range(blocks):
            piece = cols[:, step * blocks + j, :].astype(bf16)
            picked = lax.dot_general(
                place, piece, (((0,), (0,)), ((), ())), preferred_element_type=f32
            )
            picked_ref[step, :, j * LANES : (j + 1) * LANES] = picked.astype(bf16)
    third = pltpu.make_async_copy(picked_ref, far_picked_ref, sem_ref.at[3])
    third.start()
    tile = sums_tile(resid, prob, picked_ref[0].astype(f32))
    second = send_tile(tile, tiles_ref, out_ref, sem_ref.at[1])
    wait_all([first, second, third])


def second_table_body(
    shared_ref, state_ref, state_taken_ref, picked_ref, picked_taken_ref, both_ref,
    out_ref, coef_ref, table_ref, tiles_ref, sem_ref,
):
    half = table_ref.shape[2]
    coef = coefficients(shared_ref[:, :, half:])
    coef_ref[...] = coef
    coef = lane_tile(coef, state_ref.shape[1] // LANES)
    logits = state_ref[:K] + coef * picked_ref[0].astype(f32)
    resid, prob = residuals(logits, state_ref[K : K + 1])
    tile = sums_tile(resid, prob, picked_ref[1].astype(f32))
    sums_copy = send_tile(tile, tiles_ref, out_ref, sem_ref.at[0])
    logits_taken = state_taken_ref[:K] + coef * picked_taken_ref[0].astype(f32)
    resid_taken, _ = residuals(logits_taken, state_taken_ref[K : K + 1])
    table_copies = send_table(
        resid, resid_taken, both_ref, table_ref, out_ref, sem_ref.at[pl.ds(2, 2)],
        SUMS_ORDER,
    )
    wait_all([sums_copy] + table_copies)


def third_table_body(
    shared_ref, coef_ref, state_ref, state_taken_ref, picked_ref, picked_taken_ref, both_ref,
    out_ref, logits_ref, table_ref, new_ref, sem_ref,
):
    half = table_ref.shape[2]
    blocks = state_ref.shape[1] // LANES
    now = coefficients(shared_ref[:, :, half:])
    coefs = [lane_tile(coef, blocks) for coef in (coef_ref[...], now)]

    def updated(start, columns_ref):
        for step in range(ITERS):
            start = start + coefs[step] * columns_ref[step].astype(f32)
        return start

    logits = updated(state_ref[:K], picked_ref)
    new_ref[...] = logits
    logits_copy = pltpu.make_async_copy(new_ref, logits_ref, sem_ref.at[0])
    logits_copy.start()
    resid, _ = residuals(logits, state_ref[K : K + 1])
    resid_taken, _ = residuals(
        updated(state_taken_ref[:K], picked_taken_ref), state_taken_ref[K : K + 1]
    )
    table_copies = send_table(
        resid, resid_taken, both_ref, table_ref, out_ref, sem_ref.at[pl.ds(2, 2)],
        LAST_ORDER,
    )
    wait_all([logits_copy] + table_copies)


def shards(genotypes, labels, base_margin, winners):
    samples, columns = genotypes.shape
    feat_count = lax.axis_size("feat")
    rows_count = lax.axis_size("rows")
    class_share = K // rows_count
    half = columns // 2
    partners = [(i, i ^ 1) for i in range(rows_count)]
    work = 2 * K * 2 * samples * half
    payload_shape = (rows_count, class_share, half + 2 * K)
    table_shape = (rows_count, class_share, half)
    tiles = pltpu.VMEM((rows_count, 8, 2 * K), bf16)
    sems = pltpu.SemaphoreType.DMA

    sent, state = call(
        pick_body,
        (
            pltpu.VMEM((feat_count, ITERS * samples // LANES, LANES), bf16),
            pltpu.VMEM((K + 8, samples), f32),
        ),
        [VMEM, HBM, HBM, HBM],
        [
            pltpu.VMEM((ITERS, samples, LANES), bf16),
            pltpu.VMEM((1, samples), i32),
            sems((2 + ITERS,)),
        ],
        moved=samples * LANES * 4,
    )(near(winners), far(genotypes), far(base_margin.T), far(labels[None, :]))
    listed = [reverse_bits(i, feat_count) for i in range(feat_count)]
    cols = lax.all_to_all(sent, "feat", 0, 0, tiled=True, axis_index_groups=[listed])

    taken = far(lax.ppermute(genotypes, "rows", partners))
    geno = far(genotypes)
    state_taken = near(lax.ppermute(state, "rows", partners))
    state = near(state)

    own, both, place = call(
        own_table_body,
        (
            pltpu.VMEM((K, half), f32),
            pltpu.VMEM((2 * samples, half), bf16),
            pltpu.VMEM((ITERS, feat_count, K), bf16),
        ),
        [VMEM, HBM, HBM, HBM],
        [pltpu.VMEM((ITERS, K), i32), sems((3,))],
        flops=work // 2,
        moved=4 * samples * half,
    )(state, geno, taken, far(winners))
    table = call(
        pair_table_body,
        pltpu.VMEM(table_shape, bf16),
        [VMEM] * 3,
        flops=work // 2,
        moved=2 * samples * half,
    )(own, state_taken, both)

    picked_shape = (ITERS, K, samples)
    payload, picked, far_picked = call(
        first_sums_body,
        (
            pltpu.HBM(payload_shape, bf16),
            pltpu.VMEM(picked_shape, bf16),
            pltpu.HBM(picked_shape, bf16),
        ),
        [VMEM] * 4,
        [tiles, sems((4,))],
        moved=4 * samples * half,
    )(near(cols), place, state, table)
    shared0 = exchange(payload, SUMS_ORDER)
    picked_taken = near(lax.ppermute(far_picked, "rows", partners))

    payload, coef = call(
        second_table_body,
        (pltpu.HBM(payload_shape, bf16), pltpu.VMEM((K, LANES), f32)),
        [VMEM] * 6,
        [pltpu.VMEM(table_shape, bf16), tiles, sems((4,))],
        flops=work,
        moved=4 * samples * half,
    )(near(shared0), state, state_taken, near(picked), picked_taken, both)
    shared1 = exchange(payload, SUMS_ORDER)

    payload, logits = call(
        third_table_body,
        (pltpu.HBM(table_shape, bf16), pltpu.HBM((K, samples), f32)),
        [VMEM] * 7,
        [pltpu.VMEM(table_shape, bf16), pltpu.VMEM((K, samples), f32), sems((4,))],
        flops=work,
        moved=4 * samples * half,
    )(near(shared1), near(coef), state, state_taken, near(picked), picked_taken, both)
    shared2 = exchange(payload, LAST_ORDER)

    tables = []
    for shared, order in ((shared0, SUMS_ORDER), (shared1, SUMS_ORDER), (shared2, LAST_ORDER)):
        parts = shared[:, :, :half].astype(f32)
        sides = [
            sum(parts[place] for place, peer in enumerate(order) if peer % 2 == side)
            for side in range(2)
        ]
        tables.append(jnp.concatenate(sides, axis=1))
    return (logits.T, jnp.stack(tables))


def solution(mesh):
    in_specs = (P("rows", "feat"), P("rows"), P("rows", None), P())
    out_specs = (P("rows", None), P(None, "rows", "feat"))
    return jax.shard_map(shards, mesh=mesh, in_specs=in_specs, out_specs=out_specs, check_vma=False)
```

```python
import jax
import jax.numpy as jnp
from jax import lax
from jax.experimental import pallas as pl
from jax.experimental.pallas import tpu as pltpu
from jax.sharding import PartitionSpec as P

K = 64
ITERS = 2
LANES = 128
SUMS_ORDER = (0, 4, 2, 6, 1, 5, 3, 7)
LAST_ORDER = (0, 4, 2, 6, 1, 5, 3, 7)


shrink_rate = 0.5
ridge_term = 1.0

bf16 = jnp.bfloat16
f32 = jnp.float32
i32 = jnp.int32
BlockSpec = pl.BlockSpec
VMEM = pl.BlockSpec(memory_space=pltpu.VMEM)
HBM = pl.BlockSpec(memory_space=pltpu.HBM)


def call(body, out_shape, in_specs, scratch=(), flops=0, moved=0, room=8 << 20):
    out_specs = jax.tree.map(
        lambda out: BlockSpec(memory_space=out.memory_space), out_shape, is_leaf=is_out
    )
    return pl.pallas_call(
        body,
        out_shape=out_shape,
        in_specs=in_specs,
        out_specs=out_specs,
        scratch_shapes=list(scratch),
        cost_estimate=pl.CostEstimate(flops=flops, bytes_accessed=moved, transcendentals=0),
        compiler_params=pltpu.CompilerParams(vmem_limit_bytes=room),
    )


def is_out(value):
    return hasattr(value, "memory_space")


def far(values):
    return pltpu.with_memory_space_constraint(values, pltpu.HBM)


def wait_all(copies):
    for copy in copies:
        copy.wait()


def near(values):
    return pltpu.with_memory_space_constraint(values, pltpu.VMEM)


def reverse_bits(values, count):
    bits = count.bit_length() - 1
    return sum(((values >> bit) & 1) << (bits - 1 - bit) for bit in range(bits))


def place_classes(table, out_ref, span, order):
    share = out_ref.shape[1]
    for place, peer in enumerate(order):
        out_ref[place, :, span] = table[peer * share : (peer + 1) * share].astype(bf16)


def exchange(payload, order):
    return lax.all_to_all(
        payload, "rows", 0, 0, tiled=True, axis_index_groups=[list(order)]
    )


def rounded(values):
    return values.astype(bf16).astype(f32)


def split3(values):
    high = rounded(values)
    rest = values - high
    middle = rounded(rest)
    return high, middle, rest - middle


def softmax_classes(values):
    top = jnp.max(values, axis=0, keepdims=True)
    expo = jnp.exp(values - top)
    return expo / jnp.sum(expo, axis=0, keepdims=True)


def residuals(logits, label_row):
    prob = softmax_classes(logits)
    classes = lax.broadcasted_iota(i32, logits.shape, 0).astype(f32)
    onehot = jnp.where(classes == label_row, 1.0, 0.0)
    return (onehot - prob).astype(bf16), prob


def pick_body(
    win_ref, geno_ref, margin_ref, far_labels_ref, out_ref, state_ref, block_ref, labels_ref,
    sem_ref,
):
    samples, columns = geno_ref.shape
    marks = pltpu.make_async_copy(far_labels_ref, labels_ref, sem_ref.at[1])
    marks.start()
    margins = pltpu.make_async_copy(margin_ref, state_ref.at[pl.ds(0, K)], sem_ref.at[0])
    margins.start()
    local = win_ref[...] - lax.axis_index("feat") * columns
    mine = jnp.where((local >= 0) & (local < columns), local, 0).astype(f32)
    copies, lanes = [], []
    for step in range(ITERS):
        col = jnp.sum(mine[step : step + 1]).astype(i32)
        start = pl.multiple_of((col // LANES) * LANES, LANES)
        copy = pltpu.make_async_copy(
            geno_ref.at[:, pl.ds(start, LANES)], block_ref.at[step], sem_ref.at[2 + step]
        )
        copy.start()
        copies.append(copy)
        lanes.append(col - start)
    marks.wait()
    state_ref[K:] = jnp.broadcast_to(labels_ref[...].astype(f32), (8, samples))
    rows = lax.broadcasted_iota(i32, (8, LANES), 0)
    lane = lax.broadcasted_iota(i32, (8, LANES), 1)
    tile = jnp.zeros((8, LANES), f32)
    for step in range(ITERS):
        copies[step].wait()
        pick = jnp.where(lane == lanes[step], 1.0, 0.0).astype(bf16)
        x = lax.dot_general(
            pick, block_ref[step], (((1,), (1,)), ((), ())), preferred_element_type=f32
        )
        for j in range(samples // LANES):
            here = rows == step * (samples // LANES) + j
            tile = tile + jnp.where(here, x[:, j * LANES : (j + 1) * LANES], 0.0)
    out_ref[...] = jnp.broadcast_to(tile.astype(bf16)[None], out_ref.shape)
    margins.wait()


def load_halves(geno_ref, far_taken_ref, both_ref, sem_ref):
    samples = geno_ref.shape[0]
    half = both_ref.shape[1]
    start = pl.multiple_of(lax.rem(lax.axis_index("rows"), 2) * half, LANES)
    copies = [
        pltpu.make_async_copy(
            whole_ref.at[:, pl.ds(start, half)],
            both_ref.at[pl.ds(place * samples, samples)],
            sem_ref.at[place],
        )
        for place, whole_ref in enumerate((geno_ref, far_taken_ref))
    ]
    for copy in copies:
        copy.start()
    return copies


def half_table(resid, resid_taken, both_ref, start, width):
    whole = jnp.concatenate([resid, resid_taken], axis=1)
    return jnp.dot(whole, both_ref[:, pl.ds(start, width)], preferred_element_type=f32)


def sums_tile(resid, prob, picked):
    grad = resid.astype(f32) * picked
    curv = prob * (1.0 - prob) * picked * picked
    both = 0.5 * jnp.concatenate([grad, curv], axis=0)
    folded = both[:, :LANES]
    for j in range(1, both.shape[1] // LANES):
        folded = folded + both[:, j * LANES : (j + 1) * LANES]
    ones = jnp.ones((8, LANES), bf16)
    total = jnp.zeros((8, 2 * K), f32)
    for term in split3(folded):
        total = total + lax.dot_general(
            ones, term.astype(bf16), (((1,), (1,)), ((), ())), preferred_element_type=f32
        )
    high, middle, low = split3(total)
    row = lax.broadcasted_iota(i32, total.shape, 0)
    tile = jnp.where(row == 0, high, jnp.where(row == 1, middle, jnp.where(row == 2, low, 0.0)))
    return tile.astype(bf16)


def coefficients(tiles):
    tiles = tiles.astype(f32)
    row = jnp.sum(jnp.sum(tiles, axis=0), axis=0, keepdims=True)
    column = jnp.transpose(jnp.broadcast_to(row, (2 * K, LANES)))
    return shrink_rate * (2.0 * column[:K]) / (2.0 * column[K:] + ridge_term)


def lane_tile(values, count):
    return jnp.concatenate([values] * count, axis=1)


def send_tile(tile, both_ref, out_ref, sem_ref):
    half = out_ref.shape[2] - 2 * K
    both_ref[...] = jnp.broadcast_to(tile[None], both_ref.shape)
    copy = pltpu.make_async_copy(both_ref, out_ref.at[:, :, pl.ds(half, 2 * K)], sem_ref)
    copy.start()
    return copy


def send_table(resid, resid_taken, both_ref, table_ref, out_ref, sem_ref, order, pieces=2):
    width = table_ref.shape[2] // pieces
    copies = []
    for piece in range(pieces):
        span = pl.ds(piece * width, width)
        table = half_table(resid, resid_taken, both_ref, piece * width, width)
        place_classes(table, table_ref, span, order)
        copy = pltpu.make_async_copy(
            table_ref.at[:, :, span], out_ref.at[:, :, span], sem_ref.at[piece]
        )
        copy.start()
        copies.append(copy)
    return copies


def own_table_body(
    state_ref, geno_ref, far_taken_ref, far_win_ref, out_ref, both_ref, place_ref, win_ref, sem_ref
):
    wins = pltpu.make_async_copy(far_win_ref, win_ref, sem_ref.at[2])
    wins.start()
    copies = load_halves(geno_ref, far_taken_ref, both_ref, sem_ref)
    resid, _ = residuals(state_ref[:K], state_ref[K : K + 1])
    feat = reverse_bits(
        lax.broadcasted_iota(i32, place_ref.shape[1:], 0), place_ref.shape[1]
    )
    wins.wait()
    for step in range(ITERS):
        owner = win_ref[step : step + 1] // geno_ref.shape[1]
        place_ref[step] = jnp.where(feat == owner, 1.0, 0.0).astype(bf16)
    copies[0].wait()
    out_ref[...] = jnp.dot(resid, both_ref[: geno_ref.shape[0]], preferred_element_type=f32)
    copies[1].wait()


def pair_table_body(own_ref, state_taken_ref, both_ref, out_ref):
    samples = state_taken_ref.shape[1]
    resid_taken, _ = residuals(state_taken_ref[:K], state_taken_ref[K : K + 1])
    table = own_ref[...] + jnp.dot(resid_taken, both_ref[samples:], preferred_element_type=f32)
    place_classes(table, out_ref, slice(None), SUMS_ORDER)


def first_sums_body(
    cols_ref, place_ref, state_ref, table_ref, out_ref, picked_ref, far_picked_ref, tiles_ref,
    sem_ref,
):
    half = table_ref.shape[2]
    blocks = state_ref.shape[1] // LANES
    first = pltpu.make_async_copy(
        table_ref, out_ref.at[:, :, pl.ds(0, half)], sem_ref.at[0]
    )
    first.start()
    resid, prob = residuals(state_ref[:K], state_ref[K : K + 1])
    cols = cols_ref[...].astype(f32)
    for step in range(ITERS):
        place = place_ref[step]
        for j in range(blocks):
            piece = cols[:, step * blocks + j, :].astype(bf16)
            picked = lax.dot_general(
                place, piece, (((0,), (0,)), ((), ())), preferred_element_type=f32
            )
            picked_ref[step, :, j * LANES : (j + 1) * LANES] = picked.astype(bf16)
    third = pltpu.make_async_copy(picked_ref, far_picked_ref, sem_ref.at[3])
    third.start()
    tile = sums_tile(resid, prob, picked_ref[0].astype(f32))
    second = send_tile(tile, tiles_ref, out_ref, sem_ref.at[1])
    wait_all([first, second, third])


def second_table_body(
    shared_ref, state_ref, state_taken_ref, picked_ref, picked_taken_ref, both_ref,
    out_ref, coef_ref, table_ref, tiles_ref, sem_ref,
):
    half = table_ref.shape[2]
    coef = coefficients(shared_ref[:, :, half:])
    coef_ref[...] = coef
    coef = lane_tile(coef, state_ref.shape[1] // LANES)
    logits = state_ref[:K] + coef * picked_ref[0].astype(f32)
    resid, prob = residuals(logits, state_ref[K : K + 1])
    tile = sums_tile(resid, prob, picked_ref[1].astype(f32))
    sums_copy = send_tile(tile, tiles_ref, out_ref, sem_ref.at[0])
    logits_taken = state_taken_ref[:K] + coef * picked_taken_ref[0].astype(f32)
    resid_taken, _ = residuals(logits_taken, state_taken_ref[K : K + 1])
    table_copies = send_table(
        resid, resid_taken, both_ref, table_ref, out_ref, sem_ref.at[pl.ds(2, 2)],
        SUMS_ORDER,
    )
    wait_all([sums_copy] + table_copies)


def third_table_body(
    shared_ref, coef_ref, state_ref, state_taken_ref, picked_ref, picked_taken_ref, both_ref,
    out_ref, logits_ref, table_ref, new_ref, sem_ref,
):
    half = table_ref.shape[2]
    blocks = state_ref.shape[1] // LANES
    now = coefficients(shared_ref[:, :, half:])
    coefs = [lane_tile(coef, blocks) for coef in (coef_ref[...], now)]

    def updated(start, columns_ref):
        for step in range(ITERS):
            start = start + coefs[step] * columns_ref[step].astype(f32)
        return start

    logits = updated(state_ref[:K], picked_ref)
    new_ref[...] = logits
    logits_copy = pltpu.make_async_copy(new_ref, logits_ref, sem_ref.at[0])
    logits_copy.start()
    resid, _ = residuals(logits, state_ref[K : K + 1])
    resid_taken, _ = residuals(
        updated(state_taken_ref[:K], picked_taken_ref), state_taken_ref[K : K + 1]
    )
    table_copies = send_table(
        resid, resid_taken, both_ref, table_ref, out_ref, sem_ref.at[pl.ds(2, 2)],
        LAST_ORDER,
    )
    wait_all([logits_copy] + table_copies)


def shards(genotypes, labels, base_margin, winners):
    samples, columns = genotypes.shape
    feat_count = lax.axis_size("feat")
    rows_count = lax.axis_size("rows")
    class_share = K // rows_count
    half = columns // 2
    partners = [(i, i ^ 1) for i in range(rows_count)]
    work = 2 * K * 2 * samples * half
    payload_shape = (rows_count, class_share, half + 2 * K)
    table_shape = (rows_count, class_share, half)
    tiles = pltpu.VMEM((rows_count, 8, 2 * K), bf16)
    sems = pltpu.SemaphoreType.DMA

    sent, state = call(
        pick_body,
        (
            pltpu.VMEM((feat_count, ITERS * samples // LANES, LANES), bf16),
            pltpu.VMEM((K + 8, samples), f32),
        ),
        [VMEM, HBM, HBM, HBM],
        [
            pltpu.VMEM((ITERS, samples, LANES), bf16),
            pltpu.VMEM((1, samples), i32),
            sems((2 + ITERS,)),
        ],
        moved=samples * LANES * 4,
    )(near(winners), far(genotypes), far(base_margin.T), far(labels[None, :]))
    listed = [reverse_bits(i, feat_count) for i in range(feat_count)]
    cols = lax.all_to_all(sent, "feat", 0, 0, tiled=True, axis_index_groups=[listed])

    taken = far(lax.ppermute(genotypes, "rows", partners))
    geno = far(genotypes)
    state_taken = near(lax.ppermute(state, "rows", partners))
    state = near(state)

    own, both, place = call(
        own_table_body,
        (
            pltpu.VMEM((K, half), f32),
            pltpu.VMEM((2 * samples, half), bf16),
            pltpu.VMEM((ITERS, feat_count, K), bf16),
        ),
        [VMEM, HBM, HBM, HBM],
        [pltpu.VMEM((ITERS, K), i32), sems((3,))],
        flops=work // 2,
        moved=4 * samples * half,
    )(state, geno, taken, far(winners))
    table = call(
        pair_table_body,
        pltpu.VMEM(table_shape, bf16),
        [VMEM] * 3,
        flops=work // 2,
        moved=2 * samples * half,
    )(own, state_taken, both)

    picked_shape = (ITERS, K, samples)
    payload, picked, far_picked = call(
        first_sums_body,
        (
            pltpu.HBM(payload_shape, bf16),
            pltpu.VMEM(picked_shape, bf16),
            pltpu.HBM(picked_shape, bf16),
        ),
        [VMEM] * 4,
        [tiles, sems((4,))],
        moved=4 * samples * half,
    )(near(cols), place, state, table)
    shared0 = exchange(payload, SUMS_ORDER)
    picked_taken = near(lax.ppermute(far_picked, "rows", partners))

    payload, coef = call(
        second_table_body,
        (pltpu.HBM(payload_shape, bf16), pltpu.VMEM((K, LANES), f32)),
        [VMEM] * 6,
        [pltpu.VMEM(table_shape, bf16), tiles, sems((4,))],
        flops=work,
        moved=4 * samples * half,
    )(near(shared0), state, state_taken, near(picked), picked_taken, both)
    shared1 = exchange(payload, SUMS_ORDER)

    payload, logits = call(
        third_table_body,
        (pltpu.HBM(table_shape, bf16), pltpu.HBM((K, samples), f32)),
        [VMEM] * 7,
        [pltpu.VMEM(table_shape, bf16), pltpu.VMEM((K, samples), f32), sems((4,))],
        flops=work,
        moved=4 * samples * half,
    )(near(shared1), near(coef), state, state_taken, near(picked), picked_taken, both)
    shared2 = exchange(payload, LAST_ORDER)

    tables = []
    for shared, order in ((shared0, SUMS_ORDER), (shared1, SUMS_ORDER), (shared2, LAST_ORDER)):
        parts = shared[:, :, :half].astype(f32)
        sides = [
            sum(parts[place] for place, peer in enumerate(order) if peer % 2 == side)
            for side in range(2)
        ]
        tables.append(jnp.concatenate(sides, axis=1))
    return (logits.T, jnp.stack(tables))


def solution(mesh):
    in_specs = (P("rows", "feat"), P("rows"), P("rows", None), P())
    out_specs = (P("rows", None), P(None, "rows", "feat"))
    return jax.shard_map(shards, mesh=mesh, in_specs=in_specs, out_specs=out_specs, check_vma=False)
```

```python
import jax
import jax.numpy as jnp
from jax import lax
from jax.experimental import pallas as pl
from jax.experimental.pallas import tpu as pltpu
from jax.sharding import PartitionSpec as P

K = 64
ITERS = 2
LANES = 128
SUMS_ORDER = (0, 4, 2, 6, 1, 5, 3, 7)
LAST_ORDER = (0, 4, 2, 6, 1, 5, 3, 7)


shrink_rate = 0.5
ridge_term = 1.0

bf16 = jnp.bfloat16
f32 = jnp.float32
i32 = jnp.int32
BlockSpec = pl.BlockSpec
VMEM = pl.BlockSpec(memory_space=pltpu.VMEM)
HBM = pl.BlockSpec(memory_space=pltpu.HBM)


def call(body, out_shape, in_specs, scratch=(), flops=0, moved=0, room=8 << 20):
    out_specs = jax.tree.map(
        lambda out: BlockSpec(memory_space=out.memory_space), out_shape, is_leaf=is_out
    )
    return pl.pallas_call(
        body,
        out_shape=out_shape,
        in_specs=in_specs,
        out_specs=out_specs,
        scratch_shapes=list(scratch),
        cost_estimate=pl.CostEstimate(flops=flops, bytes_accessed=moved, transcendentals=0),
        compiler_params=pltpu.CompilerParams(vmem_limit_bytes=room),
    )


def is_out(value):
    return hasattr(value, "memory_space")


def far(values):
    return pltpu.with_memory_space_constraint(values, pltpu.HBM)


def wait_all(copies):
    for copy in copies:
        copy.wait()


def near(values):
    return pltpu.with_memory_space_constraint(values, pltpu.VMEM)


def reverse_bits(values, count):
    bits = count.bit_length() - 1
    return sum(((values >> bit) & 1) << (bits - 1 - bit) for bit in range(bits))


def place_classes(table, out_ref, span, order):
    share = out_ref.shape[1]
    for place, peer in enumerate(order):
        out_ref[place, :, span] = table[peer * share : (peer + 1) * share].astype(bf16)


def exchange(payload, order):
    return lax.all_to_all(
        payload, "rows", 0, 0, tiled=True, axis_index_groups=[list(order)]
    )


def rounded(values):
    return values.astype(bf16).astype(f32)


def split3(values):
    high = rounded(values)
    rest = values - high
    middle = rounded(rest)
    return high, middle, rest - middle


def softmax_classes(values):
    top = jnp.max(values, axis=0, keepdims=True)
    expo = jnp.exp(values - top)
    return expo / jnp.sum(expo, axis=0, keepdims=True)


def residuals(logits, label_row):
    prob = softmax_classes(logits)
    classes = lax.broadcasted_iota(i32, logits.shape, 0).astype(f32)
    onehot = jnp.where(classes == label_row, 1.0, 0.0)
    return (onehot - prob).astype(bf16), prob


def pick_body(
    win_ref, geno_ref, margin_ref, far_labels_ref, out_ref, state_ref, block_ref, labels_ref,
    sem_ref,
):
    samples, columns = geno_ref.shape
    marks = pltpu.make_async_copy(far_labels_ref, labels_ref, sem_ref.at[1])
    marks.start()
    margins = pltpu.make_async_copy(margin_ref, state_ref.at[pl.ds(0, K)], sem_ref.at[0])
    margins.start()
    local = win_ref[...] - lax.axis_index("feat") * columns
    mine = jnp.where((local >= 0) & (local < columns), local, 0).astype(f32)
    copies, lanes = [], []
    for step in range(ITERS):
        col = jnp.sum(mine[step : step + 1]).astype(i32)
        start = pl.multiple_of((col // LANES) * LANES, LANES)
        copy = pltpu.make_async_copy(
            geno_ref.at[:, pl.ds(start, LANES)], block_ref.at[step], sem_ref.at[2 + step]
        )
        copy.start()
        copies.append(copy)
        lanes.append(col - start)
    marks.wait()
    state_ref[K:] = jnp.broadcast_to(labels_ref[...].astype(f32), (8, samples))
    rows = lax.broadcasted_iota(i32, (8, LANES), 0)
    lane = lax.broadcasted_iota(i32, (8, LANES), 1)
    tile = jnp.zeros((8, LANES), f32)
    for step in range(ITERS):
        copies[step].wait()
        pick = jnp.where(lane == lanes[step], 1.0, 0.0).astype(bf16)
        x = lax.dot_general(
            pick, block_ref[step], (((1,), (1,)), ((), ())), preferred_element_type=f32
        )
        for j in range(samples // LANES):
            here = rows == step * (samples // LANES) + j
            tile = tile + jnp.where(here, x[:, j * LANES : (j + 1) * LANES], 0.0)
    out_ref[...] = jnp.broadcast_to(tile.astype(bf16)[None], out_ref.shape)
    margins.wait()


def load_halves(geno_ref, far_taken_ref, both_ref, sem_ref):
    samples = geno_ref.shape[0]
    half = both_ref.shape[1]
    start = pl.multiple_of(lax.rem(lax.axis_index("rows"), 2) * half, LANES)
    copies = [
        pltpu.make_async_copy(
            whole_ref.at[:, pl.ds(start, half)],
            both_ref.at[pl.ds(place * samples, samples)],
            sem_ref.at[place],
        )
        for place, whole_ref in enumerate((geno_ref, far_taken_ref))
    ]
    for copy in copies:
        copy.start()
    return copies


def half_table(resid, resid_taken, both_ref, start, width):
    whole = jnp.concatenate([resid, resid_taken], axis=1)
    return jnp.dot(whole, both_ref[:, pl.ds(start, width)], preferred_element_type=f32)


def sums_tile(resid, prob, picked):
    grad = resid.astype(f32) * picked
    curv = prob * (1.0 - prob) * picked * picked
    both = 0.5 * jnp.concatenate([grad, curv], axis=0)
    folded = both[:, :LANES]
    for j in range(1, both.shape[1] // LANES):
        folded = folded + both[:, j * LANES : (j + 1) * LANES]
    ones = jnp.ones((8, LANES), bf16)
    total = jnp.zeros((8, 2 * K), f32)
    for term in split3(folded):
        total = total + lax.dot_general(
            ones, term.astype(bf16), (((1,), (1,)), ((), ())), preferred_element_type=f32
        )
    high, middle, low = split3(total)
    row = lax.broadcasted_iota(i32, total.shape, 0)
    tile = jnp.where(row == 0, high, jnp.where(row == 1, middle, jnp.where(row == 2, low, 0.0)))
    return tile.astype(bf16)


def coefficients(tiles):
    tiles = tiles.astype(f32)
    row = jnp.sum(jnp.sum(tiles, axis=0), axis=0, keepdims=True)
    column = jnp.transpose(jnp.broadcast_to(row, (2 * K, LANES)))
    return shrink_rate * (2.0 * column[:K]) / (2.0 * column[K:] + ridge_term)


def lane_tile(values, count):
    return jnp.concatenate([values] * count, axis=1)


def send_tile(tile, both_ref, out_ref, sem_ref):
    half = out_ref.shape[2] - 2 * K
    both_ref[...] = jnp.broadcast_to(tile[None], both_ref.shape)
    copy = pltpu.make_async_copy(both_ref, out_ref.at[:, :, pl.ds(half, 2 * K)], sem_ref)
    copy.start()
    return copy


def send_table(resid, resid_taken, both_ref, table_ref, out_ref, sem_ref, order, pieces=1):
    width = table_ref.shape[2] // pieces
    copies = []
    for piece in range(pieces):
        span = pl.ds(piece * width, width)
        table = half_table(resid, resid_taken, both_ref, piece * width, width)
        place_classes(table, table_ref, span, order)
        copy = pltpu.make_async_copy(
            table_ref.at[:, :, span], out_ref.at[:, :, span], sem_ref.at[piece]
        )
        copy.start()
        copies.append(copy)
    return copies


def own_table_body(
    state_ref, geno_ref, far_taken_ref, far_win_ref, out_ref, both_ref, place_ref, win_ref, sem_ref
):
    wins = pltpu.make_async_copy(far_win_ref, win_ref, sem_ref.at[2])
    wins.start()
    copies = load_halves(geno_ref, far_taken_ref, both_ref, sem_ref)
    resid, _ = residuals(state_ref[:K], state_ref[K : K + 1])
    feat = reverse_bits(
        lax.broadcasted_iota(i32, place_ref.shape[1:], 0), place_ref.shape[1]
    )
    wins.wait()
    for step in range(ITERS):
        owner = win_ref[step : step + 1] // geno_ref.shape[1]
        place_ref[step] = jnp.where(feat == owner, 1.0, 0.0).astype(bf16)
    copies[0].wait()
    out_ref[...] = jnp.dot(resid, both_ref[: geno_ref.shape[0]], preferred_element_type=f32)
    copies[1].wait()


def pair_table_body(own_ref, state_taken_ref, both_ref, out_ref):
    samples = state_taken_ref.shape[1]
    resid_taken, _ = residuals(state_taken_ref[:K], state_taken_ref[K : K + 1])
    table = own_ref[...] + jnp.dot(resid_taken, both_ref[samples:], preferred_element_type=f32)
    place_classes(table, out_ref, slice(None), SUMS_ORDER)


def first_sums_body(
    cols_ref, place_ref, state_ref, table_ref, out_ref, picked_ref, far_picked_ref, tiles_ref,
    sem_ref,
):
    half = table_ref.shape[2]
    blocks = state_ref.shape[1] // LANES
    first = pltpu.make_async_copy(
        table_ref, out_ref.at[:, :, pl.ds(0, half)], sem_ref.at[0]
    )
    first.start()
    resid, prob = residuals(state_ref[:K], state_ref[K : K + 1])
    cols = cols_ref[...].astype(f32)
    for step in range(ITERS):
        place = place_ref[step]
        for j in range(blocks):
            piece = cols[:, step * blocks + j, :].astype(bf16)
            picked = lax.dot_general(
                place, piece, (((0,), (0,)), ((), ())), preferred_element_type=f32
            )
            picked_ref[step, :, j * LANES : (j + 1) * LANES] = picked.astype(bf16)
    third = pltpu.make_async_copy(picked_ref, far_picked_ref, sem_ref.at[3])
    third.start()
    tile = sums_tile(resid, prob, picked_ref[0].astype(f32))
    second = send_tile(tile, tiles_ref, out_ref, sem_ref.at[1])
    wait_all([first, second, third])


def second_table_body(
    shared_ref, state_ref, state_taken_ref, picked_ref, picked_taken_ref, both_ref,
    out_ref, coef_ref, table_ref, tiles_ref, sem_ref,
):
    half = table_ref.shape[2]
    coef = coefficients(shared_ref[:, :, half:])
    coef_ref[...] = coef
    coef = lane_tile(coef, state_ref.shape[1] // LANES)
    logits = state_ref[:K] + coef * picked_ref[0].astype(f32)
    resid, prob = residuals(logits, state_ref[K : K + 1])
    tile = sums_tile(resid, prob, picked_ref[1].astype(f32))
    sums_copy = send_tile(tile, tiles_ref, out_ref, sem_ref.at[0])
    logits_taken = state_taken_ref[:K] + coef * picked_taken_ref[0].astype(f32)
    resid_taken, _ = residuals(logits_taken, state_taken_ref[K : K + 1])
    table_copies = send_table(
        resid, resid_taken, both_ref, table_ref, out_ref, sem_ref.at[pl.ds(2, 2)],
        SUMS_ORDER,
    )
    wait_all([sums_copy] + table_copies)


def third_table_body(
    shared_ref, coef_ref, state_ref, state_taken_ref, picked_ref, picked_taken_ref, both_ref,
    out_ref, logits_ref, table_ref, new_ref, sem_ref,
):
    half = table_ref.shape[2]
    blocks = state_ref.shape[1] // LANES
    now = coefficients(shared_ref[:, :, half:])
    coefs = [lane_tile(coef, blocks) for coef in (coef_ref[...], now)]

    def updated(start, columns_ref):
        for step in range(ITERS):
            start = start + coefs[step] * columns_ref[step].astype(f32)
        return start

    logits = updated(state_ref[:K], picked_ref)
    new_ref[...] = logits
    logits_copy = pltpu.make_async_copy(new_ref, logits_ref, sem_ref.at[0])
    logits_copy.start()
    resid, _ = residuals(logits, state_ref[K : K + 1])
    resid_taken, _ = residuals(
        updated(state_taken_ref[:K], picked_taken_ref), state_taken_ref[K : K + 1]
    )
    table_copies = send_table(
        resid, resid_taken, both_ref, table_ref, out_ref, sem_ref.at[pl.ds(2, 2)],
        LAST_ORDER,
    )
    wait_all([logits_copy] + table_copies)


def shards(genotypes, labels, base_margin, winners):
    samples, columns = genotypes.shape
    feat_count = lax.axis_size("feat")
    rows_count = lax.axis_size("rows")
    class_share = K // rows_count
    half = columns // 2
    partners = [(i, i ^ 1) for i in range(rows_count)]
    work = 2 * K * 2 * samples * half
    payload_shape = (rows_count, class_share, half + 2 * K)
    table_shape = (rows_count, class_share, half)
    tiles = pltpu.VMEM((rows_count, 8, 2 * K), bf16)
    sems = pltpu.SemaphoreType.DMA

    sent, state = call(
        pick_body,
        (
            pltpu.VMEM((feat_count, ITERS * samples // LANES, LANES), bf16),
            pltpu.VMEM((K + 8, samples), f32),
        ),
        [VMEM, HBM, HBM, HBM],
        [
            pltpu.VMEM((ITERS, samples, LANES), bf16),
            pltpu.VMEM((1, samples), i32),
            sems((2 + ITERS,)),
        ],
        moved=samples * LANES * 4,
    )(near(winners), far(genotypes), far(base_margin.T), far(labels[None, :]))
    listed = [reverse_bits(i, feat_count) for i in range(feat_count)]
    cols = lax.all_to_all(sent, "feat", 0, 0, tiled=True, axis_index_groups=[listed])

    taken = far(lax.ppermute(genotypes, "rows", partners))
    geno = far(genotypes)
    state_taken = near(lax.ppermute(state, "rows", partners))
    state = near(state)

    own, both, place = call(
        own_table_body,
        (
            pltpu.VMEM((K, half), f32),
            pltpu.VMEM((2 * samples, half), bf16),
            pltpu.VMEM((ITERS, feat_count, K), bf16),
        ),
        [VMEM, HBM, HBM, HBM],
        [pltpu.VMEM((ITERS, K), i32), sems((3,))],
        flops=work // 2,
        moved=4 * samples * half,
    )(state, geno, taken, far(winners))
    table = call(
        pair_table_body,
        pltpu.VMEM(table_shape, bf16),
        [VMEM] * 3,
        flops=work // 2,
        moved=2 * samples * half,
    )(own, state_taken, both)

    picked_shape = (ITERS, K, samples)
    payload, picked, far_picked = call(
        first_sums_body,
        (
            pltpu.HBM(payload_shape, bf16),
            pltpu.VMEM(picked_shape, bf16),
            pltpu.HBM(picked_shape, bf16),
        ),
        [VMEM] * 4,
        [tiles, sems((4,))],
        moved=4 * samples * half,
    )(near(cols), place, state, table)
    shared0 = exchange(payload, SUMS_ORDER)
    picked_taken = near(lax.ppermute(far_picked, "rows", partners))

    payload, coef = call(
        second_table_body,
        (pltpu.HBM(payload_shape, bf16), pltpu.VMEM((K, LANES), f32)),
        [VMEM] * 6,
        [pltpu.VMEM(table_shape, bf16), tiles, sems((4,))],
        flops=work,
        moved=4 * samples * half,
    )(near(shared0), state, state_taken, near(picked), picked_taken, both)
    shared1 = exchange(payload, SUMS_ORDER)

    payload, logits = call(
        third_table_body,
        (pltpu.HBM(table_shape, bf16), pltpu.HBM((K, samples), f32)),
        [VMEM] * 7,
        [pltpu.VMEM(table_shape, bf16), pltpu.VMEM((K, samples), f32), sems((4,))],
        flops=work,
        moved=4 * samples * half,
    )(near(shared1), near(coef), state, state_taken, near(picked), picked_taken, both)
    shared2 = exchange(payload, LAST_ORDER)

    tables = []
    for shared, order in ((shared0, SUMS_ORDER), (shared1, SUMS_ORDER), (shared2, LAST_ORDER)):
        parts = shared[:, :, :half].astype(f32)
        sides = [
            sum(parts[place] for place, peer in enumerate(order) if peer % 2 == side)
            for side in range(2)
        ]
        tables.append(jnp.concatenate(sides, axis=1))
    return (logits.T, jnp.stack(tables))


def solution(mesh):
    in_specs = (P("rows", "feat"), P("rows"), P("rows", None), P())
    out_specs = (P("rows", None), P(None, "rows", "feat"))
    return jax.shard_map(shards, mesh=mesh, in_specs=in_specs, out_specs=out_specs, check_vma=False)
```
